256 devices in a mesh: height: 8 (over z_hi, core), plane: 32 (over z_lo, y, x).
Axes of the slice: x: 4, y: 4, z: 8 (z_hi: 4, z_lo: 2; z = z_hi * 2 + z_lo), core: 2. Of those that a mesh axis runs over, the one named last changes fastest.
Arguments:
- cotangent: float32 [128, 256, 128], P('height', 'plane'), may hold values from -36 to 36
- conductivity: float32 [16, 32, 16], P('height', 'plane'), may hold values from 0.2 to 5
- capacity: float32 [16, 32, 16], P('height', 'plane'), may hold values from 0.5 to 2
- sources: int32 [2, 128], replicated, may hold values from 0 to 8191
Outputs:
- adjoint_second: float32 [128, 256, 128], P('height', 'plane')
- adjoint_first: float32 [128, 256, 128], P('height', 'plane')
- source_grad: float32 [2, 128], replicated
The draws below stay inside these ranges and needn't reach their ends.
Inputs may be any that keep to these rules, and one draw needn't show every extreme that they name: `sources`: element numbers; element (ez, ex, ey) has number (ez * 32 + ex) * 16 + ey, and a number may repeat.
All inputs are finite; a program needn't handle non-finite values.
Results may differ from the reference program's by a relative error of at most 0.0001.
Values sent between devices are 32-bit elements; how exact they have to be, the bound alone decides.
A program may use at most 64 MiB of HBM per device.

```python
import math
import jax
import jax.numpy as jnp
import numpy as np
from jax import lax

EY = 16
ITERS = 3
SRC = 128
EXG = 32
EZG = 16
NXN = 256
NYN = 128
NZN = 128
ELEMS = 8192


def draw_cotangent(key, part):
    sample_key = jax.random.fold_in(key, 11)
    sample = jnp.clip(jax.random.normal(sample_key, (NZN, NXN, NYN), jnp.float32), -4.0, 4.0)
    depth_ramp = 1.0 + 2.0 * jnp.arange(NZN, dtype=jnp.float32) / (NZN - 1)
    width_ramp = 1.0 + 2.0 * jnp.arange(NXN, dtype=jnp.float32) / (NXN - 1)
    return sample * depth_ramp[:, None, None] * width_ramp[None, :, None]


def place_ends(entries, own_key, least, high):
    index_at = [jax.random.randint(jax.random.fold_in(own_key, axis), (), 0, length) for axis, length in enumerate(entries.shape)]
    longest = entries.shape.index(max(entries.shape))
    neighbour = index_at[:longest] + [(index_at[longest] + 1) % entries.shape[longest]] + index_at[longest + 1:]
    return entries.at[tuple(index_at)].set(least).at[tuple(neighbour)].set(high)


def level_of(key, dims, cuts, least, largest):
    def one(dim, shards_of):
        steps = jax.random.uniform(jax.random.fold_in(jax.random.fold_in(key, 6), dim), (shards_of,), jnp.float32, least / len(cuts), largest / len(cuts))
        return jnp.repeat(jnp.exp(steps), dims[dim] // shards_of).reshape((-1,) + (1,) * (len(dims) - dim - 1))

    loudness = one(*cuts[0])
    for cut in cuts[1:]:
        loudness = loudness * one(*cut)
    return loudness


def setup_inputs(seed: int = 0) -> dict:
    streams_of = jax.random.split(jax.random.key(seed), 5)
    cotangent = draw_cotangent(jax.random.fold_in(streams_of[4], 71), 0)
    conductivity = jnp.clip(jnp.exp(math.log(5.0) - 3.218876 * jax.random.uniform(streams_of[1], (EZG, EXG, EY), jnp.float32) ** level_of(streams_of[1], (EZG, EXG, EY), ((0, 8), (1, 32)), -0.2, 0.2)), 0.2, 5.0)
    capacity = jnp.clip(jnp.exp(math.log(2.0) - 1.3862944 * jax.random.uniform(streams_of[2], (EZG, EXG, EY), jnp.float32) ** level_of(streams_of[2], (EZG, EXG, EY), ((0, 8), (1, 32)), -0.2, 0.2)), 0.5, 2.0)
    sources = place_ends(jax.random.randint(streams_of[3], (2, SRC), 0, ELEMS), jax.random.fold_in(streams_of[3], 1), 0, ELEMS - 1).astype(jnp.int32)
    return {"cotangent": cotangent, "conductivity": conductivity, "capacity": capacity, "sources": sources}


precise = lax.Precision.HIGHEST
INV_STEP = 20.0


def gll_tables():
    points = np.array([-1.0, -0.8717401485096066, -0.5917001814331423, -0.2092992179024789, 0.2092992179024789, 0.5917001814331423, 0.8717401485096066, 1.0])
    weights = np.array([1.0 / 28.0, 0.2107042271435061, 0.3411226924835044, 0.4124587946587038, 0.4124587946587038, 0.3411226924835044, 0.2107042271435061, 1.0 / 28.0])
    product = np.array([np.prod([points[column] - points[others] for others in range(8) if others != column]) for column in range(8)])
    derivative = np.zeros((8, 8))
    for row_idx in range(8):
        for col_idx in range(8):
            if row_idx != col_idx:
                derivative[row_idx, col_idx] = product[row_idx] / (product[col_idx] * (points[row_idx] - points[col_idx]))
        derivative[row_idx, row_idx] = -np.sum(derivative[row_idx])
    stiff_diag = np.sum(derivative ** 2 * weights[:, None], axis=0)
    return derivative, weights, stiff_diag


def multiplicity(extent):
    position = jnp.arange(extent, dtype=jnp.int32)
    ending = ((position % 8 == 7) & (position < extent - 1)).astype(jnp.float32)
    opening = ((position % 8 == 0) & (position > 0)).astype(jnp.float32)
    return 1.0 + ending + opening


def pair_sum(values, dim_index):
    ending = [slice(None)] * 3
    opening = [slice(None)] * 3
    ending[dim_index] = slice(7, -1, 8)
    opening[dim_index] = slice(8, None, 8)
    joined = values[tuple(ending)] + values[tuple(opening)]
    return values.at[tuple(ending)].set(joined).at[tuple(opening)].set(joined)


def assemble(values):
    return pair_sum(pair_sum(pair_sum(values, 1), 2), 0)


def reference(cotangent, conductivity, capacity, sources):
    derivative, weights, stiff_diag = gll_tables()
    depth_nodes, width_nodes, span_nodes = cotangent.shape
    diff = jnp.asarray(derivative, jnp.float32)
    weight_depth = jnp.asarray(np.tile(weights, depth_nodes // 8), jnp.float32)
    weight_width = jnp.asarray(np.tile(weights, width_nodes // 8), jnp.float32)
    weight_span = jnp.asarray(np.tile(weights, span_nodes // 8), jnp.float32)
    stiff_depth = jnp.asarray(np.tile(stiff_diag, depth_nodes // 8), jnp.float32)
    stiff_width = jnp.asarray(np.tile(stiff_diag, width_nodes // 8), jnp.float32)
    stiff_span = jnp.asarray(np.tile(stiff_diag, span_nodes // 8), jnp.float32)
    kappa_nodes = jnp.repeat(jnp.repeat(jnp.repeat(conductivity, 8, axis=0), 8, axis=1), 8, axis=2)
    cap_nodes = jnp.repeat(jnp.repeat(jnp.repeat(capacity, 8, axis=0), 8, axis=1), 8, axis=2)
    omega_nodes = weight_depth[:, None, None] * weight_width[None, :, None] * weight_span[None, None, :]
    mass_local = INV_STEP * cap_nodes * omega_nodes
    kappa_weight = kappa_nodes * omega_nodes
    diag_local = mass_local + kappa_nodes * (stiff_depth[:, None, None] * weight_width[None, :, None] * weight_span[None, None, :] + weight_depth[:, None, None] * stiff_width[None, :, None] * weight_span[None, None, :] + weight_depth[:, None, None] * weight_width[None, :, None] * stiff_span[None, None, :])
    diag_total = assemble(diag_local)
    share_weight = 1.0 / (multiplicity(depth_nodes)[:, None, None] * multiplicity(width_nodes)[None, :, None] * multiplicity(span_nodes)[None, None, :])
    shape_depth = (depth_nodes // 8, 8, width_nodes, span_nodes)
    shape_width = (depth_nodes, width_nodes // 8, 8, span_nodes)
    shape_span = (depth_nodes, width_nodes, span_nodes // 8, 8)
    full_shape = cotangent.shape

    def stiffness(values):
        grad_depth = jnp.einsum("ab,ebxy->eaxy", diff, values.reshape(shape_depth), precision=precise).reshape(full_shape)
        grad_width = jnp.einsum("ab,zeby->zeay", diff, values.reshape(shape_width), precision=precise).reshape(full_shape)
        grad_span = jnp.einsum("ab,zxeb->zxea", diff, values.reshape(shape_span), precision=precise).reshape(full_shape)
        back_depth = jnp.einsum("ab,eaxy->ebxy", diff, (kappa_weight * grad_depth).reshape(shape_depth), precision=precise).reshape(full_shape)
        back_width = jnp.einsum("ab,zeay->zeby", diff, (kappa_weight * grad_width).reshape(shape_width), precision=precise).reshape(full_shape)
        back_span = jnp.einsum("ab,zxea->zxeb", diff, (kappa_weight * grad_span).reshape(shape_span), precision=precise).reshape(full_shape)
        return mass_local * values + (back_depth + back_width + back_span)

    def inner_sum(left_values, right_values):
        return jnp.sum(left_values * right_values * share_weight)

    def adjoint_solve(source_term):
        iterate = jnp.zeros_like(source_term)
        residual = source_term
        precond = residual / diag_total
        direction = precond
        rho_now = inner_sum(residual, precond)
        for sweep_idx in range(ITERS):
            applied = assemble(stiffness(direction))
            step_len = rho_now / inner_sum(direction, applied)
            iterate = iterate + step_len * direction
            residual = residual - step_len * applied
            precond = residual / diag_total
            rho_next = inner_sum(residual, precond)
            direction = precond + (rho_next / rho_now) * direction
            rho_now = rho_next
        return iterate

    adjoint_second = adjoint_solve(assemble(mass_local * cotangent))
    adjoint_first = adjoint_solve(assemble(mass_local * adjoint_second))

    def element_sums(values):
        return (mass_local * values).reshape(depth_nodes // 8, 8, width_nodes // 8, 8, span_nodes // 8, 8).sum(axis=(1, 3, 5)).reshape(-1)

    grad_first = element_sums(adjoint_first)[sources[0]] / (8.0 * INV_STEP)
    grad_second = element_sums(adjoint_second)[sources[1]] / (8.0 * INV_STEP)
    return adjoint_second, adjoint_first, jnp.stack([grad_first, grad_second])
```

```python
import functools

import jax
import jax.numpy as jnp
import numpy as np
from jax import lax
from jax.experimental import pallas as pl
from jax.experimental.pallas import tpu as pltpu
from jax.sharding import PartitionSpec as P

MESH = pl.DeviceIdType.MESH
HIGH = lax.Precision.HIGHEST
INV_STEP = 20.0
SHIFT = 0.75
FIELDS = (3, 1, 1, 1, 1)
STARTS = (0, 3, 4, 5, 6)
TOTAL = 7


def gll_tables():
    points = np.array(
        [
            -1.0,
            -0.8717401485096066,
            -0.5917001814331423,
            -0.2092992179024789,
            0.2092992179024789,
            0.5917001814331423,
            0.8717401485096066,
            1.0,
        ]
    )
    weights = np.array(
        [
            1.0 / 28.0,
            0.2107042271435061,
            0.3411226924835044,
            0.4124587946587038,
            0.4124587946587038,
            0.3411226924835044,
            0.2107042271435061,
            1.0 / 28.0,
        ]
    )
    product = np.array(
        [
            np.prod([points[column] - points[others] for others in range(8) if others != column])
            for column in range(8)
        ]
    )
    derivative = np.zeros((8, 8))
    for row_idx in range(8):
        for col_idx in range(8):
            if row_idx != col_idx:
                derivative[row_idx, col_idx] = product[row_idx] / (
                    product[col_idx] * (points[row_idx] - points[col_idx])
                )
        derivative[row_idx, row_idx] = -np.sum(derivative[row_idx])
    return derivative, weights


def tables():
    derivative, weights = gll_tables()
    stiff = derivative.T @ np.diag(weights) @ derivative
    scaled = stiff / weights[:, None]
    eye8, eye2, eye16 = np.eye(8), np.eye(2), np.eye(16)
    rows = np.kron(eye2, np.kron(scaled, eye8) + np.kron(eye8, scaled))
    lanes = np.kron(eye16, scaled.T)
    face = weights[:, None] * np.tile(weights, 16)[None, :]
    slope = np.diag(scaled)
    face_slope = slope[:, None] + np.tile(slope, 16)[None, :]
    const = np.concatenate([rows, lanes, face, face_slope]).astype(np.float32)
    return const, weights, slope


def kernel(
    shape,
    weights,
    slope,
    cot_ref,
    kap_ref,
    cap_ref,
    src_ref,
    const_ref,
    second_ref,
    first_ref,
    grad_ref,
    y_ref,
    face_ref,
    plane_in,
    height_in,
    work_ref,
    mat_ref,
    tile_a,
    tile_b,
    send_sem,
    recv_sem,
    send_red,
    recv_red,
):
    heights, planes = shape
    runs = 2
    per_run = planes // runs
    stack = heights * runs
    h = lax.axis_index("height")
    p = lax.axis_index("plane")
    run = p // per_run
    pos = lax.rem(p, per_run)
    level = h * runs + run
    h_lo, h_hi = lax.rem(h + heights - 1, heights), lax.rem(h + 1, heights)
    p_lo, p_hi = lax.rem(p + planes - 1, planes), lax.rem(p + 1, planes)

    def run_peer(step):
        return (h, run * per_run + lax.rem(pos + step, per_run))

    def stack_peer(step):
        other = lax.rem(level + step, stack)
        return (other // runs, lax.rem(other, runs) * per_run + pos)

    halo = (
        (h, p_lo),
        (h, p_hi),
        (h_lo, p),
        (h_hi, p),
        (h_lo, p_lo),
        (h_lo, p_hi),
        (h_hi, p_lo),
        (h_hi, p_hi),
    )
    barrier = pltpu.get_barrier_semaphore()
    for device in halo:
        pl.semaphore_signal(barrier, inc=1, device_id=device, device_id_type=MESH)

    def greet_run(step, carry):
        pl.semaphore_signal(barrier, inc=1, device_id=run_peer(step), device_id_type=MESH)
        return carry

    def greet_stack(step, carry):
        pl.semaphore_signal(barrier, inc=1, device_id=stack_peer(step), device_id_type=MESH)
        return carry

    lax.fori_loop(1, per_run, greet_run, 0)
    lax.fori_loop(1, stack, greet_stack, 0)

    has_p_lo = jnp.where(p > 0, 1.0, 0.0)
    has_p_hi = jnp.where(p < planes - 1, 1.0, 0.0)
    has_h_lo = jnp.where(h > 0, 1.0, 0.0)
    has_h_hi = jnp.where(h < heights - 1, 1.0, 0.0)

    lane = lax.broadcasted_iota(jnp.int32, (8, 128), 1)
    sub = lax.broadcasted_iota(jnp.int32, (8, 128), 0)
    lane_mod = lax.rem(lane, 8)
    opening = jnp.where((lane_mod == 0) & (lane > 0), 1.0, 0.0)
    ending = jnp.where((lane_mod == 7) & (lane < 127), 1.0, 0.0)
    row_first = jnp.where(sub == 0, 1.0, 0.0)
    row_last = jnp.where(sub == 7, 1.0, 0.0)

    spread = jnp.where(
        lax.broadcasted_iota(jnp.int32, (16, 128), 1) // 8
        == lax.broadcasted_iota(jnp.int32, (16, 128), 0),
        1.0,
        0.0,
    )
    elems = jnp.concatenate([kap_ref[0], kap_ref[1], cap_ref[0], cap_ref[1]] * 2, axis=0)
    wide = jnp.dot(elems, spread, precision=HIGH, preferred_element_type=jnp.float32)
    face_w = const_ref[256:264, :]
    face_slope = const_ref[264:272, :]
    stiff_w = [face_w * wide[e : e + 1, :] for e in range(2)]
    mass_w = [face_w * (INV_STEP * wide[2 + e : 3 + e, :]) for e in range(2)]

    def put(slot, values):
        y_ref[slot] = values
        flat = values.reshape(128, 128)
        work_ref[slot] = flat
        for side, row in ((0, 0), (1, 7)):
            face_ref[side, slot] = work_ref.at[slot][pl.ds(row, 16, stride=8), :]

    def copies(index):
        slots = pl.ds(STARTS[index], FIELDS[index])
        routes = (
            (face_ref.at[0, slots], plane_in.at[1, slots]),
            (face_ref.at[1, slots], plane_in.at[0, slots]),
            (y_ref.at[slots, 0], height_in.at[1, slots]),
            (y_ref.at[slots, 15], height_in.at[0, slots]),
            (y_ref.at[slots, 0], height_in.at[5, slots]),
            (y_ref.at[slots, 0], height_in.at[4, slots]),
            (y_ref.at[slots, 15], height_in.at[3, slots]),
            (y_ref.at[slots, 15], height_in.at[2, slots]),
        )
        return [
            pltpu.make_async_remote_copy(
                src_ref=source,
                dst_ref=target,
                send_sem=send_sem.at[index, way],
                recv_sem=recv_sem.at[index, way],
                device_id=halo[way],
                device_id_type=MESH,
            )
            for way, (source, target) in enumerate(routes)
        ]

    def gathered(slot):
        work = work_ref.at[slot]
        work[pl.ds(0, 16, stride=8), :] += has_p_lo * plane_in[0, slot]
        work[pl.ds(7, 16, stride=8), :] += has_p_hi * plane_in[1, slot]
        low = (
            height_in[0, slot]
            + (row_first * has_p_lo) * pltpu.roll(height_in[2, slot], 1, axis=0)
            + (row_last * has_p_hi) * pltpu.roll(height_in[3, slot], 7, axis=0)
        )
        high = (
            height_in[1, slot]
            + (row_first * has_p_lo) * pltpu.roll(height_in[4, slot], 1, axis=0)
            + (row_last * has_p_hi) * pltpu.roll(height_in[5, slot], 7, axis=0)
        )
        work[0:8, :] += has_h_lo * low
        work[120:128, :] += has_h_hi * high
        joined = work[56:64, :] + work[64:72, :]
        work[56:64, :] = joined
        work[64:72, :] = joined
        flat = work[...]
        after = pltpu.roll(flat, 127, axis=1).reshape(16, 8, 128)
        before = pltpu.roll(flat, 1, axis=1).reshape(16, 8, 128)
        return flat.reshape(16, 8, 128) + ending[None] * after + opening[None] * before

    def layered(parts):
        return jnp.stack([weights[a] * parts[e] for e in range(2) for a in range(8)])

    mass = layered(mass_w)
    conduct = layered(stiff_w)
    slopes = jnp.stack([face_slope + slope[a] for a in range(8)] * 2)

    def stiffness(values):
        flat = values.reshape(128, 128)
        inner = jnp.dot(
            const_ref[0:128, :], flat, precision=HIGH, preferred_element_type=jnp.float32
        ) + jnp.dot(flat, const_ref[128:256, :], precision=HIGH, preferred_element_type=jnp.float32)
        return mat_ref[0] * values + mat_ref[1] * inner.reshape(16, 8, 128)

    mat_ref[0] = mass
    mat_ref[1] = conduct
    put(0, mass * cot_ref[...])
    put(1, mass)
    put(2, mass + conduct * slopes)

    pl.semaphore_wait(barrier, 8 + per_run - 1 + stack - 1)

    started = []

    def send(index):
        batch = copies(index)
        for copy in batch:
            copy.start()
        started.append(batch)

    def arrive(index):
        for copy in started[index]:
            copy.wait_recv()

    send(0)

    local = lax.broadcasted_iota(jnp.int32, (128, 128), 0) // 8
    hits = []
    for step in range(2):
        wanted = src_ref[step : step + 1, :]
        hits.append(
            jnp.concatenate(
                [
                    jnp.where(wanted == ((h * 2 + e) * planes + p) * 16 + local, 1.0, 0.0)
                    for e in range(2)
                ],
                axis=0,
            )
        )

    def source_sums(fields, hit):
        rows = []
        for values in fields:
            weighed = mat_ref[0] * values
            rows.append(
                jnp.concatenate(
                    [
                        jnp.sum(weighed[8 * e : 8 * e + 8].reshape(64, 128), axis=0, keepdims=True)
                        for e in range(2)
                    ],
                    axis=1,
                )
            )
        rows = jnp.concatenate(rows + [jnp.zeros((5, 256), jnp.float32)], axis=0)
        return jnp.dot(rows, hit, precision=HIGH, preferred_element_type=jnp.float32)

    depth_copies = [jnp.ones((1, 1), jnp.float32)] * 16
    depth_copies[0] = jnp.full((1, 1), 1.0 / (1.0 + has_h_lo))
    depth_copies[7] = depth_copies[8] = jnp.full((1, 1), 0.5)
    depth_copies[15] = jnp.full((1, 1), 1.0 / (1.0 + has_h_hi))
    plane_copies = (
        1.0 / ((1.0 + row_first * has_p_lo + row_last * has_p_hi) * (1.0 + opening + ending))
    )

    arrive(0)
    diag = gathered(2)
    inv_diag = 1.0 / diag
    mat_ref[2] = inv_diag
    mat_ref[3] = jnp.stack([diag[i] * plane_copies * depth_copies[i] for i in range(16)])
    mat_ref[4] = gathered(1) * inv_diag

    def dot_rows(left, right):
        return jnp.sum((left * right).reshape(128, 128), axis=0, keepdims=True)

    def total(index, tile):
        for stage, (ref, spot, count, peer) in enumerate(
            ((tile_a, pos, per_run, run_peer), (tile_b, level, stack, stack_peer))
        ):
            own = ref.at[index, spot]
            own[...] = tile

            def push(step, carry):
                pltpu.make_async_remote_copy(
                    src_ref=own,
                    dst_ref=own,
                    send_sem=send_red.at[index, stage],
                    recv_sem=recv_red.at[index, stage],
                    device_id=peer(step),
                    device_id_type=MESH,
                ).start()
                return carry

            lax.fori_loop(1, count, push, 0)
            rest = ref.at[index, pl.ds(0, count - 1)]
            waiter = pltpu.make_async_remote_copy(
                src_ref=rest,
                dst_ref=rest,
                send_sem=send_red.at[index, stage],
                recv_sem=recv_red.at[index, stage],
                device_id=peer(1),
                device_id_type=MESH,
            )
            waiter.wait_send()
            waiter.wait_recv()
            tile = jnp.sum(ref[index], axis=0)
        return tile

    def solve(index, first, hit):
        base = 2 * index + 1
        applied = stiffness(first)
        put(STARTS[base], applied)
        send(base)
        weighted = mat_ref[3]
        arrive(base)
        second = gathered(STARTS[base]) * mat_ref[2] - SHIFT * first
        applied = stiffness(second)
        put(STARTS[base + 1], applied)
        send(base + 1)
        m = [dot_rows(weighted * first, first), dot_rows(weighted * first, second)]
        m.append(dot_rows(weighted * second, second))
        arrive(base + 1)
        third = gathered(STARTS[base + 1]) * mat_ref[2] - SHIFT * second
        m.append(dot_rows(weighted * second, third))
        m.append(dot_rows(weighted * third, third))
        m.append(dot_rows(third, stiffness(third)) - SHIFT * m[4])
        basis = (first, second, third)
        tile = jnp.concatenate(
            m + [jnp.zeros((2, 128), jnp.float32), source_sums(basis, hit)], axis=0
        )
        tile = total(index, tile)
        m = jnp.broadcast_to(jnp.sum(tile[0:8], axis=1, keepdims=True), (8, 128))
        m = [m[k : k + 1] for k in range(6)]
        a = [m[k + 1] + SHIFT * m[k] for k in range(5)]
        pivot0 = a[0]
        l1 = a[1] / pivot0
        l2 = a[2] / pivot0
        pivot1 = a[2] - l1 * a[1]
        cross = a[3] - l1 * a[2]
        inv1 = jnp.where(pivot1 > 1e-7 * a[2], 1.0 / pivot1, 0.0)
        l12 = cross * inv1
        pivot2 = a[4] - l2 * a[2] - l12 * cross
        inv2 = jnp.where(pivot2 > 1e-7 * a[4], 1.0 / pivot2, 0.0)
        g1 = m[1] - l1 * m[0]
        g2 = m[2] - l2 * m[0] - l12 * g1
        c2 = g2 * inv2
        c1 = g1 * inv1 - l12 * c2
        c0 = m[0] / pivot0 - l1 * c1 - l2 * c2
        answer = c0[None] * first + c1[None] * second + c2[None] * third
        grads = c0 * tile[8:9] + c1 * tile[9:10] + c2 * tile[10:11]
        return answer, grads * (1.0 / (8.0 * INV_STEP))

    later, later_grad = solve(0, gathered(0) * inv_diag, hits[1])
    second_ref[...] = later
    earlier, earlier_grad = solve(1, later * mat_ref[4], hits[0])
    first_ref[...] = earlier
    grad_ref[0:1, :] = earlier_grad
    grad_ref[1:2, :] = later_grad
    for batch in started:
        for copy in batch:
            copy.wait_send()


def solution(mesh):
    shape = (mesh.shape["height"], mesh.shape["plane"])
    const, weights, slope = tables()
    weights = [float(value) for value in weights]
    slope = [float(value) for value in slope]
    run, stack = shape[1] // 2, shape[0] * 2

    def per_device(cotangent, conductivity, capacity, sources):
        block = jax.ShapeDtypeStruct(cotangent.shape, jnp.float32)
        return pl.pallas_call(
            functools.partial(kernel, shape, weights, slope),
            out_shape=(block, block, jax.ShapeDtypeStruct(sources.shape, jnp.float32)),
            in_specs=[pl.BlockSpec(memory_space=pltpu.VMEM)] * 5,
            out_specs=(pl.BlockSpec(memory_space=pltpu.VMEM),) * 3,
            scratch_shapes=[
                pltpu.VMEM((TOTAL, 16, 8, 128), jnp.float32),
                pltpu.VMEM((2, TOTAL, 16, 128), jnp.float32),
                pltpu.VMEM((2, TOTAL, 16, 128), jnp.float32),
                pltpu.VMEM((6, TOTAL, 8, 128), jnp.float32),
                pltpu.VMEM((TOTAL, 128, 128), jnp.float32),
                pltpu.VMEM((5, 16, 8, 128), jnp.float32),
                pltpu.VMEM((2, run, 16, 128), jnp.float32),
                pltpu.VMEM((2, stack, 16, 128), jnp.float32),
                pltpu.SemaphoreType.DMA((5, 8)),
                pltpu.SemaphoreType.DMA((5, 8)),
                pltpu.SemaphoreType.DMA((2, 2)),
                pltpu.SemaphoreType.DMA((2, 2)),
            ],
            compiler_params=pltpu.CompilerParams(collective_id=0, has_side_effects=True),
        )(cotangent, conductivity, capacity, sources, jnp.asarray(const))

    split = P("height", "plane", None)
    return jax.shard_map(
        per_device,
        mesh=mesh,
        in_specs=(split, split, split, P(None, None)),
        out_specs=(split, split, P(None, None)),
        check_vma=False,
    )
```

```python
import functools

import jax
import jax.numpy as jnp
import numpy as np
from jax import lax
from jax.experimental import pallas as pl
from jax.experimental.pallas import tpu as pltpu
from jax.sharding import PartitionSpec as P

MESH = pl.DeviceIdType.MESH
HIGH = lax.Precision.HIGHEST
INV_STEP = 20.0
SHIFT = 0.75
FIELDS = (3, 1, 1, 1, 1)
STARTS = (0, 3, 4, 5, 6)
TOTAL = 7


def gll_tables():
    points = np.array(
        [
            -1.0,
            -0.8717401485096066,
            -0.5917001814331423,
            -0.2092992179024789,
            0.2092992179024789,
            0.5917001814331423,
            0.8717401485096066,
            1.0,
        ]
    )
    weights = np.array(
        [
            1.0 / 28.0,
            0.2107042271435061,
            0.3411226924835044,
            0.4124587946587038,
            0.4124587946587038,
            0.3411226924835044,
            0.2107042271435061,
            1.0 / 28.0,
        ]
    )
    product = np.array(
        [
            np.prod([points[column] - points[others] for others in range(8) if others != column])
            for column in range(8)
        ]
    )
    derivative = np.zeros((8, 8))
    for row_idx in range(8):
        for col_idx in range(8):
            if row_idx != col_idx:
                derivative[row_idx, col_idx] = product[row_idx] / (
                    product[col_idx] * (points[row_idx] - points[col_idx])
                )
        derivative[row_idx, row_idx] = -np.sum(derivative[row_idx])
    return derivative, weights


def tables():
    derivative, weights = gll_tables()
    stiff = derivative.T @ np.diag(weights) @ derivative
    scaled = stiff / weights[:, None]
    eye8, eye2, eye16 = np.eye(8), np.eye(2), np.eye(16)
    rows = np.kron(eye2, np.kron(scaled, eye8) + np.kron(eye8, scaled))
    lanes = np.kron(eye16, scaled.T)
    face = weights[:, None] * np.tile(weights, 16)[None, :]
    slope = np.diag(scaled)
    face_slope = slope[:, None] + np.tile(slope, 16)[None, :]
    const = np.concatenate([rows, lanes, face, face_slope]).astype(np.float32)
    return const, weights, slope


def kernel(
    shape,
    weights,
    slope,
    cot_ref,
    kap_ref,
    cap_ref,
    src_ref,
    const_ref,
    second_ref,
    first_ref,
    grad_ref,
    home_ref,
    moved_ref,
    back_ref,
    out_ref,
    y_ref,
    face_ref,
    plane_in,
    height_in,
    work_ref,
    mat_ref,
    tile_a,
    tile_b,
    send_sem,
    recv_sem,
    send_red,
    recv_red,
    send_move,
    recv_move,
):
    heights, planes = shape[:2]
    runs = 2
    per_run = planes // runs
    stack = heights * runs
    high = lax.axis_index("height")
    wide = lax.axis_index("plane")
    run = wide // per_run
    pos = lax.rem(wide, per_run)
    level = high * runs + run
    side = shape[2]
    rows_per_run = per_run // side

    def host(block_h, block_p):
        half = block_p // per_run
        row = lax.rem(block_p, per_run) // side
        column = lax.rem(block_p, side)
        column = column + lax.rem(row, 2) * (side - 1 - 2 * column)
        row = row + half * (rows_per_run - 1 - 2 * row)
        pair = block_h // 2
        return (2 * pair + half, lax.rem(block_h, 2) * per_run + row * side + column)

    half = lax.rem(high, 2)
    row = pos // side
    column = lax.rem(pos, side)
    row = row + half * (rows_per_run - 1 - 2 * row)
    column = column + lax.rem(row, 2) * (side - 1 - 2 * column)
    h = 2 * (high // 2) + run
    p = half * per_run + row * side + column
    target = host(high, wide)
    source = (h, p)
    moves = jnp.logical_or(h != high, p != wide)
    h_lo, h_hi = lax.rem(h + heights - 1, heights), lax.rem(h + 1, heights)
    p_lo, p_hi = lax.rem(p + planes - 1, planes), lax.rem(p + 1, planes)

    def run_peer(step):
        return (high, run * per_run + lax.rem(pos + step, per_run))

    def stack_peer(step):
        other = lax.rem(level + step, stack)
        return (other // runs, lax.rem(other, runs) * per_run + pos)

    halo = tuple(
        host(*block)
        for block in (
            (h, p_lo),
            (h, p_hi),
            (h_lo, p),
            (h_hi, p),
            (h_lo, p_lo),
            (h_lo, p_hi),
            (h_hi, p_lo),
            (h_hi, p_hi),
        )
    )
    barrier = pltpu.get_barrier_semaphore()
    for device in halo:
        pl.semaphore_signal(barrier, inc=1, device_id=device, device_id_type=MESH)

    def greet_run(step, carry):
        pl.semaphore_signal(barrier, inc=1, device_id=run_peer(step), device_id_type=MESH)
        return carry

    def greet_stack(step, carry):
        pl.semaphore_signal(barrier, inc=1, device_id=stack_peer(step), device_id_type=MESH)
        return carry

    @pl.when(moves)
    def _():
        pl.semaphore_signal(barrier, inc=1, device_id=target, device_id_type=MESH)
        pl.semaphore_signal(barrier, inc=1, device_id=source, device_id_type=MESH)

    lax.fori_loop(1, per_run, greet_run, 0)
    lax.fori_loop(1, stack, greet_stack, 0)

    has_p_lo = jnp.where(p > 0, 1.0, 0.0)
    has_p_hi = jnp.where(p < planes - 1, 1.0, 0.0)
    has_h_lo = jnp.where(h > 0, 1.0, 0.0)
    has_h_hi = jnp.where(h < heights - 1, 1.0, 0.0)

    lane = lax.broadcasted_iota(jnp.int32, (8, 128), 1)
    sub = lax.broadcasted_iota(jnp.int32, (8, 128), 0)
    lane_mod = lax.rem(lane, 8)
    opening = jnp.where((lane_mod == 0) & (lane > 0), 1.0, 0.0)
    ending = jnp.where((lane_mod == 7) & (lane < 127), 1.0, 0.0)
    row_first = jnp.where(sub == 0, 1.0, 0.0)
    row_last = jnp.where(sub == 7, 1.0, 0.0)

    spread = jnp.where(
        lax.broadcasted_iota(jnp.int32, (16, 128), 1) // 8
        == lax.broadcasted_iota(jnp.int32, (16, 128), 0),
        1.0,
        0.0,
    )
    elems = jnp.concatenate([kap_ref[0], kap_ref[1], cap_ref[0], cap_ref[1]] * 2, axis=0)
    home_ref[0:16] = cot_ref[...]
    home_ref[16] = jnp.dot(elems, spread, precision=HIGH, preferred_element_type=jnp.float32)
    greetings = 8 + per_run - 1 + stack - 1

    def move(index, source_ref, target_ref, device):
        return pltpu.make_async_remote_copy(
            src_ref=source_ref,
            dst_ref=target_ref,
            send_sem=send_move.at[index],
            recv_sem=recv_move.at[index],
            device_id=device,
            device_id_type=MESH,
        )

    bring = move(0, home_ref, moved_ref, target)

    @pl.when(moves)
    def _():
        pl.semaphore_wait(barrier, greetings + 2)
        bring.start()

    @pl.when(jnp.logical_not(moves))
    def _():
        pl.semaphore_wait(barrier, greetings)
        moved_ref[...] = home_ref[...]

    def put(slot, values):
        y_ref[slot] = values
        flat = values.reshape(128, 128)
        work_ref[slot] = flat
        for side, row in ((0, 0), (1, 7)):
            face_ref[side, slot] = work_ref.at[slot][pl.ds(row, 16, stride=8), :]

    def copies(index):
        slots = pl.ds(STARTS[index], FIELDS[index])
        routes = (
            (face_ref.at[0, slots], plane_in.at[1, slots]),
            (face_ref.at[1, slots], plane_in.at[0, slots]),
            (y_ref.at[slots, 0], height_in.at[1, slots]),
            (y_ref.at[slots, 15], height_in.at[0, slots]),
            (y_ref.at[slots, 0], height_in.at[5, slots]),
            (y_ref.at[slots, 0], height_in.at[4, slots]),
            (y_ref.at[slots, 15], height_in.at[3, slots]),
            (y_ref.at[slots, 15], height_in.at[2, slots]),
        )
        return [
            pltpu.make_async_remote_copy(
                src_ref=source,
                dst_ref=target,
                send_sem=send_sem.at[index, way],
                recv_sem=recv_sem.at[index, way],
                device_id=halo[way],
                device_id_type=MESH,
            )
            for way, (source, target) in enumerate(routes)
        ]

    def gathered(slot):
        work = work_ref.at[slot]
        work[pl.ds(0, 16, stride=8), :] += has_p_lo * plane_in[0, slot]
        work[pl.ds(7, 16, stride=8), :] += has_p_hi * plane_in[1, slot]
        low = (
            height_in[0, slot]
            + (row_first * has_p_lo) * pltpu.roll(height_in[2, slot], 1, axis=0)
            + (row_last * has_p_hi) * pltpu.roll(height_in[3, slot], 7, axis=0)
        )
        high = (
            height_in[1, slot]
            + (row_first * has_p_lo) * pltpu.roll(height_in[4, slot], 1, axis=0)
            + (row_last * has_p_hi) * pltpu.roll(height_in[5, slot], 7, axis=0)
        )
        work[0:8, :] += has_h_lo * low
        work[120:128, :] += has_h_hi * high
        joined = work[56:64, :] + work[64:72, :]
        work[56:64, :] = joined
        work[64:72, :] = joined
        flat = work[...]
        after = pltpu.roll(flat, 127, axis=1).reshape(16, 8, 128)
        before = pltpu.roll(flat, 1, axis=1).reshape(16, 8, 128)
        return flat.reshape(16, 8, 128) + ending[None] * after + opening[None] * before

    def layered(parts):
        return jnp.stack([weights[a] * parts[e] for e in range(2) for a in range(8)])

    @pl.when(moves)
    def _():
        bring.wait_recv()

    elems = moved_ref[16]
    face_w = const_ref[256:264, :]
    face_slope = const_ref[264:272, :]
    stiff_w = [face_w * elems[e : e + 1, :] for e in range(2)]
    mass_w = [face_w * (INV_STEP * elems[2 + e : 3 + e, :]) for e in range(2)]
    mass = layered(mass_w)
    conduct = layered(stiff_w)
    slopes = jnp.stack([face_slope + slope[a] for a in range(8)] * 2)

    def stiffness(values):
        flat = values.reshape(128, 128)
        inner = jnp.dot(
            const_ref[0:128, :], flat, precision=HIGH, preferred_element_type=jnp.float32
        ) + jnp.dot(flat, const_ref[128:256, :], precision=HIGH, preferred_element_type=jnp.float32)
        return mat_ref[0] * values + mat_ref[1] * inner.reshape(16, 8, 128)

    mat_ref[0] = mass
    mat_ref[1] = conduct
    put(0, mass * moved_ref[0:16])
    put(1, mass)
    put(2, mass + conduct * slopes)

    started = []

    def send(index):
        batch = copies(index)
        for copy in batch:
            copy.start()
        started.append(batch)

    def arrive(index):
        for copy in started[index]:
            copy.wait_recv()

    send(0)

    local = lax.broadcasted_iota(jnp.int32, (128, 128), 0) // 8
    hits = []
    for step in range(2):
        wanted = src_ref[step : step + 1, :]
        hits.append(
            jnp.concatenate(
                [
                    jnp.where(wanted == ((h * 2 + e) * planes + p) * 16 + local, 1.0, 0.0)
                    for e in range(2)
                ],
                axis=0,
            )
        )

    def source_sums(fields, hit):
        rows = []
        for values in fields:
            weighed = mat_ref[0] * values
            rows.append(
                jnp.concatenate(
                    [
                        jnp.sum(weighed[8 * e : 8 * e + 8].reshape(64, 128), axis=0, keepdims=True)
                        for e in range(2)
                    ],
                    axis=1,
                )
            )
        rows = jnp.concatenate(rows + [jnp.zeros((5, 256), jnp.float32)], axis=0)
        return jnp.dot(rows, hit, precision=HIGH, preferred_element_type=jnp.float32)

    depth_copies = [jnp.ones((1, 1), jnp.float32)] * 16
    depth_copies[0] = jnp.full((1, 1), 1.0 / (1.0 + has_h_lo))
    depth_copies[7] = depth_copies[8] = jnp.full((1, 1), 0.5)
    depth_copies[15] = jnp.full((1, 1), 1.0 / (1.0 + has_h_hi))
    plane_copies = (
        1.0 / ((1.0 + row_first * has_p_lo + row_last * has_p_hi) * (1.0 + opening + ending))
    )

    arrive(0)
    diag = gathered(2)
    inv_diag = 1.0 / diag
    mat_ref[2] = inv_diag
    mat_ref[3] = jnp.stack([diag[i] * plane_copies * depth_copies[i] for i in range(16)])
    mat_ref[4] = gathered(1) * inv_diag

    def dot_rows(left, right):
        return jnp.sum((left * right).reshape(128, 128), axis=0, keepdims=True)

    def total(index, tile, between):
        for stage, (ref, spot, count, peer) in enumerate(
            ((tile_a, pos, per_run, run_peer), (tile_b, level, stack, stack_peer))
        ):
            own = ref.at[index, spot]
            own[...] = tile

            def push(step, carry):
                pltpu.make_async_remote_copy(
                    src_ref=own,
                    dst_ref=own,
                    send_sem=send_red.at[index, stage],
                    recv_sem=recv_red.at[index, stage],
                    device_id=peer(step),
                    device_id_type=MESH,
                ).start()
                return carry

            lax.fori_loop(1, count, push, 0)
            if between and stage == 0:
                between()
            rest = ref.at[index, pl.ds(0, count - 1)]
            waiter = pltpu.make_async_remote_copy(
                src_ref=rest,
                dst_ref=rest,
                send_sem=send_red.at[index, stage],
                recv_sem=recv_red.at[index, stage],
                device_id=peer(1),
                device_id_type=MESH,
            )
            waiter.wait_send()
            waiter.wait_recv()
            tile = jnp.sum(ref[index], axis=0)
        return tile

    def solve(index, first, hit, keep):
        base = 2 * index + 1
        applied = stiffness(first)
        put(STARTS[base], applied)
        send(base)
        if keep:
            keep(1, first)
        weighted = mat_ref[3]
        arrive(base)
        second = gathered(STARTS[base]) * mat_ref[2] - SHIFT * first
        applied = stiffness(second)
        put(STARTS[base + 1], applied)
        send(base + 1)
        if keep:
            keep(2, second)
        m = [dot_rows(weighted * first, first), dot_rows(weighted * first, second)]
        m.append(dot_rows(weighted * second, second))
        arrive(base + 1)
        third = gathered(STARTS[base + 1]) * mat_ref[2] - SHIFT * second
        m.append(dot_rows(weighted * second, third))
        m.append(dot_rows(weighted * third, third))
        m.append(dot_rows(third, stiffness(third)) - SHIFT * m[4])
        basis = (first, second, third)
        m = [part + pltpu.roll(part, 64, axis=1) for part in m]
        m = [jnp.where(lane[0:1] < 64, m[2 * k], m[2 * k + 1]) for k in range(3)]
        sums = source_sums(basis, hit)
        tile = jnp.concatenate(m + [sums[0:3], jnp.zeros((2, 128), jnp.float32)], axis=0)
        tile = total(index, tile, (lambda: keep(3, third)) if keep else None)
        left = jnp.where(lane < 64, tile, 0.0)
        left_sum = jnp.broadcast_to(jnp.sum(left, axis=1, keepdims=True), (8, 128))
        right_sum = jnp.broadcast_to(jnp.sum(tile - left, axis=1, keepdims=True), (8, 128))
        m = [
            (right_sum if k % 2 else left_sum)[k // 2 : k // 2 + 1] for k in range(6)
        ]
        a = [m[k + 1] + SHIFT * m[k] for k in range(5)]
        pivot0 = a[0]
        l1 = a[1] / pivot0
        l2 = a[2] / pivot0
        pivot1 = a[2] - l1 * a[1]
        cross = a[3] - l1 * a[2]
        inv1 = jnp.where(pivot1 > 1e-7 * a[2], 1.0 / pivot1, 0.0)
        l12 = cross * inv1
        pivot2 = a[4] - l2 * a[2] - l12 * cross
        inv2 = jnp.where(pivot2 > 1e-7 * a[4], 1.0 / pivot2, 0.0)
        g1 = m[1] - l1 * m[0]
        g2 = m[2] - l2 * m[0] - l12 * g1
        c2 = g2 * inv2
        c1 = g1 * inv1 - l12 * c2
        c0 = m[0] / pivot0 - l1 * c1 - l2 * c2
        grads = c0 * tile[3:4] + c1 * tile[4:5] + c2 * tile[5:6]
        return (c0[None], c1[None], c2[None]), grads * (1.0 / (8.0 * INV_STEP)), basis

    def give_back(index):
        send_back = move(1 + index, out_ref.at[index], back_ref.at[index], source)

        @pl.when(moves)
        def _():
            send_back.start()

        @pl.when(jnp.logical_not(moves))
        def _():
            back_ref[index] = out_ref[index]

        return send_back

    returns = []

    def keep(index, values):
        out_ref[index] = values
        returns.append(give_back(index))

    coef, later_grad, basis = solve(0, gathered(0) * inv_diag, hits[1], None)
    later = coef[0] * basis[0] + coef[1] * basis[1] + coef[2] * basis[2]
    keep(0, later)
    coef, earlier_grad, _ = solve(1, later * mat_ref[4], hits[0], keep)
    for send_back in returns:

        @pl.when(moves)
        def _():
            send_back.wait_recv()

    second_ref[...] = back_ref[0]
    first_ref[...] = coef[0] * back_ref[1] + coef[1] * back_ref[2] + coef[2] * back_ref[3]
    grad_ref[0:1, :] = earlier_grad
    grad_ref[1:2, :] = later_grad
    for batch in started:
        for copy in batch:
            copy.wait_send()

    @pl.when(moves)
    def _():
        bring.wait_send()
        for send_back in returns:
            send_back.wait_send()


def solution(mesh):
    shape = (mesh.shape["height"], mesh.shape["plane"], 4)
    const, weights, slope = tables()
    weights = [float(value) for value in weights]
    slope = [float(value) for value in slope]
    run, stack = shape[1] // 2, shape[0] * 2

    def per_device(cotangent, conductivity, capacity, sources):
        block = jax.ShapeDtypeStruct(cotangent.shape, jnp.float32)
        return pl.pallas_call(
            functools.partial(kernel, shape, weights, slope),
            out_shape=(block, block, jax.ShapeDtypeStruct(sources.shape, jnp.float32)),
            in_specs=[pl.BlockSpec(memory_space=pltpu.VMEM)] * 5,
            out_specs=(pl.BlockSpec(memory_space=pltpu.VMEM),) * 3,
            scratch_shapes=[
                pltpu.VMEM((17, 8, 128), jnp.float32),
                pltpu.VMEM((17, 8, 128), jnp.float32),
                pltpu.VMEM((4, 16, 8, 128), jnp.float32),
                pltpu.VMEM((4, 16, 8, 128), jnp.float32),
                pltpu.VMEM((TOTAL, 16, 8, 128), jnp.float32),
                pltpu.VMEM((2, TOTAL, 16, 128), jnp.float32),
                pltpu.VMEM((2, TOTAL, 16, 128), jnp.float32),
                pltpu.VMEM((6, TOTAL, 8, 128), jnp.float32),
                pltpu.VMEM((TOTAL, 128, 128), jnp.float32),
                pltpu.VMEM((5, 16, 8, 128), jnp.float32),
                pltpu.VMEM((2, run, 8, 128), jnp.float32),
                pltpu.VMEM((2, stack, 8, 128), jnp.float32),
                pltpu.SemaphoreType.DMA((5, 8)),
                pltpu.SemaphoreType.DMA((5, 8)),
                pltpu.SemaphoreType.DMA((2, 2)),
                pltpu.SemaphoreType.DMA((2, 2)),
                pltpu.SemaphoreType.DMA((5,)),
                pltpu.SemaphoreType.DMA((5,)),
            ],
            compiler_params=pltpu.CompilerParams(collective_id=0, has_side_effects=True),
        )(cotangent, conductivity, capacity, sources, jnp.asarray(const))

    split = P("height", "plane", None)
    return jax.shard_map(
        per_device,
        mesh=mesh,
        in_specs=(split, split, split, P(None, None)),
        out_specs=(split, split, P(None, None)),
        check_vma=False,
    )
```

```python
import functools

import jax
import jax.numpy as jnp
import numpy as np
from jax import lax
from jax.experimental import pallas as pl
from jax.experimental.pallas import tpu as pltpu
from jax.sharding import PartitionSpec as P

MESH = pl.DeviceIdType.MESH
HIGH = lax.Precision.HIGHEST
INV_STEP = 20.0
SHIFT = 0.75
FIELDS = (3, 1, 1, 3, 3)
STARTS = (0, 3, 4, 5, 8)
TOTAL = 11


def gll_tables():
    points = np.array(
        [
            -1.0,
            -0.8717401485096066,
            -0.5917001814331423,
            -0.2092992179024789,
            0.2092992179024789,
            0.5917001814331423,
            0.8717401485096066,
            1.0,
        ]
    )
    weights = np.array(
        [
            1.0 / 28.0,
            0.2107042271435061,
            0.3411226924835044,
            0.4124587946587038,
            0.4124587946587038,
            0.3411226924835044,
            0.2107042271435061,
            1.0 / 28.0,
        ]
    )
    product = np.array(
        [
            np.prod([points[column] - points[others] for others in range(8) if others != column])
            for column in range(8)
        ]
    )
    derivative = np.zeros((8, 8))
    for row_idx in range(8):
        for col_idx in range(8):
            if row_idx != col_idx:
                derivative[row_idx, col_idx] = product[row_idx] / (
                    product[col_idx] * (points[row_idx] - points[col_idx])
                )
        derivative[row_idx, row_idx] = -np.sum(derivative[row_idx])
    return derivative, weights


def tables():
    derivative, weights = gll_tables()
    stiff = derivative.T @ np.diag(weights) @ derivative
    scaled = stiff / weights[:, None]
    eye8, eye2, eye16 = np.eye(8), np.eye(2), np.eye(16)
    rows = np.kron(eye2, np.kron(scaled, eye8) + np.kron(eye8, scaled))
    lanes = np.kron(eye16, scaled.T)
    face = weights[:, None] * np.tile(weights, 16)[None, :]
    slope = np.diag(scaled)
    face_slope = slope[:, None] + np.tile(slope, 16)[None, :]
    const = np.concatenate([rows, lanes, face, face_slope]).astype(np.float32)
    return const, weights, slope


def kernel(
    shape,
    weights,
    slope,
    cot_ref,
    kap_ref,
    cap_ref,
    src_ref,
    const_ref,
    second_ref,
    first_ref,
    grad_ref,
    home_ref,
    moved_ref,
    back_ref,
    out_ref,
    y_ref,
    face_ref,
    plane_in,
    height_in,
    work_ref,
    mat_ref,
    tile_a,
    tile_b,
    send_sem,
    recv_sem,
    send_red,
    recv_red,
    send_move,
    recv_move,
):
    heights, planes, side = shape
    per_run = planes // 2
    depth = heights
    rows_per_run = per_run // side
    high = lax.axis_index("height")
    wide = lax.axis_index("plane")
    run = wide // per_run
    pos = lax.rem(wide, per_run)
    core = lax.rem(high, 2)
    level = 2 * (high // 2) + run
    spot = 2 * level + core

    def host(block_h, block_p):
        half = block_p // per_run
        row = lax.rem(block_p, per_run) // side
        column = lax.rem(block_p, side)
        column = column + lax.rem(row, 2) * (side - 1 - 2 * column)
        row = row + half * (rows_per_run - 1 - 2 * row)
        pair = block_h // 2
        return (2 * pair + half, lax.rem(block_h, 2) * per_run + row * side + column)

    row_here = pos // side
    column_here = lax.rem(pos, side)
    row = row_here + core * (rows_per_run - 1 - 2 * row_here)
    column = column_here + lax.rem(row, 2) * (side - 1 - 2 * column_here)
    h = 2 * (high // 2) + run
    p = core * per_run + row * side + column
    target = host(high, wide)
    source = (h, p)
    moves = jnp.logical_or(h != high, p != wide)
    h_lo, h_hi = lax.rem(h + heights - 1, heights), lax.rem(h + 1, heights)
    p_lo, p_hi = lax.rem(p + planes - 1, planes), lax.rem(p + 1, planes)

    def layer_peer(step):
        other_row = lax.rem(row_here + step // side, rows_per_run)
        other_column = lax.rem(column_here + step % side, side)
        return (high, run * per_run + other_row * side + other_column)

    def column_peer(step):
        other = lax.rem(level + step // 2, depth)
        other_core = lax.rem(core + step % 2, 2)
        return (2 * (other // 2) + other_core, lax.rem(other, 2) * per_run + pos)

    def far(offset, size):
        return min(offset, size - offset)

    layer_steps = sorted(
        range(1, per_run), key=lambda k: -far(k // side, rows_per_run) - far(k % side, side)
    )
    column_steps = sorted(range(1, 2 * depth), key=lambda k: -far(k // 2, depth) - 0.1 * (k % 2))

    halo = tuple(
        host(*block)
        for block in (
            (h, p_lo),
            (h, p_hi),
            (h_lo, p),
            (h_hi, p),
            (h_lo, p_lo),
            (h_lo, p_hi),
            (h_hi, p_lo),
            (h_hi, p_hi),
        )
    )
    barrier = pltpu.get_barrier_semaphore()
    for device in halo:
        pl.semaphore_signal(barrier, inc=1, device_id=device, device_id_type=MESH)

    def greet_layer(step, carry):
        pl.semaphore_signal(barrier, inc=1, device_id=layer_peer(step), device_id_type=MESH)
        return carry

    def greet_column(step, carry):
        pl.semaphore_signal(barrier, inc=1, device_id=column_peer(step), device_id_type=MESH)
        return carry

    @pl.when(moves)
    def _():
        pl.semaphore_signal(barrier, inc=1, device_id=target, device_id_type=MESH)
        pl.semaphore_signal(barrier, inc=1, device_id=source, device_id_type=MESH)

    lax.fori_loop(1, per_run, greet_layer, 0)
    lax.fori_loop(1, 2 * depth, greet_column, 0)

    has_p_lo = jnp.where(p > 0, 1.0, 0.0)
    has_p_hi = jnp.where(p < planes - 1, 1.0, 0.0)
    has_h_lo = jnp.where(h > 0, 1.0, 0.0)
    has_h_hi = jnp.where(h < heights - 1, 1.0, 0.0)

    lane = lax.broadcasted_iota(jnp.int32, (8, 128), 1)
    sub = lax.broadcasted_iota(jnp.int32, (8, 128), 0)
    lane_mod = lax.rem(lane, 8)
    opening = jnp.where((lane_mod == 0) & (lane > 0), 1.0, 0.0)
    ending = jnp.where((lane_mod == 7) & (lane < 127), 1.0, 0.0)
    row_first = jnp.where(sub == 0, 1.0, 0.0)
    row_last = jnp.where(sub == 7, 1.0, 0.0)

    spread = jnp.where(
        lax.broadcasted_iota(jnp.int32, (16, 128), 1) // 8
        == lax.broadcasted_iota(jnp.int32, (16, 128), 0),
        1.0,
        0.0,
    )
    elems = jnp.concatenate([kap_ref[0], kap_ref[1], cap_ref[0], cap_ref[1]] * 2, axis=0)
    home_ref[0:16] = cot_ref[...]
    home_ref[16] = jnp.dot(elems, spread, precision=HIGH, preferred_element_type=jnp.float32)
    greetings = 8 + per_run - 1 + 2 * depth - 1

    def move(index, source_ref, target_ref, device):
        return pltpu.make_async_remote_copy(
            src_ref=source_ref,
            dst_ref=target_ref,
            send_sem=send_move.at[index],
            recv_sem=recv_move.at[index],
            device_id=device,
            device_id_type=MESH,
        )

    bring = move(0, home_ref, moved_ref, target)

    @pl.when(moves)
    def _():
        pl.semaphore_wait(barrier, greetings + 2)
        bring.start()

    @pl.when(jnp.logical_not(moves))
    def _():
        pl.semaphore_wait(barrier, greetings)
        moved_ref[...] = home_ref[...]

    started = []

    def publish(index, fields):
        slots = pl.ds(STARTS[index], FIELDS[index])
        first_rows = y_ref.at[slots, pl.ds(0, 8)]
        last_rows = y_ref.at[slots, pl.ds(120, 8)]
        routes = (
            (face_ref.at[0, slots], plane_in.at[1, slots]),
            (face_ref.at[1, slots], plane_in.at[0, slots]),
            (first_rows, height_in.at[1, slots]),
            (last_rows, height_in.at[0, slots]),
            (first_rows, height_in.at[5, slots]),
            (first_rows, height_in.at[4, slots]),
            (last_rows, height_in.at[3, slots]),
            (last_rows, height_in.at[2, slots]),
        )
        batch = [
            pltpu.make_async_remote_copy(
                src_ref=source,
                dst_ref=target,
                send_sem=send_sem.at[index, way],
                recv_sem=recv_sem.at[index, way],
                device_id=halo[way],
                device_id_type=MESH,
            )
            for way, (source, target) in enumerate(routes)
        ]
        started.append(batch)
        for offset, values in enumerate(fields):
            y_ref[STARTS[index] + offset] = values.reshape(128, 128)
        for way in (4, 5, 6, 7, 2, 3):
            batch[way].start()
        for offset in range(FIELDS[index]):
            slot = STARTS[index] + offset
            for edge, row in ((0, 0), (1, 7)):
                face_ref[edge, slot] = y_ref.at[slot][pl.ds(row, 16, stride=8), :]
        for way in (0, 1):
            batch[way].start()
        for offset, values in enumerate(fields):
            work_ref[STARTS[index] + offset] = values.reshape(128, 128)

    def arrive(index):
        for copy in started[index]:
            copy.wait_recv()

    def gathered(slot):
        work = work_ref.at[slot]
        work[pl.ds(0, 16, stride=8), :] += has_p_lo * plane_in[0, slot]
        work[pl.ds(7, 16, stride=8), :] += has_p_hi * plane_in[1, slot]
        low = (
            height_in[0, slot]
            + (row_first * has_p_lo) * pltpu.roll(height_in[2, slot], 1, axis=0)
            + (row_last * has_p_hi) * pltpu.roll(height_in[3, slot], 7, axis=0)
        )
        high = (
            height_in[1, slot]
            + (row_first * has_p_lo) * pltpu.roll(height_in[4, slot], 1, axis=0)
            + (row_last * has_p_hi) * pltpu.roll(height_in[5, slot], 7, axis=0)
        )
        work[0:8, :] += has_h_lo * low
        work[120:128, :] += has_h_hi * high
        joined = work[56:64, :] + work[64:72, :]
        work[56:64, :] = joined
        work[64:72, :] = joined
        flat = work[...]
        after = pltpu.roll(flat, 127, axis=1).reshape(16, 8, 128)
        before = pltpu.roll(flat, 1, axis=1).reshape(16, 8, 128)
        return flat.reshape(16, 8, 128) + ending[None] * after + opening[None] * before

    def layered(parts):
        return jnp.stack([weights[a] * parts[e] for e in range(2) for a in range(8)])

    @pl.when(moves)
    def _():
        bring.wait_recv()

    elems = moved_ref[16]
    face_w = const_ref[256:264, :]
    face_slope = const_ref[264:272, :]
    stiff_w = [face_w * elems[e : e + 1, :] for e in range(2)]
    mass_w = [face_w * (INV_STEP * elems[2 + e : 3 + e, :]) for e in range(2)]
    mass = layered(mass_w)
    conduct = layered(stiff_w)
    slopes = jnp.stack([face_slope + slope[a] for a in range(8)] * 2)

    def stiffness(*fields):
        flats = [values.reshape(128, 128) for values in fields]
        across = jnp.dot(
            const_ref[0:128, :],
            jnp.concatenate(flats, axis=1),
            precision=HIGH,
            preferred_element_type=jnp.float32,
        )
        along = jnp.dot(
            jnp.concatenate(flats, axis=0),
            const_ref[128:256, :],
            precision=HIGH,
            preferred_element_type=jnp.float32,
        )
        return [
            mat_ref[0] * values
            + mat_ref[1]
            * (
                across[:, 128 * k : 128 * k + 128] + along[128 * k : 128 * k + 128]
            ).reshape(16, 8, 128)
            for k, values in enumerate(fields)
        ]

    mat_ref[0] = mass
    mat_ref[1] = conduct
    publish(0, (mass * moved_ref[0:16], mass, mass + conduct * slopes))

    local = lax.broadcasted_iota(jnp.int32, (128, 128), 0) // 8
    hits = []
    for step in range(2):
        wanted = src_ref[step : step + 1, :]
        hits.append(
            jnp.concatenate(
                [
                    jnp.where(wanted == ((h * 2 + e) * planes + p) * 16 + local, 1.0, 0.0)
                    for e in range(2)
                ],
                axis=0,
            )
        )

    def source_sums(fields, hit):
        rows = []
        for values in fields:
            weighed = mat_ref[0] * values
            rows.append(
                jnp.concatenate(
                    [
                        jnp.sum(weighed[8 * e : 8 * e + 8].reshape(64, 128), axis=0, keepdims=True)
                        for e in range(2)
                    ],
                    axis=1,
                )
            )
        rows = jnp.concatenate(rows + [jnp.zeros((5, 256), jnp.float32)], axis=0)
        return jnp.dot(rows, hit, precision=HIGH, preferred_element_type=jnp.float32)

    depth_copies = [jnp.ones((1, 1), jnp.float32)] * 16
    depth_copies[0] = jnp.full((1, 1), 1.0 / (1.0 + has_h_lo))
    depth_copies[7] = depth_copies[8] = jnp.full((1, 1), 0.5)
    depth_copies[15] = jnp.full((1, 1), 1.0 / (1.0 + has_h_hi))
    plane_copies = (
        1.0 / ((1.0 + row_first * has_p_lo + row_last * has_p_hi) * (1.0 + opening + ending))
    )

    arrive(0)
    diag = gathered(2)
    inv_diag = 1.0 / diag
    mat_ref[2] = inv_diag
    mat_ref[3] = jnp.stack([diag[i] * plane_copies * depth_copies[i] for i in range(16)])
    mat_ref[4] = gathered(1) * inv_diag

    def dot_rows(left, right):
        return jnp.sum((left * right).reshape(128, 128), axis=0, keepdims=True)

    stages = (
        (tile_a, pos, per_run, layer_peer, layer_steps),
        (tile_b, spot, 2 * depth, column_peer, column_steps),
    )

    def push(index, stage, tile):
        ref, slot, _, peer, steps = stages[stage]
        own = ref.at[index, slot]
        own[...] = tile
        for step in steps:
            pltpu.make_async_remote_copy(
                src_ref=own,
                dst_ref=own,
                send_sem=send_red.at[index, stage],
                recv_sem=recv_red.at[index, stage],
                device_id=peer(step),
                device_id_type=MESH,
            ).start()

    def rest(index, stage):
        ref, _, count, peer, _ = stages[stage]
        others = ref.at[index, pl.ds(0, count - 1)]
        return pltpu.make_async_remote_copy(
            src_ref=others,
            dst_ref=others,
            send_sem=send_red.at[index, stage],
            recv_sem=recv_red.at[index, stage],
            device_id=peer(1),
            device_id_type=MESH,
        )

    def pull(index, stage):
        rest(index, stage).wait_recv()
        return jnp.sum(stages[stage][0][index], axis=0)

    weighted = mat_ref[3]

    def moments(first, second, third, applied):
        m = [dot_rows(weighted * first, first), dot_rows(weighted * first, second)]
        m.append(dot_rows(weighted * second, second))
        m.append(dot_rows(weighted * second, third))
        m.append(dot_rows(weighted * third, third))
        m.append(dot_rows(third, applied) - SHIFT * m[4])
        m = [part + pltpu.roll(part, 64, axis=1) for part in m]
        return [jnp.where(lane[0:1] < 64, m[2 * k], m[2 * k + 1]) for k in range(3)]

    def coefficients(tile):
        left = jnp.where(lane < 64, tile, 0.0)
        left_sum = jnp.broadcast_to(jnp.sum(left, axis=1, keepdims=True), (8, 128))
        right_sum = jnp.broadcast_to(jnp.sum(tile - left, axis=1, keepdims=True), (8, 128))
        m = [(right_sum if k % 2 else left_sum)[k // 2 : k // 2 + 1] for k in range(6)]
        a = [m[k + 1] + SHIFT * m[k] for k in range(5)]
        pivot0 = a[0]
        l1 = a[1] / pivot0
        l2 = a[2] / pivot0
        pivot1 = a[2] - l1 * a[1]
        cross = a[3] - l1 * a[2]
        inv1 = jnp.where(pivot1 > 1e-7 * a[2], 1.0 / pivot1, 0.0)
        l12 = cross * inv1
        pivot2 = a[4] - l2 * a[2] - l12 * cross
        inv2 = jnp.where(pivot2 > 1e-7 * a[4], 1.0 / pivot2, 0.0)
        g1 = m[1] - l1 * m[0]
        g2 = m[2] - l2 * m[0] - l12 * g1
        c2 = g2 * inv2
        c1 = g1 * inv1 - l12 * c2
        c0 = m[0] / pivot0 - l1 * c1 - l2 * c2
        return c0, c1, c2

    def blend(coef, basis):
        return coef[0] * basis[0] + coef[1] * basis[1] + coef[2] * basis[2]

    returns = []

    def keep(index, values):
        out_ref[index] = values
        send_back = move(1 + index, out_ref.at[index], back_ref.at[index], source)

        @pl.when(moves)
        def _():
            send_back.start()

        @pl.when(jnp.logical_not(moves))
        def _():
            back_ref[index] = out_ref[index]

        returns.append(send_back)

    def advance(index, previous):
        arrive(index)
        return [
            gathered(STARTS[index] + k) * mat_ref[2] - SHIFT * values
            for k, values in enumerate(previous)
        ]

    zeros = jnp.zeros((1, 128), jnp.float32)
    v0 = gathered(0) * inv_diag
    publish(1, stiffness(v0))
    (v1,) = advance(1, (v0,))
    publish(2, stiffness(v1))
    (v2,) = advance(2, (v1,))
    basis = (v0, v1, v2)
    w0 = [values * mat_ref[4] for values in basis]
    publish(3, stiffness(*w0))
    sums = source_sums(basis, hits[1])
    push(
        0,
        0,
        jnp.concatenate(
            moments(v0, v1, v2, stiffness(v2)[0]) + [sums[0:3], zeros, zeros], axis=0
        ),
    )
    w1 = advance(3, w0)
    publish(4, stiffness(*w1))
    push(0, 1, pull(0, 0))
    w2 = advance(4, w1)
    tile = pull(0, 1)
    coef = coefficients(tile)
    later_grad = blend(coef, [tile[3 + k : 4 + k] for k in range(3)])
    wide_coef = [c[None] for c in coef]
    later = blend(wide_coef, basis)
    basis = [blend(wide_coef, fields) for fields in (w0, w1, w2)]
    sums = source_sums(basis, hits[0])
    push(
        1,
        0,
        jnp.concatenate(
            moments(*basis, stiffness(basis[2])[0]) + [sums[0:3], zeros, zeros], axis=0
        ),
    )
    keep(0, later)
    for k in range(3):
        keep(1 + k, basis[k])
    push(1, 1, pull(1, 0))
    tile = pull(1, 1)
    coef = coefficients(tile)
    earlier_grad = blend(coef, [tile[3 + k : 4 + k] for k in range(3)])

    @pl.when(moves)
    def _():
        for send_back in returns:
            send_back.wait_recv()

    second_ref[...] = back_ref[0]
    first_ref[...] = blend([c[None] for c in coef], [back_ref[1 + k] for k in range(3)])
    scale = 1.0 / (8.0 * INV_STEP)
    grad_ref[0:1, :] = earlier_grad * scale
    grad_ref[1:2, :] = later_grad * scale
    for index in range(2):
        for stage in range(2):
            rest(index, stage).wait_send()
    for batch in started:
        for copy in batch:
            copy.wait_send()

    @pl.when(moves)
    def _():
        bring.wait_send()
        for send_back in returns:
            send_back.wait_send()


def solution(mesh):
    shape = (mesh.shape["height"], mesh.shape["plane"], 4)
    const, weights, slope = tables()
    weights = [float(value) for value in weights]
    slope = [float(value) for value in slope]
    run, stack = shape[1] // 2, shape[0] * 2

    def per_device(cotangent, conductivity, capacity, sources):
        block = jax.ShapeDtypeStruct(cotangent.shape, jnp.float32)
        return pl.pallas_call(
            functools.partial(kernel, shape, weights, slope),
            out_shape=(block, block, jax.ShapeDtypeStruct(sources.shape, jnp.float32)),
            in_specs=[pl.BlockSpec(memory_space=pltpu.VMEM)] * 5,
            out_specs=(pl.BlockSpec(memory_space=pltpu.VMEM),) * 3,
            scratch_shapes=[
                pltpu.VMEM((17, 8, 128), jnp.float32),
                pltpu.VMEM((17, 8, 128), jnp.float32),
                pltpu.VMEM((4, 16, 8, 128), jnp.float32),
                pltpu.VMEM((4, 16, 8, 128), jnp.float32),
                pltpu.VMEM((TOTAL, 128, 128), jnp.float32),
                pltpu.VMEM((2, TOTAL, 16, 128), jnp.float32),
                pltpu.VMEM((2, TOTAL, 16, 128), jnp.float32),
                pltpu.VMEM((6, TOTAL, 8, 128), jnp.float32),
                pltpu.VMEM((TOTAL, 128, 128), jnp.float32),
                pltpu.VMEM((5, 16, 8, 128), jnp.float32),
                pltpu.VMEM((2, run, 8, 128), jnp.float32),
                pltpu.VMEM((2, stack, 8, 128), jnp.float32),
                pltpu.SemaphoreType.DMA((5, 8)),
                pltpu.SemaphoreType.DMA((5, 8)),
                pltpu.SemaphoreType.DMA((2, 2)),
                pltpu.SemaphoreType.DMA((2, 2)),
                pltpu.SemaphoreType.DMA((5,)),
                pltpu.SemaphoreType.DMA((5,)),
            ],
            compiler_params=pltpu.CompilerParams(collective_id=0, has_side_effects=True),
        )(cotangent, conductivity, capacity, sources, jnp.asarray(const))

    split = P("height", "plane", None)
    return jax.shard_map(
        per_device,
        mesh=mesh,
        in_specs=(split, split, split, P(None, None)),
        out_specs=(split, split, P(None, None)),
        check_vma=False,
    )
```

```python
import functools

import jax
import jax.numpy as jnp
import numpy as np
from jax import lax
from jax.experimental import pallas as pl
from jax.experimental.pallas import tpu as pltpu
from jax.sharding import PartitionSpec as P

MESH = pl.DeviceIdType.MESH
HIGH = lax.Precision.HIGHEST
INV_STEP = 20.0
SHIFT = 0.75
FIELDS = (3, 1, 1, 3, 3)
STARTS = (0, 3, 4, 5, 8)
TOTAL = 11


def gll_tables():
    points = np.array(
        [
            -1.0,
            -0.8717401485096066,
            -0.5917001814331423,
            -0.2092992179024789,
            0.2092992179024789,
            0.5917001814331423,
            0.8717401485096066,
            1.0,
        ]
    )
    weights = np.array(
        [
            1.0 / 28.0,
            0.2107042271435061,
            0.3411226924835044,
            0.4124587946587038,
            0.4124587946587038,
            0.3411226924835044,
            0.2107042271435061,
            1.0 / 28.0,
        ]
    )
    product = np.array(
        [
            np.prod([points[column] - points[others] for others in range(8) if others != column])
            for column in range(8)
        ]
    )
    derivative = np.zeros((8, 8))
    for row_idx in range(8):
        for col_idx in range(8):
            if row_idx != col_idx:
                derivative[row_idx, col_idx] = product[row_idx] / (
                    product[col_idx] * (points[row_idx] - points[col_idx])
                )
        derivative[row_idx, row_idx] = -np.sum(derivative[row_idx])
    return derivative, weights


def tables():
    derivative, weights = gll_tables()
    stiff = derivative.T @ np.diag(weights) @ derivative
    scaled = stiff / weights[:, None]
    eye8, eye2, eye16 = np.eye(8), np.eye(2), np.eye(16)
    rows = np.kron(eye2, np.kron(scaled, eye8) + np.kron(eye8, scaled))
    lanes = np.kron(eye16, scaled.T)
    face = weights[:, None] * np.tile(weights, 16)[None, :]
    slope = np.diag(scaled)
    face_slope = slope[:, None] + np.tile(slope, 16)[None, :]
    const = np.concatenate([rows, lanes, face, face_slope]).astype(np.float32)
    return const, weights, slope


def kernel(
    shape,
    weights,
    slope,
    cot_hbm,
    kap_hbm,
    cap_hbm,
    src_hbm,
    const_hbm,
    second_ref,
    first_ref,
    grad_ref,
    kap_ref,
    cap_ref,
    src_ref,
    const_ref,
    home_ref,
    moved_ref,
    back_ref,
    out_ref,
    y_ref,
    face_ref,
    plane_in,
    height_in,
    work_ref,
    mat_ref,
    tile_a,
    tile_b,
    send_sem,
    recv_sem,
    send_red,
    recv_red,
    send_move,
    recv_move,
    load_sem,
):
    loads = [
        pltpu.make_async_copy(operand, place, load_sem.at[index])
        for index, (operand, place) in enumerate(
            (
                (kap_hbm, kap_ref),
                (cap_hbm, cap_ref),
                (cot_hbm, home_ref.at[pl.ds(0, 16)]),
                (const_hbm, const_ref),
                (src_hbm, src_ref),
            )
        )
    ]
    for load in loads:
        load.start()
    heights, planes, side = shape
    per_run = planes // 2
    depth = heights
    rows_per_run = per_run // side
    high = lax.axis_index("height")
    wide = lax.axis_index("plane")
    run = wide // per_run
    pos = lax.rem(wide, per_run)
    core = lax.rem(high, 2)
    level = 2 * (high // 2) + run
    spot = 2 * level + core

    def host(block_h, block_p):
        half = block_p // per_run
        row = lax.rem(block_p, per_run) // side
        column = lax.rem(block_p, side)
        column = column + lax.rem(row, 2) * (side - 1 - 2 * column)
        row = row + half * (rows_per_run - 1 - 2 * row)
        pair = block_h // 2
        return (2 * pair + half, lax.rem(block_h, 2) * per_run + row * side + column)

    row_here = pos // side
    column_here = lax.rem(pos, side)
    row = row_here + core * (rows_per_run - 1 - 2 * row_here)
    column = column_here + lax.rem(row, 2) * (side - 1 - 2 * column_here)
    h = 2 * (high // 2) + run
    p = core * per_run + row * side + column
    target = host(high, wide)
    source = (h, p)
    moves = jnp.logical_or(h != high, p != wide)
    h_lo, h_hi = lax.rem(h + heights - 1, heights), lax.rem(h + 1, heights)
    p_lo, p_hi = lax.rem(p + planes - 1, planes), lax.rem(p + 1, planes)

    def layer_peer(step):
        other_row = lax.rem(row_here + step // side, rows_per_run)
        other_column = lax.rem(column_here + step % side, side)
        return (high, run * per_run + other_row * side + other_column)

    def column_peer(step):
        other = lax.rem(level + step // 2, depth)
        other_core = lax.rem(core + step % 2, 2)
        return (2 * (other // 2) + other_core, lax.rem(other, 2) * per_run + pos)

    def far(offset, size):
        return min(offset, size - offset)

    layer_steps = sorted(
        range(1, per_run), key=lambda k: -far(k // side, rows_per_run) - far(k % side, side)
    )
    column_steps = sorted(range(1, 2 * depth), key=lambda k: -far(k // 2, depth) - 0.1 * (k % 2))

    halo = tuple(
        host(*block)
        for block in (
            (h, p_lo),
            (h, p_hi),
            (h_lo, p),
            (h_hi, p),
            (h_lo, p_lo),
            (h_lo, p_hi),
            (h_hi, p_lo),
            (h_hi, p_hi),
        )
    )
    barrier = pltpu.get_barrier_semaphore()
    for device in halo:
        pl.semaphore_signal(barrier, inc=1, device_id=device, device_id_type=MESH)

    def greet_layer(step, carry):
        pl.semaphore_signal(barrier, inc=1, device_id=layer_peer(step), device_id_type=MESH)
        return carry

    def greet_column(step, carry):
        pl.semaphore_signal(barrier, inc=1, device_id=column_peer(step), device_id_type=MESH)
        return carry

    @pl.when(moves)
    def _():
        pl.semaphore_signal(barrier, inc=1, device_id=target, device_id_type=MESH)
        pl.semaphore_signal(barrier, inc=1, device_id=source, device_id_type=MESH)

    lax.fori_loop(1, per_run, greet_layer, 0)
    lax.fori_loop(1, 2 * depth, greet_column, 0)

    has_p_lo = jnp.where(p > 0, 1.0, 0.0)
    has_p_hi = jnp.where(p < planes - 1, 1.0, 0.0)
    has_h_lo = jnp.where(h > 0, 1.0, 0.0)
    has_h_hi = jnp.where(h < heights - 1, 1.0, 0.0)

    lane = lax.broadcasted_iota(jnp.int32, (8, 128), 1)
    sub = lax.broadcasted_iota(jnp.int32, (8, 128), 0)
    lane_mod = lax.rem(lane, 8)
    opening = jnp.where((lane_mod == 0) & (lane > 0), 1.0, 0.0)
    ending = jnp.where((lane_mod == 7) & (lane < 127), 1.0, 0.0)
    row_first = jnp.where(sub == 0, 1.0, 0.0)
    row_last = jnp.where(sub == 7, 1.0, 0.0)

    spread = jnp.where(
        lax.broadcasted_iota(jnp.int32, (16, 128), 1) // 8
        == lax.broadcasted_iota(jnp.int32, (16, 128), 0),
        1.0,
        0.0,
    )
    for load in loads[:2]:
        load.wait()
    elems = jnp.concatenate([kap_ref[0], kap_ref[1], cap_ref[0], cap_ref[1]] * 2, axis=0)
    home_ref[16] = jnp.dot(elems, spread, precision=HIGH, preferred_element_type=jnp.float32)
    for load in loads[2:]:
        load.wait()
    greetings = 8 + per_run - 1 + 2 * depth - 1

    def move(index, source_ref, target_ref, device):
        return pltpu.make_async_remote_copy(
            src_ref=source_ref,
            dst_ref=target_ref,
            send_sem=send_move.at[index],
            recv_sem=recv_move.at[index],
            device_id=device,
            device_id_type=MESH,
        )

    bring = move(0, home_ref, moved_ref, target)

    @pl.when(moves)
    def _():
        pl.semaphore_wait(barrier, greetings + 2)
        bring.start()

    @pl.when(jnp.logical_not(moves))
    def _():
        pl.semaphore_wait(barrier, greetings)
        moved_ref[...] = home_ref[...]

    started = []

    def publish(index, fields):
        slots = pl.ds(STARTS[index], FIELDS[index])
        first_rows = y_ref.at[slots, pl.ds(0, 8)]
        last_rows = y_ref.at[slots, pl.ds(120, 8)]
        routes = (
            (face_ref.at[0, slots], plane_in.at[1, slots]),
            (face_ref.at[1, slots], plane_in.at[0, slots]),
            (first_rows, height_in.at[1, slots]),
            (last_rows, height_in.at[0, slots]),
            (first_rows, height_in.at[5, slots]),
            (first_rows, height_in.at[4, slots]),
            (last_rows, height_in.at[3, slots]),
            (last_rows, height_in.at[2, slots]),
        )
        batch = [
            pltpu.make_async_remote_copy(
                src_ref=source,
                dst_ref=target,
                send_sem=send_sem.at[index, way],
                recv_sem=recv_sem.at[index, way],
                device_id=halo[way],
                device_id_type=MESH,
            )
            for way, (source, target) in enumerate(routes)
        ]
        started.append(batch)
        for offset, values in enumerate(fields):
            y_ref[STARTS[index] + offset] = values.reshape(128, 128)
        for way in (4, 5, 6, 7, 2, 3):
            batch[way].start()
        for offset in range(FIELDS[index]):
            slot = STARTS[index] + offset
            for edge, row in ((0, 0), (1, 7)):
                face_ref[edge, slot] = y_ref.at[slot][pl.ds(row, 16, stride=8), :]
        for way in (0, 1):
            batch[way].start()
        for offset, values in enumerate(fields):
            work_ref[STARTS[index] + offset] = values.reshape(128, 128)

    def arrive(index):
        for copy in started[index]:
            copy.wait_recv()

    def gathered(slot):
        work = work_ref.at[slot]
        work[pl.ds(0, 16, stride=8), :] += has_p_lo * plane_in[0, slot]
        work[pl.ds(7, 16, stride=8), :] += has_p_hi * plane_in[1, slot]
        low = (
            height_in[0, slot]
            + (row_first * has_p_lo) * pltpu.roll(height_in[2, slot], 1, axis=0)
            + (row_last * has_p_hi) * pltpu.roll(height_in[3, slot], 7, axis=0)
        )
        high = (
            height_in[1, slot]
            + (row_first * has_p_lo) * pltpu.roll(height_in[4, slot], 1, axis=0)
            + (row_last * has_p_hi) * pltpu.roll(height_in[5, slot], 7, axis=0)
        )
        work[0:8, :] += has_h_lo * low
        work[120:128, :] += has_h_hi * high
        joined = work[56:64, :] + work[64:72, :]
        work[56:64, :] = joined
        work[64:72, :] = joined
        flat = work[...]
        after = pltpu.roll(flat, 127, axis=1).reshape(16, 8, 128)
        before = pltpu.roll(flat, 1, axis=1).reshape(16, 8, 128)
        return flat.reshape(16, 8, 128) + ending[None] * after + opening[None] * before

    def layered(parts):
        return jnp.stack([weights[a] * parts[e] for e in range(2) for a in range(8)])

    @pl.when(moves)
    def _():
        bring.wait_recv()

    elems = moved_ref[16]
    face_w = const_ref[256:264, :]
    face_slope = const_ref[264:272, :]
    stiff_w = [face_w * elems[e : e + 1, :] for e in range(2)]
    mass_w = [face_w * (INV_STEP * elems[2 + e : 3 + e, :]) for e in range(2)]
    mass = layered(mass_w)
    conduct = layered(stiff_w)
    slopes = jnp.stack([face_slope + slope[a] for a in range(8)] * 2)

    def stiffness(*fields):
        flats = [values.reshape(128, 128) for values in fields]
        across = jnp.dot(
            const_ref[0:128, :],
            jnp.concatenate(flats, axis=1),
            precision=HIGH,
            preferred_element_type=jnp.float32,
        )
        along = jnp.dot(
            jnp.concatenate(flats, axis=0),
            const_ref[128:256, :],
            precision=HIGH,
            preferred_element_type=jnp.float32,
        )
        return [
            mat_ref[0] * values
            + mat_ref[1]
            * (
                across[:, 128 * k : 128 * k + 128] + along[128 * k : 128 * k + 128]
            ).reshape(16, 8, 128)
            for k, values in enumerate(fields)
        ]

    mat_ref[0] = mass
    mat_ref[1] = conduct
    publish(0, (mass * moved_ref[0:16], mass, mass + conduct * slopes))

    local = lax.broadcasted_iota(jnp.int32, (128, 128), 0) // 8
    hits = []
    for step in range(2):
        wanted = src_ref[step : step + 1, :]
        hits.append(
            jnp.concatenate(
                [
                    jnp.where(wanted == ((h * 2 + e) * planes + p) * 16 + local, 1.0, 0.0)
                    for e in range(2)
                ],
                axis=0,
            )
        )

    def source_sums(fields, hit):
        rows = []
        for values in fields:
            weighed = mat_ref[0] * values
            rows.append(
                jnp.concatenate(
                    [
                        jnp.sum(weighed[8 * e : 8 * e + 8].reshape(64, 128), axis=0, keepdims=True)
                        for e in range(2)
                    ],
                    axis=1,
                )
            )
        rows = jnp.concatenate(rows + [jnp.zeros((5, 256), jnp.float32)], axis=0)
        return jnp.dot(rows, hit, precision=HIGH, preferred_element_type=jnp.float32)

    depth_copies = [jnp.ones((1, 1), jnp.float32)] * 16
    depth_copies[0] = jnp.full((1, 1), 1.0 / (1.0 + has_h_lo))
    depth_copies[7] = depth_copies[8] = jnp.full((1, 1), 0.5)
    depth_copies[15] = jnp.full((1, 1), 1.0 / (1.0 + has_h_hi))
    plane_copies = (
        1.0 / ((1.0 + row_first * has_p_lo + row_last * has_p_hi) * (1.0 + opening + ending))
    )

    arrive(0)
    diag = gathered(2)
    inv_diag = 1.0 / diag
    mat_ref[2] = inv_diag
    mat_ref[3] = jnp.stack([diag[i] * plane_copies * depth_copies[i] for i in range(16)])
    mat_ref[4] = gathered(1) * inv_diag

    def dot_rows(left, right):
        return jnp.sum((left * right).reshape(128, 128), axis=0, keepdims=True)

    stages = (
        (tile_a, pos, per_run, layer_peer, layer_steps),
        (tile_b, spot, 2 * depth, column_peer, column_steps),
    )

    def push(index, stage, tile):
        ref, slot, _, peer, steps = stages[stage]
        own = ref.at[index, slot]
        own[...] = tile
        for step in steps:
            pltpu.make_async_remote_copy(
                src_ref=own,
                dst_ref=own,
                send_sem=send_red.at[index, stage],
                recv_sem=recv_red.at[index, stage],
                device_id=peer(step),
                device_id_type=MESH,
            ).start()

    def rest(index, stage):
        ref, _, count, peer, _ = stages[stage]
        others = ref.at[index, pl.ds(0, count - 1)]
        return pltpu.make_async_remote_copy(
            src_ref=others,
            dst_ref=others,
            send_sem=send_red.at[index, stage],
            recv_sem=recv_red.at[index, stage],
            device_id=peer(1),
            device_id_type=MESH,
        )

    def pull(index, stage):
        rest(index, stage).wait_recv()
        return jnp.sum(stages[stage][0][index], axis=0)

    weighted = mat_ref[3]

    def moments(first, second, third, applied):
        m = [dot_rows(weighted * first, first), dot_rows(weighted * first, second)]
        m.append(dot_rows(weighted * second, second))
        m.append(dot_rows(weighted * second, third))
        m.append(dot_rows(weighted * third, third))
        m.append(dot_rows(third, applied) - SHIFT * m[4])
        m = [part + pltpu.roll(part, 64, axis=1) for part in m]
        return [jnp.where(lane[0:1] < 64, m[2 * k], m[2 * k + 1]) for k in range(3)]

    def coefficients(tile):
        left = jnp.where(lane < 64, tile, 0.0)
        left_sum = jnp.broadcast_to(jnp.sum(left, axis=1, keepdims=True), (8, 128))
        right_sum = jnp.broadcast_to(jnp.sum(tile - left, axis=1, keepdims=True), (8, 128))
        m = [(right_sum if k % 2 else left_sum)[k // 2 : k // 2 + 1] for k in range(6)]
        a = [m[k + 1] + SHIFT * m[k] for k in range(5)]
        pivot0 = a[0]
        l1 = a[1] / pivot0
        l2 = a[2] / pivot0
        pivot1 = a[2] - l1 * a[1]
        cross = a[3] - l1 * a[2]
        inv1 = jnp.where(pivot1 > 1e-7 * a[2], 1.0 / pivot1, 0.0)
        l12 = cross * inv1
        pivot2 = a[4] - l2 * a[2] - l12 * cross
        inv2 = jnp.where(pivot2 > 1e-7 * a[4], 1.0 / pivot2, 0.0)
        g1 = m[1] - l1 * m[0]
        g2 = m[2] - l2 * m[0] - l12 * g1
        c2 = g2 * inv2
        c1 = g1 * inv1 - l12 * c2
        c0 = m[0] / pivot0 - l1 * c1 - l2 * c2
        return c0, c1, c2

    def blend(coef, basis):
        return coef[0] * basis[0] + coef[1] * basis[1] + coef[2] * basis[2]

    returns = []

    def keep(index, values):
        out_ref[index] = values
        send_back = move(1 + index, out_ref.at[index], back_ref.at[index], source)

        @pl.when(moves)
        def _():
            send_back.start()

        @pl.when(jnp.logical_not(moves))
        def _():
            back_ref[index] = out_ref[index]

        returns.append(send_back)

    def advance(index, previous):
        arrive(index)
        return [
            gathered(STARTS[index] + k) * mat_ref[2] - SHIFT * values
            for k, values in enumerate(previous)
        ]

    zeros = jnp.zeros((1, 128), jnp.float32)
    v0 = gathered(0) * inv_diag
    publish(1, stiffness(v0))
    (v1,) = advance(1, (v0,))
    publish(2, stiffness(v1))
    (v2,) = advance(2, (v1,))
    basis = (v0, v1, v2)
    w0 = [values * mat_ref[4] for values in basis]
    publish(3, stiffness(*w0))
    sums = source_sums(basis, hits[1])
    push(
        0,
        0,
        jnp.concatenate(
            moments(v0, v1, v2, stiffness(v2)[0]) + [sums[0:3], zeros, zeros], axis=0
        ),
    )
    w1 = advance(3, w0)
    publish(4, stiffness(*w1))
    push(0, 1, pull(0, 0))
    w2 = advance(4, w1)
    tile = pull(0, 1)
    coef = coefficients(tile)
    later_grad = blend(coef, [tile[3 + k : 4 + k] for k in range(3)])
    wide_coef = [c[None] for c in coef]
    later = blend(wide_coef, basis)
    basis = [blend(wide_coef, fields) for fields in (w0, w1, w2)]
    sums = source_sums(basis, hits[0])
    push(
        1,
        0,
        jnp.concatenate(
            moments(*basis, stiffness(basis[2])[0]) + [sums[0:3], zeros, zeros], axis=0
        ),
    )
    keep(0, later)
    for k in range(3):
        keep(1 + k, basis[k])
    push(1, 1, pull(1, 0))
    tile = pull(1, 1)
    coef = coefficients(tile)
    earlier_grad = blend(coef, [tile[3 + k : 4 + k] for k in range(3)])

    @pl.when(moves)
    def _():
        for send_back in returns:
            send_back.wait_recv()

    second_ref[...] = back_ref[0]
    first_ref[...] = blend([c[None] for c in coef], [back_ref[1 + k] for k in range(3)])
    scale = 1.0 / (8.0 * INV_STEP)
    grad_ref[0:1, :] = earlier_grad * scale
    grad_ref[1:2, :] = later_grad * scale
    for index in range(2):
        for stage in range(2):
            rest(index, stage).wait_send()
    for batch in started:
        for copy in batch:
            copy.wait_send()

    @pl.when(moves)
    def _():
        bring.wait_send()
        for send_back in returns:
            send_back.wait_send()


def write_out(*refs):
    sources, targets, sems = refs[:3], refs[3:6], refs[6]
    stores = [
        pltpu.make_async_copy(source, target, sems.at[index])
        for index, (source, target) in enumerate(zip(sources, targets))
    ]
    for store in stores:
        store.start()
    for store in stores:
        store.wait()


def solution(mesh):
    shape = (mesh.shape["height"], mesh.shape["plane"], 4)
    const, weights, slope = tables()
    weights = [float(value) for value in weights]
    slope = [float(value) for value in slope]
    run, stack = shape[1] // 2, shape[0] * 2

    def per_device(cotangent, conductivity, capacity, sources):
        block = jax.ShapeDtypeStruct(cotangent.shape, jnp.float32)
        outs = (block, block, jax.ShapeDtypeStruct(sources.shape, jnp.float32))
        results = pl.pallas_call(
            functools.partial(kernel, shape, weights, slope),
            out_shape=tuple(pltpu.VMEM(item.shape, item.dtype) for item in outs),
            in_specs=[pl.BlockSpec(memory_space=pl.ANY)] * 5,
            out_specs=(pl.BlockSpec(memory_space=pltpu.VMEM),) * 3,
            scratch_shapes=[
                pltpu.VMEM(conductivity.shape, jnp.float32),
                pltpu.VMEM(capacity.shape, jnp.float32),
                pltpu.VMEM(sources.shape, jnp.int32),
                pltpu.VMEM(const.shape, jnp.float32),
                pltpu.VMEM((17, 8, 128), jnp.float32),
                pltpu.VMEM((17, 8, 128), jnp.float32),
                pltpu.VMEM((4, 16, 8, 128), jnp.float32),
                pltpu.VMEM((4, 16, 8, 128), jnp.float32),
                pltpu.VMEM((TOTAL, 128, 128), jnp.float32),
                pltpu.VMEM((2, TOTAL, 16, 128), jnp.float32),
                pltpu.VMEM((2, TOTAL, 16, 128), jnp.float32),
                pltpu.VMEM((6, TOTAL, 8, 128), jnp.float32),
                pltpu.VMEM((TOTAL, 128, 128), jnp.float32),
                pltpu.VMEM((5, 16, 8, 128), jnp.float32),
                pltpu.VMEM((2, run, 8, 128), jnp.float32),
                pltpu.VMEM((2, stack, 8, 128), jnp.float32),
                pltpu.SemaphoreType.DMA((5, 8)),
                pltpu.SemaphoreType.DMA((5, 8)),
                pltpu.SemaphoreType.DMA((2, 2)),
                pltpu.SemaphoreType.DMA((2, 2)),
                pltpu.SemaphoreType.DMA((5,)),
                pltpu.SemaphoreType.DMA((5,)),
                pltpu.SemaphoreType.DMA((5,)),
            ],
            compiler_params=pltpu.CompilerParams(collective_id=0, has_side_effects=True),
        )(cotangent, conductivity, capacity, sources, jnp.asarray(const))
        return pl.pallas_call(
            write_out,
            out_shape=outs,
            in_specs=[pl.BlockSpec(memory_space=pltpu.VMEM)] * 3,
            out_specs=(pl.BlockSpec(memory_space=pl.ANY),) * 3,
            scratch_shapes=[pltpu.SemaphoreType.DMA((3,))],
        )(*[pltpu.with_memory_space_constraint(item, pltpu.VMEM) for item in results])

    split = P("height", "plane", None)
    return jax.shard_map(
        per_device,
        mesh=mesh,
        in_specs=(split, split, split, P(None, None)),
        out_specs=(split, split, P(None, None)),
        check_vma=False,
    )
```

```python
import functools

import jax
import jax.numpy as jnp
import numpy as np
from jax import lax
from jax.experimental import pallas as pl
from jax.experimental.pallas import tpu as pltpu
from jax.sharding import PartitionSpec as P

MESH = pl.DeviceIdType.MESH
HIGH = lax.Precision.HIGHEST
INV_STEP = 20.0
SHIFT = 0.75
FIELDS = (3, 1, 1, 3, 3)
STARTS = (0, 3, 4, 5, 8)
TOTAL = 11


def gll_tables():
    points = np.array(
        [
            -1.0,
            -0.8717401485096066,
            -0.5917001814331423,
            -0.2092992179024789,
            0.2092992179024789,
            0.5917001814331423,
            0.8717401485096066,
            1.0,
        ]
    )
    weights = np.array(
        [
            1.0 / 28.0,
            0.2107042271435061,
            0.3411226924835044,
            0.4124587946587038,
            0.4124587946587038,
            0.3411226924835044,
            0.2107042271435061,
            1.0 / 28.0,
        ]
    )
    product = np.array(
        [
            np.prod([points[column] - points[others] for others in range(8) if others != column])
            for column in range(8)
        ]
    )
    derivative = np.zeros((8, 8))
    for row_idx in range(8):
        for col_idx in range(8):
            if row_idx != col_idx:
                derivative[row_idx, col_idx] = product[row_idx] / (
                    product[col_idx] * (points[row_idx] - points[col_idx])
                )
        derivative[row_idx, row_idx] = -np.sum(derivative[row_idx])
    return derivative, weights


def tables():
    derivative, weights = gll_tables()
    stiff = derivative.T @ np.diag(weights) @ derivative
    scaled = stiff / weights[:, None]
    eye8, eye2, eye16 = np.eye(8), np.eye(2), np.eye(16)
    rows = np.kron(eye2, np.kron(scaled, eye8) + np.kron(eye8, scaled))
    lanes = np.kron(eye16, scaled.T)
    face = weights[:, None] * np.tile(weights, 16)[None, :]
    slope = np.diag(scaled)
    face_slope = slope[:, None] + np.tile(slope, 16)[None, :]
    const = np.concatenate([rows, lanes, face, face_slope]).astype(np.float32)
    return const, weights, slope


def kernel(
    shape,
    weights,
    slope,
    cot_hbm,
    kap_hbm,
    cap_hbm,
    src_hbm,
    const_hbm,
    second_ref,
    first_ref,
    grad_ref,
    kap_ref,
    cap_ref,
    src_ref,
    const_ref,
    home_ref,
    moved_ref,
    back_ref,
    out_ref,
    y_ref,
    face_ref,
    plane_in,
    height_in,
    work_ref,
    mat_ref,
    row_a,
    row_b,
    tile_a,
    tile_b,
    send_sem,
    recv_sem,
    send_red,
    recv_red,
    send_move,
    recv_move,
    load_sem,
):
    loads = [
        pltpu.make_async_copy(operand, place, load_sem.at[index])
        for index, (operand, place) in enumerate(
            (
                (kap_hbm, kap_ref),
                (cap_hbm, cap_ref),
                (cot_hbm, home_ref.at[pl.ds(0, 16)]),
                (const_hbm, const_ref),
                (src_hbm, src_ref),
            )
        )
    ]
    for load in loads:
        load.start()
    heights, planes, side = shape
    per_run = planes // 2
    depth = heights
    rows_per_run = per_run // side
    high = lax.axis_index("height")
    wide = lax.axis_index("plane")
    run = wide // per_run
    pos = lax.rem(wide, per_run)
    core = lax.rem(high, 2)
    level = 2 * (high // 2) + run
    spot = 2 * level + core

    def host(block_h, block_p):
        half = block_p // per_run
        row = lax.rem(block_p, per_run) // side
        column = lax.rem(block_p, side)
        column = column + lax.rem(row, 2) * (side - 1 - 2 * column)
        row = row + half * (rows_per_run - 1 - 2 * row)
        pair = block_h // 2
        return (2 * pair + half, lax.rem(block_h, 2) * per_run + row * side + column)

    row_here = pos // side
    column_here = lax.rem(pos, side)
    row = row_here + core * (rows_per_run - 1 - 2 * row_here)
    column = column_here + lax.rem(row, 2) * (side - 1 - 2 * column_here)
    h = 2 * (high // 2) + run
    p = core * per_run + row * side + column
    target = host(high, wide)
    source = (h, p)
    moves = jnp.logical_or(h != high, p != wide)

    def layer_peer(step):
        other_row = lax.rem(row_here + step // side, rows_per_run)
        other_column = lax.rem(column_here + step % side, side)
        return (high, run * per_run + other_row * side + other_column)

    def column_peer(step):
        other = lax.rem(level + step // 2, depth)
        other_core = lax.rem(core + step % 2, 2)
        return (2 * (other // 2) + other_core, lax.rem(other, 2) * per_run + pos)

    def far(offset, size):
        return min(offset, size - offset)

    layer_steps = sorted(
        range(1, per_run), key=lambda k: -far(k // side, rows_per_run) - far(k % side, side)
    )
    column_steps = sorted(range(1, 2 * depth), key=lambda k: -far(k // 2, depth) - 0.1 * (k % 2))

    def around(block_h, block_p):
        low_h = lax.rem(block_h + heights - 1, heights)
        high_h = lax.rem(block_h + 1, heights)
        low_p = lax.rem(block_p + planes - 1, planes)
        high_p = lax.rem(block_p + 1, planes)
        return (
            (block_h, low_p),
            (block_h, high_p),
            (low_h, block_p),
            (high_h, block_p),
            (low_h, low_p),
            (low_h, high_p),
            (high_h, low_p),
            (high_h, high_p),
        )

    halo = tuple(host(*block) for block in around(h, p))
    entry_halo = tuple(host(*block) for block in around(high, wide))
    remote = [jnp.logical_or(a != high, b != wide) for a, b in entry_halo]
    barrier = pltpu.get_barrier_semaphore()
    for device in halo + around(h, p) + (source,):
        pl.semaphore_signal(barrier, inc=1, device_id=device, device_id_type=MESH)

    def greet_layer(step, carry):
        pl.semaphore_signal(barrier, inc=1, device_id=layer_peer(step), device_id_type=MESH)
        return carry

    def greet_column(step, carry):
        pl.semaphore_signal(barrier, inc=1, device_id=column_peer(step), device_id_type=MESH)
        return carry

    lax.fori_loop(1, per_run, greet_layer, 0)
    lax.fori_loop(1, 2 * depth, greet_column, 0)

    has_p_lo = jnp.where(p > 0, 1.0, 0.0)
    has_p_hi = jnp.where(p < planes - 1, 1.0, 0.0)
    has_h_lo = jnp.where(h > 0, 1.0, 0.0)
    has_h_hi = jnp.where(h < heights - 1, 1.0, 0.0)

    lane = lax.broadcasted_iota(jnp.int32, (8, 128), 1)
    sub = lax.broadcasted_iota(jnp.int32, (8, 128), 0)
    lane_mod = lax.rem(lane, 8)
    opening = jnp.where((lane_mod == 0) & (lane > 0), 1.0, 0.0)
    ending = jnp.where((lane_mod == 7) & (lane < 127), 1.0, 0.0)
    row_first = jnp.where(sub == 0, 1.0, 0.0)
    row_last = jnp.where(sub == 7, 1.0, 0.0)

    spread = jnp.where(
        lax.broadcasted_iota(jnp.int32, (16, 128), 1) // 8
        == lax.broadcasted_iota(jnp.int32, (16, 128), 0),
        1.0,
        0.0,
    )
    for load in loads[:2]:
        load.wait()
    elems = jnp.concatenate([kap_ref[0], kap_ref[1], cap_ref[0], cap_ref[1]] * 2, axis=0)
    home_ref[16] = jnp.dot(elems, spread, precision=HIGH, preferred_element_type=jnp.float32)
    for load in loads[2:]:
        load.wait()

    def move(index, source_ref, target_ref, device):
        return pltpu.make_async_remote_copy(
            src_ref=source_ref,
            dst_ref=target_ref,
            send_sem=send_move.at[index],
            recv_sem=recv_move.at[index],
            device_id=device,
            device_id_type=MESH,
        )

    bring = move(0, home_ref, moved_ref, target)

    started = []

    def prepare(index, devices):
        slots = pl.ds(STARTS[index], FIELDS[index])
        first_rows = y_ref.at[slots, pl.ds(0, 8)]
        last_rows = y_ref.at[slots, pl.ds(120, 8)]
        routes = (
            (face_ref.at[0, slots], plane_in.at[1, slots]),
            (face_ref.at[1, slots], plane_in.at[0, slots]),
            (first_rows, height_in.at[1, slots]),
            (last_rows, height_in.at[0, slots]),
            (first_rows, height_in.at[5, slots]),
            (first_rows, height_in.at[4, slots]),
            (last_rows, height_in.at[3, slots]),
            (last_rows, height_in.at[2, slots]),
        )
        batch = [
            pltpu.make_async_remote_copy(
                src_ref=source,
                dst_ref=target,
                send_sem=send_sem.at[index, way],
                recv_sem=recv_sem.at[index, way],
                device_id=devices[way],
                device_id_type=MESH,
            )
            for way, (source, target) in enumerate(routes)
        ]
        started.append(batch)
        return batch, routes

    def publish(index, fields):
        batch, _ = prepare(index, halo)
        for offset, values in enumerate(fields):
            y_ref[STARTS[index] + offset] = values.reshape(128, 128)
        for way in (4, 5, 6, 7, 2, 3):
            batch[way].start()
        for offset in range(FIELDS[index]):
            slot = STARTS[index] + offset
            for edge, row in ((0, 0), (1, 7)):
                face_ref[edge, slot] = y_ref.at[slot][pl.ds(row, 16, stride=8), :]
        for way in (0, 1):
            batch[way].start()
        for offset, values in enumerate(fields):
            work_ref[STARTS[index] + offset] = values.reshape(128, 128)

    def arrive(index):
        for copy in started[index]:
            copy.wait_recv()

    def gathered(slot):
        work = work_ref.at[slot]
        work[pl.ds(0, 16, stride=8), :] += has_p_lo * plane_in[0, slot]
        work[pl.ds(7, 16, stride=8), :] += has_p_hi * plane_in[1, slot]
        low = (
            height_in[0, slot]
            + (row_first * has_p_lo) * pltpu.roll(height_in[2, slot], 1, axis=0)
            + (row_last * has_p_hi) * pltpu.roll(height_in[3, slot], 7, axis=0)
        )
        high = (
            height_in[1, slot]
            + (row_first * has_p_lo) * pltpu.roll(height_in[4, slot], 1, axis=0)
            + (row_last * has_p_hi) * pltpu.roll(height_in[5, slot], 7, axis=0)
        )
        work[0:8, :] += has_h_lo * low
        work[120:128, :] += has_h_hi * high
        joined = work[56:64, :] + work[64:72, :]
        work[56:64, :] = joined
        work[64:72, :] = joined
        flat = work[...]
        after = pltpu.roll(flat, 127, axis=1).reshape(16, 8, 128)
        before = pltpu.roll(flat, 1, axis=1).reshape(16, 8, 128)
        return flat.reshape(16, 8, 128) + ending[None] * after + opening[None] * before

    def layered(parts):
        return jnp.stack([weights[a] * parts[e] for e in range(2) for a in range(8)])

    face_w = const_ref[256:264, :]
    slopes = jnp.stack([const_ref[264:272, :] + slope[a] for a in range(8)] * 2)

    def materials(elems):
        mass = layered([face_w * (INV_STEP * elems[2 + e : 3 + e, :]) for e in range(2)])
        conduct = layered([face_w * elems[e : e + 1, :] for e in range(2)])
        return mass, conduct, mass + conduct * slopes

    mass, _, diag_local = materials(home_ref[16])
    home_ref[0:16] = mass * home_ref[0:16]
    for slot, values in enumerate((home_ref[0:16], mass, diag_local)):
        y_ref[slot] = values.reshape(128, 128)
    for slot in range(3):
        for edge, line in ((0, 0), (1, 7)):
            face_ref[edge, slot] = y_ref.at[slot][pl.ds(line, 16, stride=8), :]
    pl.semaphore_wait(barrier, 8 + 8 + 1 + per_run - 1 + 2 * depth - 1)

    batch, routes = prepare(0, entry_halo)

    def launch(way):
        @pl.when(remote[way])
        def _():
            batch[way].start()

        @pl.when(jnp.logical_not(remote[way]))
        def _():
            pltpu.make_async_copy(*routes[way], recv_sem.at[0, way]).start()

    for way in (4, 5, 6, 7):
        launch(way)

    @pl.when(moves)
    def _():
        bring.start()

    for way in (2, 3, 0, 1):
        launch(way)

    @pl.when(moves)
    def _():
        bring.wait_recv()

    @pl.when(jnp.logical_not(moves))
    def _():
        moved_ref[...] = home_ref[...]

    mass, conduct, diag_local = materials(moved_ref[16])
    mat_ref[0] = mass
    mat_ref[1] = conduct
    for slot, values in enumerate((moved_ref[0:16], mass, diag_local)):
        work_ref[slot] = values.reshape(128, 128)

    def stiffness(*fields):
        flats = [values.reshape(128, 128) for values in fields]
        across = jnp.dot(
            const_ref[0:128, :],
            jnp.concatenate(flats, axis=1),
            precision=HIGH,
            preferred_element_type=jnp.float32,
        )
        along = jnp.dot(
            jnp.concatenate(flats, axis=0),
            const_ref[128:256, :],
            precision=HIGH,
            preferred_element_type=jnp.float32,
        )
        return [
            mat_ref[0] * values
            + mat_ref[1]
            * (
                across[:, 128 * k : 128 * k + 128] + along[128 * k : 128 * k + 128]
            ).reshape(16, 8, 128)
            for k, values in enumerate(fields)
        ]

    local = lax.broadcasted_iota(jnp.int32, (128, 128), 0) // 8
    hits = []
    for step in range(2):
        wanted = src_ref[step : step + 1, :]
        hits.append(
            jnp.concatenate(
                [
                    jnp.where(wanted == ((h * 2 + e) * planes + p) * 16 + local, 1.0, 0.0)
                    for e in range(2)
                ],
                axis=0,
            )
        )

    def source_sums(fields, hit):
        rows = []
        for values in fields:
            weighed = mat_ref[0] * values
            rows.append(
                jnp.concatenate(
                    [
                        jnp.sum(weighed[8 * e : 8 * e + 8].reshape(64, 128), axis=0, keepdims=True)
                        for e in range(2)
                    ],
                    axis=1,
                )
            )
        rows = jnp.concatenate(
            rows + [jnp.zeros((8 - len(rows), 256), jnp.float32)], axis=0
        )
        return jnp.dot(rows, hit, precision=HIGH, preferred_element_type=jnp.float32)

    depth_copies = [jnp.ones((1, 1), jnp.float32)] * 16
    depth_copies[0] = jnp.full((1, 1), 1.0 / (1.0 + has_h_lo))
    depth_copies[7] = depth_copies[8] = jnp.full((1, 1), 0.5)
    depth_copies[15] = jnp.full((1, 1), 1.0 / (1.0 + has_h_hi))
    plane_copies = (
        1.0 / ((1.0 + row_first * has_p_lo + row_last * has_p_hi) * (1.0 + opening + ending))
    )

    arrive(0)
    diag = gathered(2)
    inv_diag = 1.0 / diag
    mat_ref[2] = inv_diag
    mat_ref[3] = jnp.stack([diag[i] * plane_copies * depth_copies[i] for i in range(16)])
    mat_ref[4] = gathered(1) * inv_diag

    def dot_rows(left, right):
        return jnp.sum((left * right).reshape(128, 128), axis=0, keepdims=True)

    stages = (
        ((row_b, tile_b), spot, 2 * depth, column_peer, column_steps),
        ((row_a, tile_a), pos, per_run, layer_peer, layer_steps),
    )

    def push(index, stage, tile):
        refs, slot, _, peer, steps = stages[stage]
        own = refs[index].at[slot]
        own[...] = tile
        for step in steps:
            pltpu.make_async_remote_copy(
                src_ref=own,
                dst_ref=own,
                send_sem=send_red.at[index, stage],
                recv_sem=recv_red.at[index, stage],
                device_id=peer(step),
                device_id_type=MESH,
            ).start()

    def rest(index, stage):
        refs, _, count, peer, _ = stages[stage]
        others = refs[index].at[pl.ds(0, count - 1)]
        return pltpu.make_async_remote_copy(
            src_ref=others,
            dst_ref=others,
            send_sem=send_red.at[index, stage],
            recv_sem=recv_red.at[index, stage],
            device_id=peer(1),
            device_id_type=MESH,
        )

    def pull(index, stage):
        rest(index, stage).wait_recv()
        return jnp.sum(stages[stage][0][index][...], axis=0)

    weighted = mat_ref[3]

    zeros = jnp.zeros((1, 128), jnp.float32)

    def moments(first, second, third, applied):
        m = [dot_rows(weighted * first, first), dot_rows(weighted * first, second)]
        m.append(dot_rows(weighted * second, second))
        m.append(dot_rows(weighted * second, third))
        m.append(dot_rows(weighted * third, third))
        m.append(dot_rows(third, applied) - SHIFT * m[4])
        m = jnp.concatenate(m + [zeros, zeros], axis=0)
        for shift in (64, 32, 16):
            m = m + pltpu.roll(m, shift, axis=1)
        return jnp.sum(jnp.where(lane // 16 == sub, m, 0.0), axis=0, keepdims=True)

    def coefficients(tile):
        m = jnp.where(lane // 16 == sub, tile, 0.0)
        m = jnp.broadcast_to(jnp.sum(m, axis=1, keepdims=True), (8, 128))
        m = [m[k : k + 1] for k in range(6)]
        a = [m[k + 1] + SHIFT * m[k] for k in range(5)]
        pivot0 = a[0]
        l1 = a[1] / pivot0
        l2 = a[2] / pivot0
        pivot1 = a[2] - l1 * a[1]
        cross = a[3] - l1 * a[2]
        inv1 = jnp.where(pivot1 > 1e-7 * a[2], 1.0 / pivot1, 0.0)
        l12 = cross * inv1
        pivot2 = a[4] - l2 * a[2] - l12 * cross
        inv2 = jnp.where(pivot2 > 1e-7 * a[4], 1.0 / pivot2, 0.0)
        g1 = m[1] - l1 * m[0]
        g2 = m[2] - l2 * m[0] - l12 * g1
        c2 = g2 * inv2
        c1 = g1 * inv1 - l12 * c2
        c0 = m[0] / pivot0 - l1 * c1 - l2 * c2
        return c0, c1, c2

    def blend(coef, basis):
        return coef[0] * basis[0] + coef[1] * basis[1] + coef[2] * basis[2]

    returns = []

    def keep(index, values):
        out_ref[index] = values
        send_back = move(1 + index, out_ref.at[index], back_ref.at[index], source)

        @pl.when(moves)
        def _():
            send_back.start()

        @pl.when(jnp.logical_not(moves))
        def _():
            back_ref[index] = out_ref[index]

        returns.append(send_back)

    def advance(index, previous):
        arrive(index)
        return [
            gathered(STARTS[index] + k) * mat_ref[2] - SHIFT * values
            for k, values in enumerate(previous)
        ]

    v0 = gathered(0) * inv_diag
    publish(1, stiffness(v0))
    keep(3, mat_ref[4])
    (v1,) = advance(1, (v0,))
    publish(2, stiffness(v1))
    (v2,) = advance(2, (v1,))
    basis = (v0, v1, v2)
    w0 = [values * mat_ref[4] for values in basis]
    publish(3, stiffness(*w0))
    push(0, 0, moments(v0, v1, v2, stiffness(v2)[0]))
    w1 = advance(3, w0)
    publish(4, stiffness(*w1))
    push(0, 1, pull(0, 0))
    w2 = advance(4, w1)
    tile = pull(0, 1)
    coef = coefficients(tile)
    wide_coef = [c[None] for c in coef]
    later = blend(wide_coef, basis)
    basis = [blend(wide_coef, fields) for fields in (w0, w1, w2)]
    sums = source_sums(basis, hits[0])
    later_sums = source_sums((later,), hits[1])
    push(
        1,
        0,
        jnp.concatenate(
            [moments(*basis, stiffness(basis[2])[0]), sums[0:3], later_sums[0:1]], axis=0
        ),
    )
    keep(0, later)
    keep(1, basis[1])
    keep(2, basis[2])
    push(1, 1, pull(1, 0))
    tile = pull(1, 1)
    coef = coefficients(tile[0:1])
    earlier_grad = blend(coef, [tile[1 + k : 2 + k] for k in range(3)])

    @pl.when(moves)
    def _():
        for send_back in returns:
            send_back.wait_recv()

    second_ref[...] = back_ref[0]
    first_ref[...] = blend(
        [c[None] for c in coef], (back_ref[0] * back_ref[3], back_ref[1], back_ref[2])
    )
    scale = 1.0 / (8.0 * INV_STEP)
    grad_ref[0:1, :] = earlier_grad * scale
    grad_ref[1:2, :] = tile[4:5] * scale
    for index in range(2):
        for stage in range(2):
            rest(index, stage).wait_send()
    for way, copy in enumerate(started[0]):
        pl.when(remote[way])(copy.wait_send)
    for batch in started[1:]:
        for copy in batch:
            copy.wait_send()

    @pl.when(moves)
    def _():
        bring.wait_send()
        for send_back in returns:
            send_back.wait_send()


def write_out(*refs):
    sources, targets, sems = refs[:3], refs[3:6], refs[6]
    stores = [
        pltpu.make_async_copy(source, target, sems.at[index])
        for index, (source, target) in enumerate(zip(sources, targets))
    ]
    for store in stores:
        store.start()
    for store in stores:
        store.wait()


def solution(mesh):
    shape = (mesh.shape["height"], mesh.shape["plane"], 4)
    const, weights, slope = tables()
    weights = [float(value) for value in weights]
    slope = [float(value) for value in slope]
    run, stack = shape[1] // 2, shape[0] * 2

    def per_device(cotangent, conductivity, capacity, sources):
        block = jax.ShapeDtypeStruct(cotangent.shape, jnp.float32)
        outs = (block, block, jax.ShapeDtypeStruct(sources.shape, jnp.float32))
        results = pl.pallas_call(
            functools.partial(kernel, shape, weights, slope),
            out_shape=tuple(pltpu.VMEM(item.shape, item.dtype) for item in outs),
            in_specs=[pl.BlockSpec(memory_space=pl.ANY)] * 5,
            out_specs=(pl.BlockSpec(memory_space=pltpu.VMEM),) * 3,
            scratch_shapes=[
                pltpu.VMEM(conductivity.shape, jnp.float32),
                pltpu.VMEM(capacity.shape, jnp.float32),
                pltpu.VMEM(sources.shape, jnp.int32),
                pltpu.VMEM(const.shape, jnp.float32),
                pltpu.VMEM((17, 8, 128), jnp.float32),
                pltpu.VMEM((17, 8, 128), jnp.float32),
                pltpu.VMEM((4, 16, 8, 128), jnp.float32),
                pltpu.VMEM((4, 16, 8, 128), jnp.float32),
                pltpu.VMEM((TOTAL, 128, 128), jnp.float32),
                pltpu.VMEM((2, TOTAL, 16, 128), jnp.float32),
                pltpu.VMEM((2, TOTAL, 16, 128), jnp.float32),
                pltpu.VMEM((6, TOTAL, 8, 128), jnp.float32),
                pltpu.VMEM((TOTAL, 128, 128), jnp.float32),
                pltpu.VMEM((5, 16, 8, 128), jnp.float32),
                pltpu.VMEM((run, 1, 128), jnp.float32),
                pltpu.VMEM((stack, 1, 128), jnp.float32),
                pltpu.VMEM((run, 5, 128), jnp.float32),
                pltpu.VMEM((stack, 5, 128), jnp.float32),
                pltpu.SemaphoreType.DMA((5, 8)),
                pltpu.SemaphoreType.DMA((5, 8)),
                pltpu.SemaphoreType.DMA((2, 2)),
                pltpu.SemaphoreType.DMA((2, 2)),
                pltpu.SemaphoreType.DMA((5,)),
                pltpu.SemaphoreType.DMA((5,)),
                pltpu.SemaphoreType.DMA((5,)),
            ],
            compiler_params=pltpu.CompilerParams(collective_id=0, has_side_effects=True),
        )(cotangent, conductivity, capacity, sources, jnp.asarray(const))
        return pl.pallas_call(
            write_out,
            out_shape=outs,
            in_specs=[pl.BlockSpec(memory_space=pltpu.VMEM)] * 3,
            out_specs=(pl.BlockSpec(memory_space=pl.ANY),) * 3,
            scratch_shapes=[pltpu.SemaphoreType.DMA((3,))],
        )(*[pltpu.with_memory_space_constraint(item, pltpu.VMEM) for item in results])

    split = P("height", "plane", None)
    return jax.shard_map(
        per_device,
        mesh=mesh,
        in_specs=(split, split, split, P(None, None)),
        out_specs=(split, split, P(None, None)),
        check_vma=False,
    )
```

```python
import functools

import jax
import jax.numpy as jnp
import numpy as np
from jax import lax
from jax.experimental import pallas as pl
from jax.experimental.pallas import tpu as pltpu
from jax.sharding import PartitionSpec as P

MESH = pl.DeviceIdType.MESH
HIGH = lax.Precision.HIGHEST
INV_STEP = 20.0
SHIFT = 0.75
FIELDS = (3, 1, 1, 3, 3)
STARTS = (0, 3, 4, 5, 8)
TOTAL = 11


def gll_tables():
    points = np.array(
        [
            -1.0,
            -0.8717401485096066,
            -0.5917001814331423,
            -0.2092992179024789,
            0.2092992179024789,
            0.5917001814331423,
            0.8717401485096066,
            1.0,
        ]
    )
    weights = np.array(
        [
            1.0 / 28.0,
            0.2107042271435061,
            0.3411226924835044,
            0.4124587946587038,
            0.4124587946587038,
            0.3411226924835044,
            0.2107042271435061,
            1.0 / 28.0,
        ]
    )
    product = np.array(
        [
            np.prod([points[column] - points[others] for others in range(8) if others != column])
            for column in range(8)
        ]
    )
    derivative = np.zeros((8, 8))
    for row_idx in range(8):
        for col_idx in range(8):
            if row_idx != col_idx:
                derivative[row_idx, col_idx] = product[row_idx] / (
                    product[col_idx] * (points[row_idx] - points[col_idx])
                )
        derivative[row_idx, row_idx] = -np.sum(derivative[row_idx])
    return derivative, weights


def tables():
    derivative, weights = gll_tables()
    stiff = derivative.T @ np.diag(weights) @ derivative
    scaled = stiff / weights[:, None]
    eye8, eye2, eye16 = np.eye(8), np.eye(2), np.eye(16)
    rows = np.kron(eye2, np.kron(scaled, eye8) + np.kron(eye8, scaled))
    lanes = np.kron(eye16, scaled.T)
    face = weights[:, None] * np.tile(weights, 16)[None, :]
    slope = np.diag(scaled)
    face_slope = slope[:, None] + np.tile(slope, 16)[None, :]
    const = np.concatenate([rows, lanes, face, face_slope]).astype(np.float32)
    return const, weights, slope


def kernel(
    shape,
    weights,
    slope,
    cot_hbm,
    kap_hbm,
    cap_hbm,
    src_hbm,
    const_hbm,
    second_ref,
    first_ref,
    grad_ref,
    kap_ref,
    cap_ref,
    src_ref,
    const_ref,
    cot_ref,
    elems_ref,
    home_ref,
    moved_ref,
    back_ref,
    out_ref,
    y_ref,
    face_ref,
    plane_in,
    height_in,
    work_ref,
    mat_ref,
    row_a,
    row_b,
    tile_a,
    tile_b,
    send_sem,
    recv_sem,
    send_red,
    recv_red,
    send_move,
    recv_move,
    load_sem,
):
    loads = [
        pltpu.make_async_copy(operand, place, load_sem.at[index])
        for index, (operand, place) in enumerate(
            (
                (kap_hbm, kap_ref),
                (cap_hbm, cap_ref),
                (cot_hbm, cot_ref),
                (const_hbm, const_ref),
                (src_hbm, src_ref),
            )
        )
    ]
    for load in loads:
        load.start()
    heights, planes, side = shape
    per_run = planes // 2
    depth = heights
    rows_per_run = per_run // side
    high = lax.axis_index("height")
    wide = lax.axis_index("plane")
    run = wide // per_run
    pos = lax.rem(wide, per_run)
    core = lax.rem(high, 2)
    level = 2 * (high // 2) + run
    spot = 2 * level + core

    def host(block_h, block_p):
        half = block_p // per_run
        row = lax.rem(block_p, per_run) // side
        column = lax.rem(block_p, side)
        column = column + lax.rem(row, 2) * (side - 1 - 2 * column)
        row = row + half * (rows_per_run - 1 - 2 * row)
        pair = block_h // 2
        return (2 * pair + half, lax.rem(block_h, 2) * per_run + row * side + column)

    row_here = pos // side
    column_here = lax.rem(pos, side)
    row = row_here + core * (rows_per_run - 1 - 2 * row_here)
    column = column_here + lax.rem(row, 2) * (side - 1 - 2 * column_here)
    h = 2 * (high // 2) + run
    p = core * per_run + row * side + column
    target = host(high, wide)
    source = (h, p)
    moves = jnp.logical_or(h != high, p != wide)

    def layer_peer(step):
        other_row = lax.rem(row_here + step // side, rows_per_run)
        other_column = lax.rem(column_here + step % side, side)
        return (high, run * per_run + other_row * side + other_column)

    def column_peer(step):
        other = lax.rem(level + step // 2, depth)
        other_core = lax.rem(core + step % 2, 2)
        return (2 * (other // 2) + other_core, lax.rem(other, 2) * per_run + pos)

    def far(offset, size):
        return min(offset, size - offset)

    layer_steps = sorted(
        range(1, per_run), key=lambda k: -far(k // side, rows_per_run) - far(k % side, side)
    )
    column_steps = sorted(range(1, 2 * depth), key=lambda k: -far(k // 2, depth) - 0.1 * (k % 2))

    def around(block_h, block_p):
        low_h = lax.rem(block_h + heights - 1, heights)
        high_h = lax.rem(block_h + 1, heights)
        low_p = lax.rem(block_p + planes - 1, planes)
        high_p = lax.rem(block_p + 1, planes)
        return (
            (block_h, low_p),
            (block_h, high_p),
            (low_h, block_p),
            (high_h, block_p),
            (low_h, low_p),
            (low_h, high_p),
            (high_h, low_p),
            (high_h, high_p),
        )

    halo = tuple(host(*block) for block in around(h, p))
    entry_halo = tuple(host(*block) for block in around(high, wide))
    remote = [jnp.logical_or(a != high, b != wide) for a, b in entry_halo]
    barrier = pltpu.get_barrier_semaphore()
    def greet(devices):
        for device in devices:
            pl.semaphore_signal(barrier, inc=1, device_id=device, device_id_type=MESH)

    greet(around(h, p)[::-1] + (source,))
    greet(column_peer(step) for step in column_steps)
    greet(layer_peer(step) for step in layer_steps)
    greet(halo[::-1])

    has_p_lo = jnp.where(p > 0, 1.0, 0.0)
    has_p_hi = jnp.where(p < planes - 1, 1.0, 0.0)
    has_h_lo = jnp.where(h > 0, 1.0, 0.0)
    has_h_hi = jnp.where(h < heights - 1, 1.0, 0.0)

    lane = lax.broadcasted_iota(jnp.int32, (8, 128), 1)
    sub = lax.broadcasted_iota(jnp.int32, (8, 128), 0)
    lane_mod = lax.rem(lane, 8)
    opening = jnp.where((lane_mod == 0) & (lane > 0), 1.0, 0.0)
    ending = jnp.where((lane_mod == 7) & (lane < 127), 1.0, 0.0)
    row_first = jnp.where(sub == 0, 1.0, 0.0)
    row_last = jnp.where(sub == 7, 1.0, 0.0)

    spread = jnp.where(
        lax.broadcasted_iota(jnp.int32, (16, 128), 1) // 8
        == lax.broadcasted_iota(jnp.int32, (16, 128), 0),
        1.0,
        0.0,
    )
    for load in loads[:2]:
        load.wait()
    elems = jnp.concatenate([kap_ref[0], kap_ref[1], cap_ref[0], cap_ref[1]] * 2, axis=0)
    elems_ref[...] = jnp.dot(elems, spread, precision=HIGH, preferred_element_type=jnp.float32)
    for load in loads[2:]:
        load.wait()

    def move(index, source_ref, target_ref, device):
        return pltpu.make_async_remote_copy(
            src_ref=source_ref,
            dst_ref=target_ref,
            send_sem=send_move.at[index],
            recv_sem=recv_move.at[index],
            device_id=device,
            device_id_type=MESH,
        )

    bring = (
        move(0, elems_ref, moved_ref, target),
        move(5, home_ref, work_ref.at[0], target),
    )

    started = []

    def prepare(index, devices):
        slots = pl.ds(STARTS[index], FIELDS[index])
        first_rows = y_ref.at[slots, pl.ds(0, 8)]
        last_rows = y_ref.at[slots, pl.ds(120, 8)]
        routes = (
            (face_ref.at[0, slots], plane_in.at[1, slots]),
            (face_ref.at[1, slots], plane_in.at[0, slots]),
            (first_rows, height_in.at[1, slots]),
            (last_rows, height_in.at[0, slots]),
            (first_rows, height_in.at[5, slots]),
            (first_rows, height_in.at[4, slots]),
            (last_rows, height_in.at[3, slots]),
            (last_rows, height_in.at[2, slots]),
        )
        batch = [
            pltpu.make_async_remote_copy(
                src_ref=source,
                dst_ref=target,
                send_sem=send_sem.at[index, way],
                recv_sem=recv_sem.at[index, way],
                device_id=devices[way],
                device_id_type=MESH,
            )
            for way, (source, target) in enumerate(routes)
        ]
        started.append(batch)
        return batch, routes

    def publish(index, fields):
        batch, _ = prepare(index, halo)
        for offset, values in enumerate(fields):
            y_ref[STARTS[index] + offset] = values.reshape(128, 128)
        for way in (4, 5, 6, 7, 2, 3):
            batch[way].start()
        for offset in range(FIELDS[index]):
            slot = STARTS[index] + offset
            for edge, row in ((0, 0), (1, 7)):
                face_ref[edge, slot] = y_ref.at[slot][pl.ds(row, 16, stride=8), :]
        for way in (0, 1):
            batch[way].start()
        for offset, values in enumerate(fields):
            work_ref[STARTS[index] + offset] = values.reshape(128, 128)

    from_low = (row_first * (has_p_lo * has_h_lo), row_last * (has_p_hi * has_h_lo))
    from_high = (row_first * (has_p_lo * has_h_hi), row_last * (has_p_hi * has_h_hi))

    def arrive(index):
        for copy in started[index][:4]:
            copy.wait_recv()
        for slot in range(STARTS[index], STARTS[index] + FIELDS[index]):
            work = work_ref.at[slot]
            work[pl.ds(0, 16, stride=8), :] += has_p_lo * plane_in[0, slot]
            work[pl.ds(7, 16, stride=8), :] += has_p_hi * plane_in[1, slot]
            work[0:8, :] += has_h_lo * height_in[0, slot]
            work[120:128, :] += has_h_hi * height_in[1, slot]
        for copy in started[index][4:]:
            copy.wait_recv()

    def gathered(slot):
        work = work_ref.at[slot]
        work[0:8, :] += from_low[0] * pltpu.roll(height_in[2, slot], 1, axis=0) + from_low[
            1
        ] * pltpu.roll(height_in[3, slot], 7, axis=0)
        work[120:128, :] += from_high[0] * pltpu.roll(
            height_in[4, slot], 1, axis=0
        ) + from_high[1] * pltpu.roll(height_in[5, slot], 7, axis=0)
        joined = work[56:64, :] + work[64:72, :]
        work[56:64, :] = joined
        work[64:72, :] = joined
        flat = work[...]
        after = pltpu.roll(flat, 127, axis=1).reshape(16, 8, 128)
        before = pltpu.roll(flat, 1, axis=1).reshape(16, 8, 128)
        return flat.reshape(16, 8, 128) + ending[None] * after + opening[None] * before

    def layered(parts):
        return jnp.stack([weights[a] * parts[e] for e in range(2) for a in range(8)])

    face_w = const_ref[256:264, :]
    slopes = jnp.stack([const_ref[264:272, :] + slope[a] for a in range(8)] * 2)

    def materials(elems):
        mass = layered([face_w * (INV_STEP * elems[2 + e : 3 + e, :]) for e in range(2)])
        conduct = layered([face_w * elems[e : e + 1, :] for e in range(2)])
        return mass, conduct, mass + conduct * slopes

    mass, _, diag_local = materials(elems_ref[...])
    rhs = mass * cot_ref[...]
    home_ref[...] = rhs.reshape(128, 128)
    for slot, values in enumerate((rhs, mass, diag_local)):
        y_ref[slot] = values.reshape(128, 128)
    for slot in range(3):
        for edge, line in ((0, 0), (1, 7)):
            face_ref[edge, slot] = y_ref.at[slot][pl.ds(line, 16, stride=8), :]
    pl.semaphore_wait(barrier, 8 + 8 + 1 + per_run - 1 + 2 * depth - 1)

    batch, routes = prepare(0, entry_halo)

    def launch(way):
        @pl.when(remote[way])
        def _():
            batch[way].start()

        @pl.when(jnp.logical_not(remote[way]))
        def _():
            pltpu.make_async_copy(*routes[way], recv_sem.at[0, way]).start()

    @pl.when(moves)
    def _():
        bring[0].start()

    for way in (4, 5, 6, 7, 2, 3, 0, 1):
        launch(way)

    @pl.when(moves)
    def _():
        bring[1].start()

    @pl.when(moves)
    def _():
        bring[0].wait_recv()

    @pl.when(jnp.logical_not(moves))
    def _():
        moved_ref[...] = elems_ref[...]
        work_ref[0] = home_ref[...]

    mass, conduct, diag_local = materials(moved_ref[...])
    mat_ref[0] = mass
    mat_ref[1] = conduct
    for slot, values in enumerate((mass, diag_local)):
        work_ref[1 + slot] = values.reshape(128, 128)

    @pl.when(moves)
    def _():
        bring[1].wait_recv()

    def stiffness(*fields):
        flats = [values.reshape(128, 128) for values in fields]
        across = jnp.dot(
            const_ref[0:128, :],
            jnp.concatenate(flats, axis=1),
            precision=HIGH,
            preferred_element_type=jnp.float32,
        )
        along = jnp.dot(
            jnp.concatenate(flats, axis=0),
            const_ref[128:256, :],
            precision=HIGH,
            preferred_element_type=jnp.float32,
        )
        return [
            mat_ref[0] * values
            + mat_ref[1]
            * (
                across[:, 128 * k : 128 * k + 128] + along[128 * k : 128 * k + 128]
            ).reshape(16, 8, 128)
            for k, values in enumerate(fields)
        ]

    local = lax.broadcasted_iota(jnp.int32, (128, 128), 0) // 8
    hits = []
    for step in range(2):
        wanted = src_ref[step : step + 1, :]
        hits.append(
            jnp.concatenate(
                [
                    jnp.where(wanted == ((h * 2 + e) * planes + p) * 16 + local, 1.0, 0.0)
                    for e in range(2)
                ],
                axis=0,
            )
        )

    hits = jnp.concatenate(hits, axis=1)

    def source_rows(fields):
        rows = []
        for values in fields:
            weighed = mat_ref[0] * values
            rows.append(
                jnp.concatenate(
                    [
                        jnp.sum(weighed[8 * e : 8 * e + 8].reshape(64, 128), axis=0, keepdims=True)
                        for e in range(2)
                    ],
                    axis=1,
                )
            )
        return rows

    depth_copies = [jnp.ones((1, 1), jnp.float32)] * 16
    depth_copies[0] = jnp.full((1, 1), 1.0 / (1.0 + has_h_lo))
    depth_copies[7] = depth_copies[8] = jnp.full((1, 1), 0.5)
    depth_copies[15] = jnp.full((1, 1), 1.0 / (1.0 + has_h_hi))
    plane_copies = (
        1.0 / ((1.0 + row_first * has_p_lo + row_last * has_p_hi) * (1.0 + opening + ending))
    )

    arrive(0)
    diag = gathered(2)
    inv_diag = 1.0 / diag
    mat_ref[2] = inv_diag

    def dot_rows(left, right):
        return jnp.sum((left * right).reshape(128, 128), axis=0, keepdims=True)

    stages = (
        ((row_b, tile_b), spot, 2 * depth, column_peer, column_steps),
        ((row_a, tile_a), pos, per_run, layer_peer, layer_steps),
    )

    def push(index, stage, tile):
        refs, slot, _, peer, steps = stages[stage]
        own = refs[index].at[slot]
        own[...] = tile
        for step in steps:
            pltpu.make_async_remote_copy(
                src_ref=own,
                dst_ref=own,
                send_sem=send_red.at[index, stage],
                recv_sem=recv_red.at[index, stage],
                device_id=peer(step),
                device_id_type=MESH,
            ).start()

    def rest(index, stage):
        refs, _, count, peer, _ = stages[stage]
        others = refs[index].at[pl.ds(0, count - 1)]
        return pltpu.make_async_remote_copy(
            src_ref=others,
            dst_ref=others,
            send_sem=send_red.at[index, stage],
            recv_sem=recv_red.at[index, stage],
            device_id=peer(1),
            device_id_type=MESH,
        )

    def pull(index, stage):
        rest(index, stage).wait_recv()
        return jnp.sum(stages[stage][0][index][...], axis=0)

    zeros = jnp.zeros((1, 128), jnp.float32)

    def moments(first, second, third, applied):
        m = [dot_rows(weighted * first, first), dot_rows(weighted * first, second)]
        m.append(dot_rows(weighted * second, second))
        m.append(dot_rows(weighted * second, third))
        m.append(dot_rows(weighted * third, third))
        m.append(dot_rows(third, applied) - SHIFT * m[4])
        m = jnp.concatenate(m + [zeros, zeros], axis=0)
        for shift in (64, 32, 16):
            m = m + pltpu.roll(m, shift, axis=1)
        return jnp.sum(jnp.where(lane // 16 == sub, m, 0.0), axis=0, keepdims=True)

    def coefficients(tile):
        m = jnp.where(lane // 16 == sub, tile, 0.0)
        m = jnp.broadcast_to(jnp.sum(m, axis=1, keepdims=True), (8, 128))
        m = [m[k : k + 1] for k in range(6)]
        a = [m[k + 1] + SHIFT * m[k] for k in range(5)]
        pivot0 = a[0]
        l1 = a[1] / pivot0
        l2 = a[2] / pivot0
        pivot1 = a[2] - l1 * a[1]
        cross = a[3] - l1 * a[2]
        inv1 = jnp.where(pivot1 > 1e-7 * a[2], 1.0 / pivot1, 0.0)
        l12 = cross * inv1
        pivot2 = a[4] - l2 * a[2] - l12 * cross
        inv2 = jnp.where(pivot2 > 1e-7 * a[4], 1.0 / pivot2, 0.0)
        g1 = m[1] - l1 * m[0]
        g2 = m[2] - l2 * m[0] - l12 * g1
        c2 = g2 * inv2
        c1 = g1 * inv1 - l12 * c2
        c0 = m[0] / pivot0 - l1 * c1 - l2 * c2
        return c0, c1, c2

    def blend(coef, basis):
        return coef[0] * basis[0] + coef[1] * basis[1] + coef[2] * basis[2]

    returns = []

    def keep(index, values):
        out_ref[index] = values
        send_back = move(1 + index, out_ref.at[index], back_ref.at[index], source)

        @pl.when(moves)
        def _():
            send_back.start()

        @pl.when(jnp.logical_not(moves))
        def _():
            back_ref[index] = out_ref[index]

        returns.append(send_back)

    def advance(index, previous):
        arrive(index)
        return [
            gathered(STARTS[index] + k) * mat_ref[2] - SHIFT * values
            for k, values in enumerate(previous)
        ]

    v0 = gathered(0) * inv_diag
    publish(1, stiffness(v0))
    mat_ref[3] = jnp.stack([diag[i] * plane_copies * depth_copies[i] for i in range(16)])
    weighted = mat_ref[3]
    mat_ref[4] = gathered(1) * inv_diag
    keep(3, mat_ref[4])
    (v1,) = advance(1, (v0,))
    publish(2, stiffness(v1))
    (v2,) = advance(2, (v1,))
    basis = (v0, v1, v2)
    w0 = [values * mat_ref[4] for values in basis]
    publish(3, stiffness(*w0))
    push(0, 0, moments(v0, v1, v2, stiffness(v2)[0]))
    w1 = advance(3, w0)
    publish(4, stiffness(*w1))
    push(0, 1, pull(0, 0))
    rows = source_rows([*basis, *w0, *w1])
    w2 = advance(4, w1)
    applied = stiffness(*w2)
    rows = jnp.concatenate(
        rows + source_rows(w2) + [jnp.zeros((4, 256), jnp.float32)], axis=0
    )
    sums = jnp.dot(rows, hits, precision=HIGH, preferred_element_type=jnp.float32)
    tile = pull(0, 1)
    coef = coefficients(tile)
    wide_coef = [c[None] for c in coef]
    later_sum = blend(coef, [sums[k : k + 1, 128:256] for k in range(3)])
    earlier_sums = [
        blend(coef, [sums[3 * n + k : 3 * n + k + 1, 0:128] for k in range(3)]) for n in (1, 2, 3)
    ]
    later = blend(wide_coef, basis)
    basis = [blend(wide_coef, fields) for fields in (w0, w1, w2)]
    applied = blend(wide_coef, applied)
    push(
        1, 0, jnp.concatenate([moments(*basis, applied)] + earlier_sums + [later_sum], axis=0)
    )
    keep(0, later)
    keep(1, basis[1])
    keep(2, basis[2])
    push(1, 1, pull(1, 0))
    tile = pull(1, 1)
    coef = coefficients(tile[0:1])
    earlier_grad = blend(coef, [tile[1 + k : 2 + k] for k in range(3)])

    @pl.when(moves)
    def _():
        for send_back in returns:
            send_back.wait_recv()

    second_ref[...] = back_ref[0]
    first_ref[...] = blend(
        [c[None] for c in coef], (back_ref[0] * back_ref[3], back_ref[1], back_ref[2])
    )
    scale = 1.0 / (8.0 * INV_STEP)
    grad_ref[0:1, :] = earlier_grad * scale
    grad_ref[1:2, :] = tile[4:5] * scale
    for index in range(2):
        for stage in range(2):
            rest(index, stage).wait_send()
    for way, copy in enumerate(started[0]):
        pl.when(remote[way])(copy.wait_send)
    for batch in started[1:]:
        for copy in batch:
            copy.wait_send()

    @pl.when(moves)
    def _():
        for part in bring:
            part.wait_send()
        for send_back in returns:
            send_back.wait_send()


def write_out(*refs):
    sources, targets, sems = refs[:3], refs[3:6], refs[6]
    stores = [
        pltpu.make_async_copy(source, target, sems.at[index])
        for index, (source, target) in enumerate(zip(sources, targets))
    ]
    for store in stores:
        store.start()
    for store in stores:
        store.wait()


def solution(mesh):
    shape = (mesh.shape["height"], mesh.shape["plane"], 4)
    const, weights, slope = tables()
    weights = [float(value) for value in weights]
    slope = [float(value) for value in slope]
    run, stack = shape[1] // 2, shape[0] * 2

    def per_device(cotangent, conductivity, capacity, sources):
        block = jax.ShapeDtypeStruct(cotangent.shape, jnp.float32)
        outs = (block, block, jax.ShapeDtypeStruct(sources.shape, jnp.float32))
        results = pl.pallas_call(
            functools.partial(kernel, shape, weights, slope),
            out_shape=tuple(pltpu.VMEM(item.shape, item.dtype) for item in outs),
            in_specs=[pl.BlockSpec(memory_space=pl.ANY)] * 5,
            out_specs=(pl.BlockSpec(memory_space=pltpu.VMEM),) * 3,
            scratch_shapes=[
                pltpu.VMEM(conductivity.shape, jnp.float32),
                pltpu.VMEM(capacity.shape, jnp.float32),
                pltpu.VMEM(sources.shape, jnp.int32),
                pltpu.VMEM(const.shape, jnp.float32),
                pltpu.VMEM(cotangent.shape, jnp.float32),
                pltpu.VMEM((8, 128), jnp.float32),
                pltpu.VMEM((128, 128), jnp.float32),
                pltpu.VMEM((8, 128), jnp.float32),
                pltpu.VMEM((4, 16, 8, 128), jnp.float32),
                pltpu.VMEM((4, 16, 8, 128), jnp.float32),
                pltpu.VMEM((TOTAL, 128, 128), jnp.float32),
                pltpu.VMEM((2, TOTAL, 16, 128), jnp.float32),
                pltpu.VMEM((2, TOTAL, 16, 128), jnp.float32),
                pltpu.VMEM((6, TOTAL, 8, 128), jnp.float32),
                pltpu.VMEM((TOTAL, 128, 128), jnp.float32),
                pltpu.VMEM((5, 16, 8, 128), jnp.float32),
                pltpu.VMEM((run, 1, 128), jnp.float32),
                pltpu.VMEM((stack, 1, 128), jnp.float32),
                pltpu.VMEM((run, 5, 128), jnp.float32),
                pltpu.VMEM((stack, 5, 128), jnp.float32),
                pltpu.SemaphoreType.DMA((5, 8)),
                pltpu.SemaphoreType.DMA((5, 8)),
                pltpu.SemaphoreType.DMA((2, 2)),
                pltpu.SemaphoreType.DMA((2, 2)),
                pltpu.SemaphoreType.DMA((6,)),
                pltpu.SemaphoreType.DMA((6,)),
                pltpu.SemaphoreType.DMA((5,)),
            ],
            compiler_params=pltpu.CompilerParams(collective_id=0, has_side_effects=True),
        )(cotangent, conductivity, capacity, sources, jnp.asarray(const))
        return pl.pallas_call(
            write_out,
            out_shape=outs,
            in_specs=[pl.BlockSpec(memory_space=pltpu.VMEM)] * 3,
            out_specs=(pl.BlockSpec(memory_space=pl.ANY),) * 3,
            scratch_shapes=[pltpu.SemaphoreType.DMA((3,))],
        )(*[pltpu.with_memory_space_constraint(item, pltpu.VMEM) for item in results])

    split = P("height", "plane", None)
    return jax.shard_map(
        per_device,
        mesh=mesh,
        in_specs=(split, split, split, P(None, None)),
        out_specs=(split, split, P(None, None)),
        check_vma=False,
    )
```

```python
import functools

import jax
import jax.numpy as jnp
import numpy as np
from jax import lax
from jax.experimental import pallas as pl
from jax.experimental.pallas import tpu as pltpu
from jax.sharding import PartitionSpec as P

MESH = pl.DeviceIdType.MESH
HIGH = lax.Precision.HIGHEST
INV_STEP = 20.0
SHIFT = 0.75
FIELDS = (2, 2, 1, 3, 3)
STARTS = (0, 2, 4, 5, 8)
TOTAL = 11


def gll_tables():
    points = np.array(
        [
            -1.0,
            -0.8717401485096066,
            -0.5917001814331423,
            -0.2092992179024789,
            0.2092992179024789,
            0.5917001814331423,
            0.8717401485096066,
            1.0,
        ]
    )
    weights = np.array(
        [
            1.0 / 28.0,
            0.2107042271435061,
            0.3411226924835044,
            0.4124587946587038,
            0.4124587946587038,
            0.3411226924835044,
            0.2107042271435061,
            1.0 / 28.0,
        ]
    )
    product = np.array(
        [
            np.prod([points[column] - points[others] for others in range(8) if others != column])
            for column in range(8)
        ]
    )
    derivative = np.zeros((8, 8))
    for row_idx in range(8):
        for col_idx in range(8):
            if row_idx != col_idx:
                derivative[row_idx, col_idx] = product[row_idx] / (
                    product[col_idx] * (points[row_idx] - points[col_idx])
                )
        derivative[row_idx, row_idx] = -np.sum(derivative[row_idx])
    return derivative, weights


def tables():
    derivative, weights = gll_tables()
    stiff = derivative.T @ np.diag(weights) @ derivative
    scaled = stiff / weights[:, None]
    eye8, eye2, eye16 = np.eye(8), np.eye(2), np.eye(16)
    rows = np.kron(eye2, np.kron(scaled, eye8) + np.kron(eye8, scaled))
    lanes = np.kron(eye16, scaled.T)
    face = weights[:, None] * np.tile(weights, 16)[None, :]
    slope = np.diag(scaled)
    face_slope = slope[:, None] + np.tile(slope, 16)[None, :]
    const = np.concatenate([rows, lanes, face, face_slope]).astype(np.float32)
    return const, weights, slope


def kernel(
    shape,
    weights,
    slope,
    cot_hbm,
    kap_hbm,
    cap_hbm,
    src_hbm,
    const_hbm,
    second_ref,
    first_ref,
    grad_ref,
    kap_ref,
    cap_ref,
    src_ref,
    const_ref,
    cot_ref,
    elems_ref,
    home_ref,
    moved_ref,
    back_ref,
    out_ref,
    y_ref,
    face_ref,
    plane_in,
    height_in,
    corner_ref,
    corner_in,
    work_ref,
    mat_ref,
    row_a,
    row_b,
    tile_a,
    tile_b,
    send_sem,
    recv_sem,
    send_red,
    recv_red,
    send_move,
    recv_move,
    load_sem,
):
    loads = [
        pltpu.make_async_copy(operand, place, load_sem.at[index])
        for index, (operand, place) in enumerate(
            (
                (kap_hbm, kap_ref),
                (cap_hbm, cap_ref),
                (cot_hbm, cot_ref),
                (const_hbm, const_ref),
                (src_hbm, src_ref),
            )
        )
    ]
    for load in loads:
        load.start()
    heights, planes, side = shape
    per_run = planes // 2
    depth = heights
    rows_per_run = per_run // side
    high = lax.axis_index("height")
    wide = lax.axis_index("plane")
    run = wide // per_run
    pos = lax.rem(wide, per_run)
    core = lax.rem(high, 2)
    level = 2 * (high // 2) + run
    spot = 2 * level + core

    def host(block_h, block_p):
        half = block_p // per_run
        row = lax.rem(block_p, per_run) // side
        column = lax.rem(block_p, side)
        column = column + lax.rem(row, 2) * (side - 1 - 2 * column)
        row = row + half * (rows_per_run - 1 - 2 * row)
        pair = block_h // 2
        return (2 * pair + half, lax.rem(block_h, 2) * per_run + row * side + column)

    row_here = pos // side
    column_here = lax.rem(pos, side)
    row = row_here + core * (rows_per_run - 1 - 2 * row_here)
    column = column_here + lax.rem(row, 2) * (side - 1 - 2 * column_here)
    h = 2 * (high // 2) + run
    p = core * per_run + row * side + column
    target = host(high, wide)
    source = (h, p)
    moves = jnp.logical_or(h != high, p != wide)

    def layer_peer(step):
        other_row = lax.rem(row_here + step // side, rows_per_run)
        other_column = lax.rem(column_here + step % side, side)
        return (high, run * per_run + other_row * side + other_column)

    def column_peer(step):
        other = lax.rem(level + step // 2, depth)
        other_core = lax.rem(core + step % 2, 2)
        return (2 * (other // 2) + other_core, lax.rem(other, 2) * per_run + pos)

    def far(offset, size):
        return min(offset, size - offset)

    layer_steps = sorted(
        range(1, per_run), key=lambda k: -far(k // side, rows_per_run) - far(k % side, side)
    )
    column_steps = sorted(range(1, 2 * depth), key=lambda k: -far(k // 2, depth) - 0.1 * (k % 2))

    def around(block_h, block_p):
        low_h = lax.rem(block_h + heights - 1, heights)
        high_h = lax.rem(block_h + 1, heights)
        low_p = lax.rem(block_p + planes - 1, planes)
        high_p = lax.rem(block_p + 1, planes)
        return (
            (block_h, low_p),
            (block_h, high_p),
            (low_h, block_p),
            (high_h, block_p),
            (low_h, low_p),
            (low_h, high_p),
            (high_h, low_p),
            (high_h, high_p),
        )

    halo = tuple(host(*block) for block in around(h, p))
    entry_halo = tuple(host(*block) for block in around(high, wide))
    remote = [jnp.logical_or(a != high, b != wide) for a, b in entry_halo]
    barrier = pltpu.get_barrier_semaphore()
    def greet(devices):
        for device in devices:
            pl.semaphore_signal(barrier, inc=1, device_id=device, device_id_type=MESH)

    greet(around(h, p)[::-1] + (source,))
    greet(column_peer(step) for step in column_steps)
    greet(layer_peer(step) for step in layer_steps)
    greet(halo[4:])

    has_p_lo = jnp.where(p > 0, 1.0, 0.0)
    has_p_hi = jnp.where(p < planes - 1, 1.0, 0.0)
    has_h_lo = jnp.where(h > 0, 1.0, 0.0)
    has_h_hi = jnp.where(h < heights - 1, 1.0, 0.0)

    lane = lax.broadcasted_iota(jnp.int32, (8, 128), 1)
    sub = lax.broadcasted_iota(jnp.int32, (8, 128), 0)
    lane_mod = lax.rem(lane, 8)
    opening = jnp.where((lane_mod == 0) & (lane > 0), 1.0, 0.0)
    ending = jnp.where((lane_mod == 7) & (lane < 127), 1.0, 0.0)
    row_first = jnp.where(sub == 0, 1.0, 0.0)
    row_last = jnp.where(sub == 7, 1.0, 0.0)

    spread = jnp.where(
        lax.broadcasted_iota(jnp.int32, (16, 128), 1) // 8
        == lax.broadcasted_iota(jnp.int32, (16, 128), 0),
        1.0,
        0.0,
    )
    for load in loads[:2]:
        load.wait()
    elems = jnp.concatenate([kap_ref[0], kap_ref[1], cap_ref[0], cap_ref[1]] * 2, axis=0)
    elems_ref[...] = jnp.dot(elems, spread, precision=HIGH, preferred_element_type=jnp.float32)
    for load in loads[2:]:
        load.wait()

    def move(index, source_ref, target_ref, device):
        return pltpu.make_async_remote_copy(
            src_ref=source_ref,
            dst_ref=target_ref,
            send_sem=send_move.at[index],
            recv_sem=recv_move.at[index],
            device_id=device,
            device_id_type=MESH,
        )

    bring = (
        move(0, elems_ref, moved_ref, target),
        move(5, home_ref, work_ref.at[0], target),
    )

    started = []

    def prepare(index, devices):
        slots = pl.ds(STARTS[index], FIELDS[index])
        first_rows = y_ref.at[slots, pl.ds(0, 8)]
        last_rows = y_ref.at[slots, pl.ds(120, 8)]
        routes = (
            (face_ref.at[0, slots], plane_in.at[1, slots]),
            (face_ref.at[1, slots], plane_in.at[0, slots]),
            (first_rows, height_in.at[1, slots]),
            (last_rows, height_in.at[0, slots]),
            (corner_ref.at[0, slots], corner_in.at[3, slots]),
            (corner_ref.at[1, slots], corner_in.at[2, slots]),
            (corner_ref.at[2, slots], corner_in.at[1, slots]),
            (corner_ref.at[3, slots], corner_in.at[0, slots]),
        )
        batch = [
            pltpu.make_async_remote_copy(
                src_ref=source,
                dst_ref=target,
                send_sem=send_sem.at[index, way],
                recv_sem=recv_sem.at[index, way],
                device_id=devices[way],
                device_id_type=MESH,
            )
            for way, (source, target) in enumerate(routes)
        ]
        started.append(batch)
        return batch, routes

    def cut_corners(slot):
        for corner, line in enumerate((0, 7, 120, 127)):
            corner_ref[corner, slot] = y_ref[slot, line : line + 1]

    def publish(index, fields):
        batch, _ = prepare(index, halo)
        for offset, values in enumerate(fields):
            y_ref[STARTS[index] + offset] = values.reshape(128, 128)
            cut_corners(STARTS[index] + offset)
        for way in (4, 5, 6, 7, 2, 3):
            batch[way].start()
        for offset in range(FIELDS[index]):
            slot = STARTS[index] + offset
            for edge, row in ((0, 0), (1, 7)):
                face_ref[edge, slot] = y_ref.at[slot][pl.ds(row, 16, stride=8), :]
        for way in (0, 1):
            batch[way].start()
        for offset, values in enumerate(fields):
            work_ref[STARTS[index] + offset] = values.reshape(128, 128)
        sent(index - 1)

    def sent(index):
        if index:
            for copy in started[index]:
                copy.wait_send()
            return
        for way, copy in enumerate(started[0]):
            pl.when(remote[way])(copy.wait_send)

        @pl.when(moves)
        def _():
            for part in bring:
                part.wait_send()


    from_low = (row_first * (has_p_lo * has_h_lo), row_last * (has_p_hi * has_h_lo))
    from_high = (row_first * (has_p_lo * has_h_hi), row_last * (has_p_hi * has_h_hi))

    def arrive(index):
        for copy in started[index][:4]:
            copy.wait_recv()
        for slot in range(STARTS[index], STARTS[index] + FIELDS[index]):
            work = work_ref.at[slot]
            work[pl.ds(0, 16, stride=8), :] += has_p_lo * plane_in[0, slot]
            work[pl.ds(7, 16, stride=8), :] += has_p_hi * plane_in[1, slot]
            work[0:8, :] += has_h_lo * height_in[0, slot]
            work[120:128, :] += has_h_hi * height_in[1, slot]
        for copy in started[index][4:]:
            copy.wait_recv()

    def gathered(slot):
        work = work_ref.at[slot]
        work[0:8, :] += from_low[0] * corner_in[0, slot] + from_low[1] * corner_in[1, slot]
        work[120:128, :] += from_high[0] * corner_in[2, slot] + from_high[1] * corner_in[3, slot]
        joined = work[56:64, :] + work[64:72, :]
        work[56:64, :] = joined
        work[64:72, :] = joined
        flat = work[...]
        after = pltpu.roll(flat, 127, axis=1).reshape(16, 8, 128)
        before = pltpu.roll(flat, 1, axis=1).reshape(16, 8, 128)
        return flat.reshape(16, 8, 128) + ending[None] * after + opening[None] * before

    def layered(parts):
        return jnp.stack([weights[a] * parts[e] for e in range(2) for a in range(8)])

    face_w = const_ref[256:264, :]
    slopes = jnp.stack([const_ref[264:272, :] + slope[a] for a in range(8)] * 2)

    def materials(elems):
        mass = layered([face_w * (INV_STEP * elems[2 + e : 3 + e, :]) for e in range(2)])
        conduct = layered([face_w * elems[e : e + 1, :] for e in range(2)])
        return mass, conduct, mass + conduct * slopes

    mass, _, diag_local = materials(elems_ref[...])
    rhs = mass * cot_ref[...]
    home_ref[...] = rhs.reshape(128, 128)
    for slot, values in enumerate((rhs, diag_local)):
        y_ref[slot] = values.reshape(128, 128)
        cut_corners(slot)
    for slot in range(2):
        for edge, line in ((0, 0), (1, 7)):
            face_ref[edge, slot] = y_ref.at[slot][pl.ds(line, 16, stride=8), :]
    pl.semaphore_wait(barrier, 8 + 4 + 1 + per_run - 1 + 2 * depth - 1)

    batch, routes = prepare(0, entry_halo)

    def launch(way):
        @pl.when(remote[way])
        def _():
            batch[way].start()

        @pl.when(jnp.logical_not(remote[way]))
        def _():
            pltpu.make_async_copy(*routes[way], recv_sem.at[0, way]).start()

    @pl.when(moves)
    def _():
        bring[0].start()

    for way in (4, 5, 6, 7, 2, 3, 0, 1):
        launch(way)

    @pl.when(moves)
    def _():
        bring[1].start()

    @pl.when(moves)
    def _():
        bring[0].wait_recv()

    @pl.when(jnp.logical_not(moves))
    def _():
        moved_ref[...] = elems_ref[...]
        work_ref[0] = home_ref[...]

    mass, conduct, diag_local = materials(moved_ref[...])
    mat_ref[0] = mass
    mat_ref[1] = conduct
    work_ref[1] = diag_local.reshape(128, 128)

    @pl.when(moves)
    def _():
        bring[1].wait_recv()

    def stiffness(*fields):
        flats = [values.reshape(128, 128) for values in fields]
        across = jnp.dot(
            const_ref[0:128, :],
            jnp.concatenate(flats, axis=1),
            precision=HIGH,
            preferred_element_type=jnp.float32,
        )
        along = jnp.dot(
            jnp.concatenate(flats, axis=0),
            const_ref[128:256, :],
            precision=HIGH,
            preferred_element_type=jnp.float32,
        )
        return [
            mat_ref[0] * values
            + mat_ref[1]
            * (
                across[:, 128 * k : 128 * k + 128] + along[128 * k : 128 * k + 128]
            ).reshape(16, 8, 128)
            for k, values in enumerate(fields)
        ]

    local = lax.broadcasted_iota(jnp.int32, (128, 128), 0) // 8
    hits = []
    for step in range(2):
        wanted = src_ref[step : step + 1, :]
        hits.append(
            jnp.concatenate(
                [
                    jnp.where(wanted == ((h * 2 + e) * planes + p) * 16 + local, 1.0, 0.0)
                    for e in range(2)
                ],
                axis=0,
            )
        )

    hits = jnp.concatenate(hits, axis=1)

    def source_rows(fields):
        rows = []
        for values in fields:
            weighed = mat_ref[0] * values
            rows.append(
                jnp.concatenate(
                    [
                        jnp.sum(weighed[8 * e : 8 * e + 8].reshape(64, 128), axis=0, keepdims=True)
                        for e in range(2)
                    ],
                    axis=1,
                )
            )
        return rows

    depth_copies = [jnp.ones((1, 1), jnp.float32)] * 16
    depth_copies[0] = jnp.full((1, 1), 1.0 / (1.0 + has_h_lo))
    depth_copies[7] = depth_copies[8] = jnp.full((1, 1), 0.5)
    depth_copies[15] = jnp.full((1, 1), 1.0 / (1.0 + has_h_hi))
    plane_copies = (
        1.0 / ((1.0 + row_first * has_p_lo + row_last * has_p_hi) * (1.0 + opening + ending))
    )

    arrive(0)
    diag = gathered(1)
    inv_diag = 1.0 / diag
    mat_ref[2] = inv_diag

    def dot_rows(left, right):
        return jnp.sum((left * right).reshape(128, 128), axis=0, keepdims=True)

    stages = (
        ((row_b, tile_b), spot, 2 * depth, column_peer, column_steps),
        ((row_a, tile_a), pos, per_run, layer_peer, layer_steps),
    )

    def push(index, stage, tile):
        refs, slot, _, peer, steps = stages[stage]
        own = refs[index].at[slot]
        own[...] = tile
        for step in steps:
            pltpu.make_async_remote_copy(
                src_ref=own,
                dst_ref=own,
                send_sem=send_red.at[index, stage],
                recv_sem=recv_red.at[index, stage],
                device_id=peer(step),
                device_id_type=MESH,
            ).start()

    def rest(index, stage):
        refs, _, count, peer, _ = stages[stage]
        others = refs[index].at[pl.ds(0, count - 1)]
        return pltpu.make_async_remote_copy(
            src_ref=others,
            dst_ref=others,
            send_sem=send_red.at[index, stage],
            recv_sem=recv_red.at[index, stage],
            device_id=peer(1),
            device_id_type=MESH,
        )

    def pull(index, stage):
        rest(index, stage).wait_recv()
        return jnp.sum(stages[stage][0][index][...], axis=0)

    zeros = jnp.zeros((1, 128), jnp.float32)

    def moments(first, second, third, applied):
        m = [dot_rows(weighted * first, first), dot_rows(weighted * first, second)]
        m.append(dot_rows(weighted * second, second))
        m.append(dot_rows(weighted * second, third))
        m.append(dot_rows(weighted * third, third))
        m.append(dot_rows(third, applied) - SHIFT * m[4])
        m = jnp.concatenate(m + [zeros, zeros], axis=0)
        for shift in (64, 32, 16):
            m = m + pltpu.roll(m, shift, axis=1)
        return jnp.sum(jnp.where(lane // 16 == sub, m, 0.0), axis=0, keepdims=True)

    def coefficients(tile):
        m = jnp.where(lane // 16 == sub, tile, 0.0)
        m = jnp.broadcast_to(jnp.sum(m, axis=1, keepdims=True), (8, 128))
        m = [m[k : k + 1] for k in range(6)]
        a = [m[k + 1] + SHIFT * m[k] for k in range(5)]
        pivot0 = a[0]
        l1 = a[1] / pivot0
        l2 = a[2] / pivot0
        pivot1 = a[2] - l1 * a[1]
        cross = a[3] - l1 * a[2]
        inv1 = jnp.where(pivot1 > 1e-7 * a[2], 1.0 / pivot1, 0.0)
        l12 = cross * inv1
        pivot2 = a[4] - l2 * a[2] - l12 * cross
        inv2 = jnp.where(pivot2 > 1e-7 * a[4], 1.0 / pivot2, 0.0)
        g1 = m[1] - l1 * m[0]
        g2 = m[2] - l2 * m[0] - l12 * g1
        c2 = g2 * inv2
        c1 = g1 * inv1 - l12 * c2
        c0 = m[0] / pivot0 - l1 * c1 - l2 * c2
        return c0, c1, c2

    def blend(coef, basis):
        return coef[0] * basis[0] + coef[1] * basis[1] + coef[2] * basis[2]

    returns = []

    def keep(index, values):
        out_ref[index] = values
        send_back = move(1 + index, out_ref.at[index], back_ref.at[index], source)

        @pl.when(moves)
        def _():
            send_back.start()

        @pl.when(jnp.logical_not(moves))
        def _():
            back_ref[index] = out_ref[index]

        returns.append(send_back)

    def advance(index, previous):
        arrive(index)
        return [
            gathered(STARTS[index] + k) * mat_ref[2] - SHIFT * values
            for k, values in enumerate(previous)
        ]

    v0 = gathered(0) * inv_diag
    publish(1, (*stiffness(v0), mat_ref[0]))
    mat_ref[3] = jnp.stack([diag[i] * plane_copies * depth_copies[i] for i in range(16)])
    weighted = mat_ref[3]
    (v1,) = advance(1, (v0,))
    publish(2, stiffness(v1))
    mat_ref[4] = gathered(STARTS[1] + 1) * mat_ref[2]
    keep(3, mat_ref[4])
    (v2,) = advance(2, (v1,))
    basis = (v0, v1, v2)
    w0 = [values * mat_ref[4] for values in basis]
    publish(3, stiffness(*w0))
    push(0, 0, moments(v0, v1, v2, stiffness(v2)[0]))
    w1 = advance(3, w0)
    publish(4, stiffness(*w1))
    push(0, 1, pull(0, 0))
    rows = source_rows([*basis, *w0, *w1])
    w2 = advance(4, w1)
    applied = stiffness(*w2)
    rows = jnp.concatenate(
        rows + source_rows(w2) + [jnp.zeros((4, 256), jnp.float32)], axis=0
    )
    sums = jnp.dot(rows, hits, precision=HIGH, preferred_element_type=jnp.float32)
    tile = pull(0, 1)
    coef = coefficients(tile)
    wide_coef = [c[None] for c in coef]
    later_sum = blend(coef, [sums[k : k + 1, 128:256] for k in range(3)])
    earlier_sums = [
        blend(coef, [sums[3 * n + k : 3 * n + k + 1, 0:128] for k in range(3)]) for n in (1, 2, 3)
    ]
    later = blend(wide_coef, basis)
    basis = [blend(wide_coef, fields) for fields in (w0, w1, w2)]
    applied = blend(wide_coef, applied)
    push(
        1, 0, jnp.concatenate([moments(*basis, applied)] + earlier_sums + [later_sum], axis=0)
    )
    keep(0, later)
    keep(1, basis[1])
    keep(2, basis[2])
    sent(4)
    for stage in range(2):
        rest(0, stage).wait_send()
    push(1, 1, pull(1, 0))

    @pl.when(moves)
    def _():
        for send_back in returns:
            send_back.wait_recv()
            send_back.wait_send()

    second_ref[...] = back_ref[0]
    for stage in range(2):
        rest(1, stage).wait_send()
    tile = pull(1, 1)
    coef = coefficients(tile[0:1])
    earlier_grad = blend(coef, [tile[1 + k : 2 + k] for k in range(3)])

    first_ref[...] = blend(
        [c[None] for c in coef], (back_ref[0] * back_ref[3], back_ref[1], back_ref[2])
    )
    scale = 1.0 / (8.0 * INV_STEP)
    grad_ref[0:1, :] = earlier_grad * scale
    grad_ref[1:2, :] = tile[4:5] * scale


def write_out(*refs):
    sources, targets, sems = refs[:3], refs[3:6], refs[6]
    stores = [
        pltpu.make_async_copy(source, target, sems.at[index])
        for index, (source, target) in enumerate(zip(sources, targets))
    ]
    for store in stores:
        store.start()
    for store in stores:
        store.wait()


def solution(mesh):
    shape = (mesh.shape["height"], mesh.shape["plane"], 4)
    const, weights, slope = tables()
    weights = [float(value) for value in weights]
    slope = [float(value) for value in slope]
    run, stack = shape[1] // 2, shape[0] * 2

    def per_device(cotangent, conductivity, capacity, sources):
        block = jax.ShapeDtypeStruct(cotangent.shape, jnp.float32)
        outs = (block, block, jax.ShapeDtypeStruct(sources.shape, jnp.float32))
        results = pl.pallas_call(
            functools.partial(kernel, shape, weights, slope),
            out_shape=tuple(pltpu.VMEM(item.shape, item.dtype) for item in outs),
            in_specs=[pl.BlockSpec(memory_space=pl.ANY)] * 5,
            out_specs=(pl.BlockSpec(memory_space=pltpu.VMEM),) * 3,
            scratch_shapes=[
                pltpu.VMEM(conductivity.shape, jnp.float32),
                pltpu.VMEM(capacity.shape, jnp.float32),
                pltpu.VMEM(sources.shape, jnp.int32),
                pltpu.VMEM(const.shape, jnp.float32),
                pltpu.VMEM(cotangent.shape, jnp.float32),
                pltpu.VMEM((8, 128), jnp.float32),
                pltpu.VMEM((128, 128), jnp.float32),
                pltpu.VMEM((8, 128), jnp.float32),
                pltpu.VMEM((4, 16, 8, 128), jnp.float32),
                pltpu.VMEM((4, 16, 8, 128), jnp.float32),
                pltpu.VMEM((TOTAL, 128, 128), jnp.float32),
                pltpu.VMEM((2, TOTAL, 16, 128), jnp.float32),
                pltpu.VMEM((2, TOTAL, 16, 128), jnp.float32),
                pltpu.VMEM((2, TOTAL, 8, 128), jnp.float32),
                pltpu.VMEM((4, TOTAL, 1, 128), jnp.float32),
                pltpu.VMEM((4, TOTAL, 1, 128), jnp.float32),
                pltpu.VMEM((TOTAL, 128, 128), jnp.float32),
                pltpu.VMEM((5, 16, 8, 128), jnp.float32),
                pltpu.VMEM((run, 1, 128), jnp.float32),
                pltpu.VMEM((stack, 1, 128), jnp.float32),
                pltpu.VMEM((run, 5, 128), jnp.float32),
                pltpu.VMEM((stack, 5, 128), jnp.float32),
                pltpu.SemaphoreType.DMA((5, 8)),
                pltpu.SemaphoreType.DMA((5, 8)),
                pltpu.SemaphoreType.DMA((2, 2)),
                pltpu.SemaphoreType.DMA((2, 2)),
                pltpu.SemaphoreType.DMA((6,)),
                pltpu.SemaphoreType.DMA((6,)),
                pltpu.SemaphoreType.DMA((5,)),
            ],
            compiler_params=pltpu.CompilerParams(collective_id=0, has_side_effects=True),
        )(cotangent, conductivity, capacity, sources, jnp.asarray(const))
        return pl.pallas_call(
            write_out,
            out_shape=outs,
            in_specs=[pl.BlockSpec(memory_space=pltpu.VMEM)] * 3,
            out_specs=(pl.BlockSpec(memory_space=pl.ANY),) * 3,
            scratch_shapes=[pltpu.SemaphoreType.DMA((3,))],
        )(*[pltpu.with_memory_space_constraint(item, pltpu.VMEM) for item in results])

    split = P("height", "plane", None)
    return jax.shard_map(
        per_device,
        mesh=mesh,
        in_specs=(split, split, split, P(None, None)),
        out_specs=(split, split, P(None, None)),
        check_vma=False,
    )
```

```python
import functools

import jax
import jax.numpy as jnp
import numpy as np
from jax import lax
from jax.experimental import pallas as pl
from jax.experimental.pallas import tpu as pltpu
from jax.sharding import PartitionSpec as P

MESH = pl.DeviceIdType.MESH
HIGH = lax.Precision.HIGHEST
INV_STEP = 20.0
SHIFT = 0.75
FIELDS = (2, 2, 1, 3, 3)
STARTS = (0, 2, 4, 5, 8)
TOTAL = 11


def gll_tables():
    points = np.array(
        [
            -1.0,
            -0.8717401485096066,
            -0.5917001814331423,
            -0.2092992179024789,
            0.2092992179024789,
            0.5917001814331423,
            0.8717401485096066,
            1.0,
        ]
    )
    weights = np.array(
        [
            1.0 / 28.0,
            0.2107042271435061,
            0.3411226924835044,
            0.4124587946587038,
            0.4124587946587038,
            0.3411226924835044,
            0.2107042271435061,
            1.0 / 28.0,
        ]
    )
    product = np.array(
        [
            np.prod([points[column] - points[others] for others in range(8) if others != column])
            for column in range(8)
        ]
    )
    derivative = np.zeros((8, 8))
    for row_idx in range(8):
        for col_idx in range(8):
            if row_idx != col_idx:
                derivative[row_idx, col_idx] = product[row_idx] / (
                    product[col_idx] * (points[row_idx] - points[col_idx])
                )
        derivative[row_idx, row_idx] = -np.sum(derivative[row_idx])
    return derivative, weights


def tables():
    derivative, weights = gll_tables()
    stiff = derivative.T @ np.diag(weights) @ derivative
    scaled = stiff / weights[:, None]
    eye8, eye2, eye16 = np.eye(8), np.eye(2), np.eye(16)
    rows = np.kron(eye2, np.kron(scaled, eye8) + np.kron(eye8, scaled))
    lanes = np.kron(eye16, scaled.T)
    face = weights[:, None] * np.tile(weights, 16)[None, :]
    slope = np.diag(scaled)
    face_slope = slope[:, None] + np.tile(slope, 16)[None, :]
    const = np.concatenate([rows, lanes, face, face_slope]).astype(np.float32)
    return const, weights, slope


def kernel(
    shape,
    weights,
    slope,
    cot_hbm,
    kap_hbm,
    cap_hbm,
    src_hbm,
    const_hbm,
    second_ref,
    first_ref,
    grad_ref,
    kap_ref,
    cap_ref,
    src_ref,
    const_ref,
    cot_ref,
    elems_ref,
    home_ref,
    moved_ref,
    back_ref,
    out_ref,
    y_ref,
    face_ref,
    plane_in,
    height_in,
    corner_ref,
    corner_in,
    work_ref,
    mat_ref,
    row_a,
    row_b,
    tile_a,
    tile_b,
    send_sem,
    recv_sem,
    send_red,
    recv_red,
    send_move,
    recv_move,
    load_sem,
):
    loads = [
        pltpu.make_async_copy(operand, place, load_sem.at[index])
        for index, (operand, place) in enumerate(
            (
                (kap_hbm, kap_ref),
                (cap_hbm, cap_ref),
                (cot_hbm, cot_ref),
                (const_hbm, const_ref),
                (src_hbm, src_ref),
            )
        )
    ]
    for load in loads:
        load.start()
    heights, planes, side = shape
    per_run = planes // 2
    depth = heights
    rows_per_run = per_run // side
    high = lax.axis_index("height")
    wide = lax.axis_index("plane")
    run = wide // per_run
    pos = lax.rem(wide, per_run)
    core = lax.rem(high, 2)
    level = 2 * (high // 2) + run
    spot = 2 * level + core

    def host(block_h, block_p):
        half = block_p // per_run
        row = lax.rem(block_p, per_run) // side
        column = lax.rem(block_p, side)
        column = column + lax.rem(row, 2) * (side - 1 - 2 * column)
        row = row + half * (rows_per_run - 1 - 2 * row)
        pair = block_h // 2
        return (2 * pair + half, lax.rem(block_h, 2) * per_run + row * side + column)

    row_here = pos // side
    column_here = lax.rem(pos, side)
    row = row_here + core * (rows_per_run - 1 - 2 * row_here)
    column = column_here + lax.rem(row, 2) * (side - 1 - 2 * column_here)
    h = 2 * (high // 2) + run
    p = core * per_run + row * side + column
    target = host(high, wide)
    source = (h, p)
    moves = jnp.logical_or(h != high, p != wide)

    def layer_peer(step):
        other_row = lax.rem(row_here + step // side, rows_per_run)
        other_column = lax.rem(column_here + step % side, side)
        return (high, run * per_run + other_row * side + other_column)

    def column_peer(step):
        other = lax.rem(level + step // 2, depth)
        other_core = lax.rem(core + step % 2, 2)
        return (2 * (other // 2) + other_core, lax.rem(other, 2) * per_run + pos)

    def far(offset, size):
        return min(offset, size - offset)

    layer_steps = sorted(
        range(1, per_run), key=lambda k: -far(k // side, rows_per_run) - far(k % side, side)
    )
    column_steps = sorted(range(1, 2 * depth), key=lambda k: -far(k // 2, depth) - 0.1 * (k % 2))

    def around(block_h, block_p):
        low_h = lax.rem(block_h + heights - 1, heights)
        high_h = lax.rem(block_h + 1, heights)
        low_p = lax.rem(block_p + planes - 1, planes)
        high_p = lax.rem(block_p + 1, planes)
        return (
            (block_h, low_p),
            (block_h, high_p),
            (low_h, block_p),
            (high_h, block_p),
            (low_h, low_p),
            (low_h, high_p),
            (high_h, low_p),
            (high_h, high_p),
        )

    halo = tuple(host(*block) for block in around(h, p))
    entry_halo = tuple(host(*block) for block in around(high, wide))
    remote = [jnp.logical_or(a != high, b != wide) for a, b in entry_halo]
    barrier = pltpu.get_barrier_semaphore()
    def greet(devices):
        for device in devices:
            pl.semaphore_signal(barrier, inc=1, device_id=device, device_id_type=MESH)

    greet(column_peer(step) for step in column_steps)
    greet(around(h, p)[::-1] + (source,))
    greet(layer_peer(step) for step in layer_steps)
    greet(halo[4:])

    has_p_lo = jnp.where(p > 0, 1.0, 0.0)
    has_p_hi = jnp.where(p < planes - 1, 1.0, 0.0)
    has_h_lo = jnp.where(h > 0, 1.0, 0.0)
    has_h_hi = jnp.where(h < heights - 1, 1.0, 0.0)

    lane = lax.broadcasted_iota(jnp.int32, (8, 128), 1)
    sub = lax.broadcasted_iota(jnp.int32, (8, 128), 0)
    lane_mod = lax.rem(lane, 8)
    opening = jnp.where((lane_mod == 0) & (lane > 0), 1.0, 0.0)
    ending = jnp.where((lane_mod == 7) & (lane < 127), 1.0, 0.0)
    row_first = jnp.where(sub == 0, 1.0, 0.0)
    row_last = jnp.where(sub == 7, 1.0, 0.0)

    spread = jnp.where(
        lax.broadcasted_iota(jnp.int32, (16, 128), 1) // 8
        == lax.broadcasted_iota(jnp.int32, (16, 128), 0),
        1.0,
        0.0,
    )
    for load in loads[:2]:
        load.wait()
    elems = jnp.concatenate([kap_ref[0], kap_ref[1], cap_ref[0], cap_ref[1]] * 2, axis=0)
    elems_ref[...] = jnp.dot(elems, spread, precision=HIGH, preferred_element_type=jnp.float32)
    for load in loads[2:]:
        load.wait()

    def move(index, source_ref, target_ref, device):
        return pltpu.make_async_remote_copy(
            src_ref=source_ref,
            dst_ref=target_ref,
            send_sem=send_move.at[index],
            recv_sem=recv_move.at[index],
            device_id=device,
            device_id_type=MESH,
        )

    bring = (
        move(0, elems_ref, moved_ref, target),
        move(5, home_ref, work_ref.at[0], target),
    )

    started = []

    def prepare(index, devices):
        slots = pl.ds(STARTS[index], FIELDS[index])
        first_rows = y_ref.at[slots, pl.ds(0, 8)]
        last_rows = y_ref.at[slots, pl.ds(120, 8)]
        routes = (
            (face_ref.at[0, slots], plane_in.at[1, slots]),
            (face_ref.at[1, slots], plane_in.at[0, slots]),
            (first_rows, height_in.at[1, slots]),
            (last_rows, height_in.at[0, slots]),
            (corner_ref.at[0, slots], corner_in.at[3, slots]),
            (corner_ref.at[1, slots], corner_in.at[2, slots]),
            (corner_ref.at[2, slots], corner_in.at[1, slots]),
            (corner_ref.at[3, slots], corner_in.at[0, slots]),
        )
        batch = [
            pltpu.make_async_remote_copy(
                src_ref=source,
                dst_ref=target,
                send_sem=send_sem.at[index, way],
                recv_sem=recv_sem.at[index, way],
                device_id=devices[way],
                device_id_type=MESH,
            )
            for way, (source, target) in enumerate(routes)
        ]
        started.append(batch)
        return batch, routes

    def cut_corners(slot):
        for corner, line in enumerate((0, 7, 120, 127)):
            corner_ref[corner, slot] = y_ref[slot, line : line + 1]

    def publish(index, fields):
        batch, _ = prepare(index, halo)
        for offset, values in enumerate(fields):
            y_ref[STARTS[index] + offset] = values.reshape(128, 128)
            cut_corners(STARTS[index] + offset)
        for way in (4, 5, 6, 7, 2, 3):
            batch[way].start()
        for offset in range(FIELDS[index]):
            slot = STARTS[index] + offset
            for edge, row in ((0, 0), (1, 7)):
                face_ref[edge, slot] = y_ref.at[slot][pl.ds(row, 16, stride=8), :]
        for way in (0, 1):
            batch[way].start()
        for offset, values in enumerate(fields):
            work_ref[STARTS[index] + offset] = values.reshape(128, 128)
        sent(index - 1)

    def sent(index):
        if index:
            for copy in started[index]:
                copy.wait_send()
            return
        for way, copy in enumerate(started[0]):
            pl.when(remote[way])(copy.wait_send)

        @pl.when(moves)
        def _():
            for part in bring:
                part.wait_send()


    from_low = (row_first * (has_p_lo * has_h_lo), row_last * (has_p_hi * has_h_lo))
    from_high = (row_first * (has_p_lo * has_h_hi), row_last * (has_p_hi * has_h_hi))

    def arrive(index):
        for copy in started[index][:4]:
            copy.wait_recv()
        for slot in range(STARTS[index], STARTS[index] + FIELDS[index]):
            work = work_ref.at[slot]
            work[pl.ds(0, 16, stride=8), :] += has_p_lo * plane_in[0, slot]
            work[pl.ds(7, 16, stride=8), :] += has_p_hi * plane_in[1, slot]
            work[0:8, :] += has_h_lo * height_in[0, slot]
            work[120:128, :] += has_h_hi * height_in[1, slot]
        for copy in started[index][4:]:
            copy.wait_recv()

    def gathered(slot):
        work = work_ref.at[slot]
        work[0:8, :] += from_low[0] * corner_in[0, slot] + from_low[1] * corner_in[1, slot]
        work[120:128, :] += from_high[0] * corner_in[2, slot] + from_high[1] * corner_in[3, slot]
        joined = work[56:64, :] + work[64:72, :]
        work[56:64, :] = joined
        work[64:72, :] = joined
        flat = work[...]
        after = pltpu.roll(flat, 127, axis=1).reshape(16, 8, 128)
        before = pltpu.roll(flat, 1, axis=1).reshape(16, 8, 128)
        return flat.reshape(16, 8, 128) + ending[None] * after + opening[None] * before

    def layered(parts):
        return jnp.stack([weights[a] * parts[e] for e in range(2) for a in range(8)])

    face_w = const_ref[256:264, :]
    slopes = jnp.stack([const_ref[264:272, :] + slope[a] for a in range(8)] * 2)

    def materials(elems):
        mass = layered([face_w * (INV_STEP * elems[2 + e : 3 + e, :]) for e in range(2)])
        conduct = layered([face_w * elems[e : e + 1, :] for e in range(2)])
        return mass, conduct, mass + conduct * slopes

    mass, _, diag_local = materials(elems_ref[...])
    rhs = mass * cot_ref[...]
    home_ref[...] = rhs.reshape(128, 128)
    for slot, values in enumerate((rhs, diag_local)):
        y_ref[slot] = values.reshape(128, 128)
        cut_corners(slot)
    for slot in range(2):
        for edge, line in ((0, 0), (1, 7)):
            face_ref[edge, slot] = y_ref.at[slot][pl.ds(line, 16, stride=8), :]
    pl.semaphore_wait(barrier, 8 + 4 + 1 + per_run - 1 + 2 * depth - 1)

    batch, routes = prepare(0, entry_halo)

    def launch(way):
        @pl.when(remote[way])
        def _():
            batch[way].start()

        @pl.when(jnp.logical_not(remote[way]))
        def _():
            pltpu.make_async_copy(*routes[way], recv_sem.at[0, way]).start()

    @pl.when(moves)
    def _():
        bring[0].start()

    for way in (4, 5, 6, 7, 2, 3, 0, 1):
        launch(way)

    @pl.when(moves)
    def _():
        bring[1].start()

    @pl.when(moves)
    def _():
        bring[0].wait_recv()

    @pl.when(jnp.logical_not(moves))
    def _():
        moved_ref[...] = elems_ref[...]
        work_ref[0] = home_ref[...]

    mass, conduct, diag_local = materials(moved_ref[...])
    mat_ref[0] = mass
    mat_ref[1] = conduct
    work_ref[1] = diag_local.reshape(128, 128)

    @pl.when(moves)
    def _():
        bring[1].wait_recv()

    def stiffness(*fields):
        flats = [values.reshape(128, 128) for values in fields]
        across = jnp.dot(
            const_ref[0:128, :],
            jnp.concatenate(flats, axis=1),
            precision=HIGH,
            preferred_element_type=jnp.float32,
        )
        along = jnp.dot(
            jnp.concatenate(flats, axis=0),
            const_ref[128:256, :],
            precision=HIGH,
            preferred_element_type=jnp.float32,
        )
        if len(fields) > 1:
            return [stiffness(values)[0] for values in fields]
        return [
            mat_ref[0] * values
            + mat_ref[1]
            * (
                across[:, 128 * k : 128 * k + 128] + along[128 * k : 128 * k + 128]
            ).reshape(16, 8, 128)
            for k, values in enumerate(fields)
        ]

    local = lax.broadcasted_iota(jnp.int32, (128, 128), 0) // 8
    hits = []
    for step in range(2):
        wanted = src_ref[step : step + 1, :]
        hits.append(
            jnp.concatenate(
                [
                    jnp.where(wanted == ((h * 2 + e) * planes + p) * 16 + local, 1.0, 0.0)
                    for e in range(2)
                ],
                axis=0,
            )
        )

    hits = jnp.concatenate(hits, axis=1)

    def source_rows(fields):
        rows = []
        for values in fields:
            weighed = mat_ref[0] * values
            rows.append(
                jnp.concatenate(
                    [
                        jnp.sum(weighed[8 * e : 8 * e + 8].reshape(64, 128), axis=0, keepdims=True)
                        for e in range(2)
                    ],
                    axis=1,
                )
            )
        return rows

    depth_copies = [jnp.ones((1, 1), jnp.float32)] * 16
    depth_copies[0] = jnp.full((1, 1), 1.0 / (1.0 + has_h_lo))
    depth_copies[7] = depth_copies[8] = jnp.full((1, 1), 0.5)
    depth_copies[15] = jnp.full((1, 1), 1.0 / (1.0 + has_h_hi))
    plane_copies = (
        1.0 / ((1.0 + row_first * has_p_lo + row_last * has_p_hi) * (1.0 + opening + ending))
    )

    arrive(0)
    diag = gathered(1)
    inv_diag = 1.0 / diag
    mat_ref[2] = inv_diag

    def dot_rows(left, right):
        return jnp.sum((left * right).reshape(128, 128), axis=0, keepdims=True)

    stages = (
        ((row_b, tile_b), spot, 2 * depth, column_peer, column_steps),
        ((row_a, tile_a), pos, per_run, layer_peer, layer_steps),
    )

    def push(index, stage, tile):
        refs, slot, _, peer, steps = stages[stage]
        own = refs[index].at[slot]
        own[...] = tile
        for step in steps:
            pltpu.make_async_remote_copy(
                src_ref=own,
                dst_ref=own,
                send_sem=send_red.at[index, stage],
                recv_sem=recv_red.at[index, stage],
                device_id=peer(step),
                device_id_type=MESH,
            ).start()

    def rest(index, stage):
        refs, _, count, peer, _ = stages[stage]
        others = refs[index].at[pl.ds(0, count - 1)]
        return pltpu.make_async_remote_copy(
            src_ref=others,
            dst_ref=others,
            send_sem=send_red.at[index, stage],
            recv_sem=recv_red.at[index, stage],
            device_id=peer(1),
            device_id_type=MESH,
        )

    def pull(index, stage):
        rest(index, stage).wait_recv()
        return jnp.sum(stages[stage][0][index][...], axis=0)

    zeros = jnp.zeros((1, 128), jnp.float32)

    def moments(first, second, third, applied):
        m = [dot_rows(weighted * first, first), dot_rows(weighted * first, second)]
        m.append(dot_rows(weighted * second, second))
        m.append(dot_rows(weighted * second, third))
        m.append(dot_rows(weighted * third, third))
        m.append(dot_rows(third, applied) - SHIFT * m[4])
        m = jnp.concatenate(m + [zeros, zeros], axis=0)
        for shift in (64, 32, 16):
            m = m + pltpu.roll(m, shift, axis=1)
        return jnp.sum(jnp.where(lane // 16 == sub, m, 0.0), axis=0, keepdims=True)

    def coefficients(tile):
        m = jnp.where(lane // 16 == sub, tile, 0.0)
        m = jnp.broadcast_to(jnp.sum(m, axis=1, keepdims=True), (8, 128))
        m = [m[k : k + 1] for k in range(6)]
        a = [m[k + 1] + SHIFT * m[k] for k in range(5)]
        pivot0 = a[0]
        l1 = a[1] / pivot0
        l2 = a[2] / pivot0
        pivot1 = a[2] - l1 * a[1]
        cross = a[3] - l1 * a[2]
        inv1 = jnp.where(pivot1 > 1e-7 * a[2], 1.0 / pivot1, 0.0)
        l12 = cross * inv1
        pivot2 = a[4] - l2 * a[2] - l12 * cross
        inv2 = jnp.where(pivot2 > 1e-7 * a[4], 1.0 / pivot2, 0.0)
        g1 = m[1] - l1 * m[0]
        g2 = m[2] - l2 * m[0] - l12 * g1
        c2 = g2 * inv2
        c1 = g1 * inv1 - l12 * c2
        c0 = m[0] / pivot0 - l1 * c1 - l2 * c2
        return c0, c1, c2

    def blend(coef, basis):
        return coef[0] * basis[0] + coef[1] * basis[1] + coef[2] * basis[2]

    returns = []

    def keep(index, values):
        out_ref[index] = values
        send_back = move(1 + index, out_ref.at[index], back_ref.at[index], source)

        @pl.when(moves)
        def _():
            send_back.start()

        @pl.when(jnp.logical_not(moves))
        def _():
            back_ref[index] = out_ref[index]

        returns.append(send_back)

    def advance(index, previous):
        arrive(index)
        return [
            gathered(STARTS[index] + k) * mat_ref[2] - SHIFT * values
            for k, values in enumerate(previous)
        ]

    v0 = gathered(0) * inv_diag
    publish(1, (*stiffness(v0), mat_ref[0]))
    mat_ref[3] = jnp.stack([diag[i] * plane_copies * depth_copies[i] for i in range(16)])
    weighted = mat_ref[3]
    (v1,) = advance(1, (v0,))
    publish(2, stiffness(v1))
    mat_ref[4] = gathered(STARTS[1] + 1) * mat_ref[2]
    (v2,) = advance(2, (v1,))
    basis = (v0, v1, v2)
    w0 = [values * mat_ref[4] for values in basis]
    publish(3, stiffness(*w0))
    push(0, 0, moments(v0, v1, v2, stiffness(v2)[0]))
    w1 = advance(3, w0)
    publish(4, stiffness(*w1))
    push(0, 1, pull(0, 0))
    keep(3, mat_ref[4])
    rows = source_rows([*basis, *w0, *w1])
    w2 = advance(4, w1)
    applied = stiffness(*w2)
    rows = jnp.concatenate(
        rows + source_rows(w2) + [jnp.zeros((4, 256), jnp.float32)], axis=0
    )
    sums = jnp.dot(rows, hits, precision=HIGH, preferred_element_type=jnp.float32)
    tile = pull(0, 1)
    coef = coefficients(tile)
    wide_coef = [c[None] for c in coef]
    later_sum = blend(coef, [sums[k : k + 1, 128:256] for k in range(3)])
    earlier_sums = [
        blend(coef, [sums[3 * n + k : 3 * n + k + 1, 0:128] for k in range(3)]) for n in (1, 2, 3)
    ]
    later = blend(wide_coef, basis)
    basis = [blend(wide_coef, fields) for fields in (w0, w1, w2)]
    applied = blend(wide_coef, applied)
    push(
        1, 0, jnp.concatenate([moments(*basis, applied)] + earlier_sums + [later_sum], axis=0)
    )
    keep(0, later)
    keep(1, basis[1])
    keep(2, basis[2])
    sent(4)
    for stage in range(2):
        rest(0, stage).wait_send()
    push(1, 1, pull(1, 0))

    @pl.when(moves)
    def _():
        for send_back in returns:
            send_back.wait_recv()
            send_back.wait_send()

    second_ref[...] = back_ref[0]
    for stage in range(2):
        rest(1, stage).wait_send()
    tile = pull(1, 1)
    coef = coefficients(tile[0:1])
    earlier_grad = blend(coef, [tile[1 + k : 2 + k] for k in range(3)])

    first_ref[...] = blend(
        [c[None] for c in coef], (back_ref[0] * back_ref[3], back_ref[1], back_ref[2])
    )
    scale = 1.0 / (8.0 * INV_STEP)
    grad_ref[0:1, :] = earlier_grad * scale
    grad_ref[1:2, :] = tile[4:5] * scale


def write_out(*refs):
    sources, targets, sems = refs[:3], refs[3:6], refs[6]
    stores = [
        pltpu.make_async_copy(source, target, sems.at[index])
        for index, (source, target) in enumerate(zip(sources, targets))
    ]
    for store in stores:
        store.start()
    for store in stores:
        store.wait()


def solution(mesh):
    shape = (mesh.shape["height"], mesh.shape["plane"], 4)
    const, weights, slope = tables()
    weights = [float(value) for value in weights]
    slope = [float(value) for value in slope]
    run, stack = shape[1] // 2, shape[0] * 2

    def per_device(cotangent, conductivity, capacity, sources):
        block = jax.ShapeDtypeStruct(cotangent.shape, jnp.float32)
        outs = (block, block, jax.ShapeDtypeStruct(sources.shape, jnp.float32))
        results = pl.pallas_call(
            functools.partial(kernel, shape, weights, slope),
            out_shape=tuple(pltpu.VMEM(item.shape, item.dtype) for item in outs),
            in_specs=[pl.BlockSpec(memory_space=pl.ANY)] * 5,
            out_specs=(pl.BlockSpec(memory_space=pltpu.VMEM),) * 3,
            scratch_shapes=[
                pltpu.VMEM(conductivity.shape, jnp.float32),
                pltpu.VMEM(capacity.shape, jnp.float32),
                pltpu.VMEM(sources.shape, jnp.int32),
                pltpu.VMEM(const.shape, jnp.float32),
                pltpu.VMEM(cotangent.shape, jnp.float32),
                pltpu.VMEM((8, 128), jnp.float32),
                pltpu.VMEM((128, 128), jnp.float32),
                pltpu.VMEM((8, 128), jnp.float32),
                pltpu.VMEM((4, 16, 8, 128), jnp.float32),
                pltpu.VMEM((4, 16, 8, 128), jnp.float32),
                pltpu.VMEM((TOTAL, 128, 128), jnp.float32),
                pltpu.VMEM((2, TOTAL, 16, 128), jnp.float32),
                pltpu.VMEM((2, TOTAL, 16, 128), jnp.float32),
                pltpu.VMEM((2, TOTAL, 8, 128), jnp.float32),
                pltpu.VMEM((4, TOTAL, 1, 128), jnp.float32),
                pltpu.VMEM((4, TOTAL, 1, 128), jnp.float32),
                pltpu.VMEM((TOTAL, 128, 128), jnp.float32),
                pltpu.VMEM((5, 16, 8, 128), jnp.float32),
                pltpu.VMEM((run, 1, 128), jnp.float32),
                pltpu.VMEM((stack, 1, 128), jnp.float32),
                pltpu.VMEM((run, 5, 128), jnp.float32),
                pltpu.VMEM((stack, 5, 128), jnp.float32),
                pltpu.SemaphoreType.DMA((5, 8)),
                pltpu.SemaphoreType.DMA((5, 8)),
                pltpu.SemaphoreType.DMA((2, 2)),
                pltpu.SemaphoreType.DMA((2, 2)),
                pltpu.SemaphoreType.DMA((6,)),
                pltpu.SemaphoreType.DMA((6,)),
                pltpu.SemaphoreType.DMA((5,)),
            ],
            compiler_params=pltpu.CompilerParams(collective_id=0, has_side_effects=True),
        )(cotangent, conductivity, capacity, sources, jnp.asarray(const))
        return pl.pallas_call(
            write_out,
            out_shape=outs,
            in_specs=[pl.BlockSpec(memory_space=pltpu.VMEM)] * 3,
            out_specs=(pl.BlockSpec(memory_space=pl.ANY),) * 3,
            scratch_shapes=[pltpu.SemaphoreType.DMA((3,))],
        )(*[pltpu.with_memory_space_constraint(item, pltpu.VMEM) for item in results])

    split = P("height", "plane", None)
    return jax.shard_map(
        per_device,
        mesh=mesh,
        in_specs=(split, split, split, P(None, None)),
        out_specs=(split, split, P(None, None)),
        check_vma=False,
    )
```

```python
import functools

import jax
import jax.numpy as jnp
import numpy as np
from jax import lax
from jax.experimental import pallas as pl
from jax.experimental.pallas import tpu as pltpu
from jax.sharding import PartitionSpec as P

MESH = pl.DeviceIdType.MESH
HIGH = lax.Precision.HIGHEST
INV_STEP = 20.0
SHIFT = 0.75
FIELDS = (2, 1, 1, 3, 3, 1)
STARTS = (0, 2, 3, 4, 7, 10)
TOTAL = 11


def gll_tables():
    points = np.array(
        [
            -1.0,
            -0.8717401485096066,
            -0.5917001814331423,
            -0.2092992179024789,
            0.2092992179024789,
            0.5917001814331423,
            0.8717401485096066,
            1.0,
        ]
    )
    weights = np.array(
        [
            1.0 / 28.0,
            0.2107042271435061,
            0.3411226924835044,
            0.4124587946587038,
            0.4124587946587038,
            0.3411226924835044,
            0.2107042271435061,
            1.0 / 28.0,
        ]
    )
    product = np.array(
        [
            np.prod([points[column] - points[others] for others in range(8) if others != column])
            for column in range(8)
        ]
    )
    derivative = np.zeros((8, 8))
    for row_idx in range(8):
        for col_idx in range(8):
            if row_idx != col_idx:
                derivative[row_idx, col_idx] = product[row_idx] / (
                    product[col_idx] * (points[row_idx] - points[col_idx])
                )
        derivative[row_idx, row_idx] = -np.sum(derivative[row_idx])
    return derivative, weights


def tables():
    derivative, weights = gll_tables()
    stiff = derivative.T @ np.diag(weights) @ derivative
    scaled = stiff / weights[:, None]
    eye8, eye2, eye16 = np.eye(8), np.eye(2), np.eye(16)
    rows = np.kron(eye2, np.kron(scaled, eye8) + np.kron(eye8, scaled))
    lanes = np.kron(eye16, scaled.T)
    face = weights[:, None] * np.tile(weights, 16)[None, :]
    slope = np.diag(scaled)
    face_slope = slope[:, None] + np.tile(slope, 16)[None, :]
    const = np.concatenate([rows, lanes, face, face_slope]).astype(np.float32)
    return const, weights, slope


def kernel(
    shape,
    weights,
    slope,
    cot_hbm,
    kap_hbm,
    cap_hbm,
    src_hbm,
    const_hbm,
    second_ref,
    first_ref,
    grad_ref,
    kap_ref,
    cap_ref,
    src_ref,
    const_ref,
    cot_ref,
    elems_ref,
    home_ref,
    moved_ref,
    back_ref,
    out_ref,
    y_ref,
    face_ref,
    plane_in,
    height_in,
    corner_ref,
    corner_in,
    work_ref,
    mat_ref,
    row_a,
    row_b,
    tile_a,
    tile_b,
    send_sem,
    recv_sem,
    send_red,
    recv_red,
    send_move,
    recv_move,
    load_sem,
):
    loads = [
        pltpu.make_async_copy(operand, place, load_sem.at[index])
        for index, (operand, place) in enumerate(
            (
                (kap_hbm, kap_ref),
                (cap_hbm, cap_ref),
                (cot_hbm, cot_ref),
                (const_hbm, const_ref),
                (src_hbm, src_ref),
            )
        )
    ]
    for load in loads:
        load.start()
    heights, planes, side = shape
    per_run = planes // 2
    depth = heights
    rows_per_run = per_run // side
    high = lax.axis_index("height")
    wide = lax.axis_index("plane")
    run = wide // per_run
    pos = lax.rem(wide, per_run)
    core = lax.rem(high, 2)
    level = 2 * (high // 2) + run
    spot = 2 * level + core

    def host(block_h, block_p):
        half = block_p // per_run
        row = lax.rem(block_p, per_run) // side
        column = lax.rem(block_p, side)
        column = column + lax.rem(row, 2) * (side - 1 - 2 * column)
        row = row + half * (rows_per_run - 1 - 2 * row)
        pair = block_h // 2
        return (2 * pair + half, lax.rem(block_h, 2) * per_run + row * side + column)

    row_here = pos // side
    column_here = lax.rem(pos, side)
    row = row_here + core * (rows_per_run - 1 - 2 * row_here)
    column = column_here + lax.rem(row, 2) * (side - 1 - 2 * column_here)
    h = 2 * (high // 2) + run
    p = core * per_run + row * side + column
    target = host(high, wide)
    source = (h, p)
    moves = jnp.logical_or(h != high, p != wide)

    def layer_peer(step):
        other_row = lax.rem(row_here + step // side, rows_per_run)
        other_column = lax.rem(column_here + step % side, side)
        return (high, run * per_run + other_row * side + other_column)

    def column_peer(step):
        other = lax.rem(level + step // 2, depth)
        other_core = lax.rem(core + step % 2, 2)
        return (2 * (other // 2) + other_core, lax.rem(other, 2) * per_run + pos)

    def far(offset, size):
        return min(offset, size - offset)

    layer_steps = sorted(
        range(1, per_run), key=lambda k: -far(k // side, rows_per_run) - far(k % side, side)
    )
    column_steps = sorted(range(1, 2 * depth), key=lambda k: -far(k // 2, depth) - 0.1 * (k % 2))

    def around(block_h, block_p):
        low_h = lax.rem(block_h + heights - 1, heights)
        high_h = lax.rem(block_h + 1, heights)
        low_p = lax.rem(block_p + planes - 1, planes)
        high_p = lax.rem(block_p + 1, planes)
        return (
            (block_h, low_p),
            (block_h, high_p),
            (low_h, block_p),
            (high_h, block_p),
            (low_h, low_p),
            (low_h, high_p),
            (high_h, low_p),
            (high_h, high_p),
        )

    halo = tuple(host(*block) for block in around(h, p))
    entry_halo = tuple(host(*block) for block in around(high, wide))
    remote = [jnp.logical_or(a != high, b != wide) for a, b in entry_halo]
    barrier = pltpu.get_barrier_semaphore()
    def greet(devices):
        for device in devices:
            pl.semaphore_signal(barrier, inc=1, device_id=device, device_id_type=MESH)

    greet(around(h, p)[::-1] + (source,))
    greet(column_peer(step) for step in column_steps)
    greet(layer_peer(step) for step in layer_steps)
    greet(halo[4:])

    has_p_lo = jnp.where(p > 0, 1.0, 0.0)
    has_p_hi = jnp.where(p < planes - 1, 1.0, 0.0)
    has_h_lo = jnp.where(h > 0, 1.0, 0.0)
    has_h_hi = jnp.where(h < heights - 1, 1.0, 0.0)

    lane = lax.broadcasted_iota(jnp.int32, (8, 128), 1)
    sub = lax.broadcasted_iota(jnp.int32, (8, 128), 0)
    lane_mod = lax.rem(lane, 8)
    opening = jnp.where((lane_mod == 0) & (lane > 0), 1.0, 0.0)
    ending = jnp.where((lane_mod == 7) & (lane < 127), 1.0, 0.0)
    row_first = jnp.where(sub == 0, 1.0, 0.0)
    row_last = jnp.where(sub == 7, 1.0, 0.0)

    spread = jnp.where(
        lax.broadcasted_iota(jnp.int32, (16, 128), 1) // 8
        == lax.broadcasted_iota(jnp.int32, (16, 128), 0),
        1.0,
        0.0,
    )
    for load in loads[:2]:
        load.wait()
    elems = jnp.concatenate([kap_ref[0], kap_ref[1], cap_ref[0], cap_ref[1]] * 2, axis=0)
    elems_ref[...] = jnp.dot(elems, spread, precision=HIGH, preferred_element_type=jnp.float32)
    for load in loads[2:]:
        load.wait()

    def move(index, source_ref, target_ref, device):
        return pltpu.make_async_remote_copy(
            src_ref=source_ref,
            dst_ref=target_ref,
            send_sem=send_move.at[index],
            recv_sem=recv_move.at[index],
            device_id=device,
            device_id_type=MESH,
        )

    bring = (
        move(0, elems_ref, moved_ref, target),
        move(5, home_ref, work_ref.at[0], target),
    )

    started = {}

    def prepare(index, devices):
        slots = pl.ds(STARTS[index], FIELDS[index])
        first_rows = y_ref.at[slots, pl.ds(0, 8)]
        last_rows = y_ref.at[slots, pl.ds(120, 8)]
        routes = (
            (face_ref.at[0, slots], plane_in.at[1, slots]),
            (face_ref.at[1, slots], plane_in.at[0, slots]),
            (first_rows, height_in.at[1, slots]),
            (last_rows, height_in.at[0, slots]),
            (corner_ref.at[0, slots], corner_in.at[3, slots]),
            (corner_ref.at[1, slots], corner_in.at[2, slots]),
            (corner_ref.at[2, slots], corner_in.at[1, slots]),
            (corner_ref.at[3, slots], corner_in.at[0, slots]),
        )
        batch = [
            pltpu.make_async_remote_copy(
                src_ref=source,
                dst_ref=target,
                send_sem=send_sem.at[index, way],
                recv_sem=recv_sem.at[index, way],
                device_id=devices[way],
                device_id_type=MESH,
            )
            for way, (source, target) in enumerate(routes)
        ]
        started[index] = batch
        return batch, routes

    def cut_corners(slot):
        for corner, line in enumerate((0, 7, 120, 127)):
            corner_ref[corner, slot] = y_ref[slot, line : line + 1]

    def publish(index, fields):
        batch, _ = prepare(index, halo)
        for offset, values in enumerate(fields):
            y_ref[STARTS[index] + offset] = values.reshape(128, 128)
            cut_corners(STARTS[index] + offset)
        for way in (4, 5, 6, 7, 2, 3):
            batch[way].start()
        for offset in range(FIELDS[index]):
            slot = STARTS[index] + offset
            for edge, row in ((0, 0), (1, 7)):
                face_ref[edge, slot] = y_ref.at[slot][pl.ds(row, 16, stride=8), :]
        for way in (0, 1):
            batch[way].start()
        for offset, values in enumerate(fields):
            work_ref[STARTS[index] + offset] = values.reshape(128, 128)
        if index < 5:
            sent(index - 1)

    def sent(index):
        if index:
            for copy in started[index]:
                copy.wait_send()
            return
        for way, copy in enumerate(started[0]):
            pl.when(remote[way])(copy.wait_send)

        @pl.when(moves)
        def _():
            for part in bring:
                part.wait_send()


    from_low = (row_first * (has_p_lo * has_h_lo), row_last * (has_p_hi * has_h_lo))
    from_high = (row_first * (has_p_lo * has_h_hi), row_last * (has_p_hi * has_h_hi))

    def arrive(index):
        for copy in started[index][:4]:
            copy.wait_recv()
        for slot in range(STARTS[index], STARTS[index] + FIELDS[index]):
            work = work_ref.at[slot]
            work[pl.ds(0, 16, stride=8), :] += has_p_lo * plane_in[0, slot]
            work[pl.ds(7, 16, stride=8), :] += has_p_hi * plane_in[1, slot]
            work[0:8, :] += has_h_lo * height_in[0, slot]
            work[120:128, :] += has_h_hi * height_in[1, slot]
        for copy in started[index][4:]:
            copy.wait_recv()

    def gathered(slot):
        work = work_ref.at[slot]
        work[0:8, :] += from_low[0] * corner_in[0, slot] + from_low[1] * corner_in[1, slot]
        work[120:128, :] += from_high[0] * corner_in[2, slot] + from_high[1] * corner_in[3, slot]
        joined = work[56:64, :] + work[64:72, :]
        work[56:64, :] = joined
        work[64:72, :] = joined
        flat = work[...]
        after = pltpu.roll(flat, 127, axis=1).reshape(16, 8, 128)
        before = pltpu.roll(flat, 1, axis=1).reshape(16, 8, 128)
        return flat.reshape(16, 8, 128) + ending[None] * after + opening[None] * before

    def layered(parts):
        return jnp.stack([weights[a] * parts[e] for e in range(2) for a in range(8)])

    face_w = const_ref[256:264, :]
    slopes = jnp.stack([const_ref[264:272, :] + slope[a] for a in range(8)] * 2)

    def materials(elems):
        mass = layered([face_w * (INV_STEP * elems[2 + e : 3 + e, :]) for e in range(2)])
        conduct = layered([face_w * elems[e : e + 1, :] for e in range(2)])
        return mass, conduct, mass + conduct * slopes

    mass, _, diag_local = materials(elems_ref[...])
    rhs = mass * cot_ref[...]
    home_ref[...] = rhs.reshape(128, 128)
    for slot, values in enumerate((rhs, diag_local)):
        y_ref[slot] = values.reshape(128, 128)
        cut_corners(slot)
    for slot in range(2):
        for edge, line in ((0, 0), (1, 7)):
            face_ref[edge, slot] = y_ref.at[slot][pl.ds(line, 16, stride=8), :]
    pl.semaphore_wait(barrier, 8 + 4 + 1 + per_run - 1 + 2 * depth - 1)

    batch, routes = prepare(0, entry_halo)

    def launch(way):
        @pl.when(remote[way])
        def _():
            batch[way].start()

        @pl.when(jnp.logical_not(remote[way]))
        def _():
            pltpu.make_async_copy(*routes[way], recv_sem.at[0, way]).start()

    @pl.when(moves)
    def _():
        bring[0].start()

    for way in (4, 5, 6, 7, 2, 3, 0, 1):
        launch(way)

    @pl.when(moves)
    def _():
        bring[1].start()

    @pl.when(moves)
    def _():
        bring[0].wait_recv()

    @pl.when(jnp.logical_not(moves))
    def _():
        moved_ref[...] = elems_ref[...]
        work_ref[0] = home_ref[...]

    mass, conduct, diag_local = materials(moved_ref[...])
    mat_ref[0] = mass
    mat_ref[1] = conduct
    work_ref[1] = diag_local.reshape(128, 128)

    @pl.when(moves)
    def _():
        bring[1].wait_recv()

    def stiffness(*fields):
        flats = [values.reshape(128, 128) for values in fields]
        across = jnp.dot(
            const_ref[0:128, :],
            jnp.concatenate(flats, axis=1),
            precision=HIGH,
            preferred_element_type=jnp.float32,
        )
        along = jnp.dot(
            jnp.concatenate(flats, axis=0),
            const_ref[128:256, :],
            precision=HIGH,
            preferred_element_type=jnp.float32,
        )
        return [
            mat_ref[0] * values
            + mat_ref[1]
            * (
                across[:, 128 * k : 128 * k + 128] + along[128 * k : 128 * k + 128]
            ).reshape(16, 8, 128)
            for k, values in enumerate(fields)
        ]

    local = lax.broadcasted_iota(jnp.int32, (128, 128), 0) // 8
    hits = []
    for step in range(2):
        wanted = src_ref[step : step + 1, :]
        hits.append(
            jnp.concatenate(
                [
                    jnp.where(wanted == ((h * 2 + e) * planes + p) * 16 + local, 1.0, 0.0)
                    for e in range(2)
                ],
                axis=0,
            )
        )

    hits = jnp.concatenate(hits, axis=1)

    def source_rows(fields):
        rows = []
        for values in fields:
            weighed = mat_ref[0] * values
            rows.append(
                jnp.concatenate(
                    [
                        jnp.sum(weighed[8 * e : 8 * e + 8].reshape(64, 128), axis=0, keepdims=True)
                        for e in range(2)
                    ],
                    axis=1,
                )
            )
        return rows

    depth_copies = [jnp.ones((1, 1), jnp.float32)] * 16
    depth_copies[0] = jnp.full((1, 1), 1.0 / (1.0 + has_h_lo))
    depth_copies[7] = depth_copies[8] = jnp.full((1, 1), 0.5)
    depth_copies[15] = jnp.full((1, 1), 1.0 / (1.0 + has_h_hi))
    plane_copies = (
        1.0 / ((1.0 + row_first * has_p_lo + row_last * has_p_hi) * (1.0 + opening + ending))
    )

    arrive(0)
    diag = gathered(1)
    inv_diag = 1.0 / diag
    mat_ref[2] = inv_diag

    def dot_rows(left, right):
        return jnp.sum((left * right).reshape(128, 128), axis=0, keepdims=True)

    stages = (
        ((row_b, tile_b), spot, 2 * depth, column_peer, column_steps),
        ((row_a, tile_a), pos, per_run, layer_peer, layer_steps),
    )

    def push(index, stage, tile):
        refs, slot, _, peer, steps = stages[stage]
        own = refs[index].at[slot]
        own[...] = tile
        for step in steps:
            pltpu.make_async_remote_copy(
                src_ref=own,
                dst_ref=own,
                send_sem=send_red.at[index, stage],
                recv_sem=recv_red.at[index, stage],
                device_id=peer(step),
                device_id_type=MESH,
            ).start()

    def rest(index, stage):
        refs, _, count, peer, _ = stages[stage]
        others = refs[index].at[pl.ds(0, count - 1)]
        return pltpu.make_async_remote_copy(
            src_ref=others,
            dst_ref=others,
            send_sem=send_red.at[index, stage],
            recv_sem=recv_red.at[index, stage],
            device_id=peer(1),
            device_id_type=MESH,
        )

    def pull(index, stage):
        rest(index, stage).wait_recv()
        return jnp.sum(stages[stage][0][index][...], axis=0)

    zeros = jnp.zeros((1, 128), jnp.float32)

    def moments(first, second, third, applied):
        m = [dot_rows(weighted * first, first), dot_rows(weighted * first, second)]
        m.append(dot_rows(weighted * second, second))
        m.append(dot_rows(weighted * second, third))
        m.append(dot_rows(weighted * third, third))
        m.append(dot_rows(third, applied) - SHIFT * m[4])
        m = jnp.concatenate(m + [zeros, zeros], axis=0)
        for shift in (64, 32, 16):
            m = m + pltpu.roll(m, shift, axis=1)
        return jnp.sum(jnp.where(lane // 16 == sub, m, 0.0), axis=0, keepdims=True)

    def coefficients(tile):
        m = jnp.where(lane // 16 == sub, tile, 0.0)
        m = jnp.broadcast_to(jnp.sum(m, axis=1, keepdims=True), (8, 128))
        m = [m[k : k + 1] for k in range(6)]
        a = [m[k + 1] + SHIFT * m[k] for k in range(5)]
        pivot0 = a[0]
        l1 = a[1] / pivot0
        l2 = a[2] / pivot0
        pivot1 = a[2] - l1 * a[1]
        cross = a[3] - l1 * a[2]
        inv1 = jnp.where(pivot1 > 1e-7 * a[2], 1.0 / pivot1, 0.0)
        l12 = cross * inv1
        pivot2 = a[4] - l2 * a[2] - l12 * cross
        inv2 = jnp.where(pivot2 > 1e-7 * a[4], 1.0 / pivot2, 0.0)
        g1 = m[1] - l1 * m[0]
        g2 = m[2] - l2 * m[0] - l12 * g1
        c2 = g2 * inv2
        c1 = g1 * inv1 - l12 * c2
        c0 = m[0] / pivot0 - l1 * c1 - l2 * c2
        return c0, c1, c2

    def blend(coef, basis):
        return coef[0] * basis[0] + coef[1] * basis[1] + coef[2] * basis[2]

    returns = []

    def keep(index, values):
        out_ref[index] = values
        send_back = move(1 + index, out_ref.at[index], back_ref.at[index], source)

        @pl.when(moves)
        def _():
            send_back.start()

        @pl.when(jnp.logical_not(moves))
        def _():
            back_ref[index] = out_ref[index]

        returns.append(send_back)

    def advance(index, previous):
        arrive(index)
        return [
            gathered(STARTS[index] + k) * mat_ref[2] - SHIFT * values
            for k, values in enumerate(previous)
        ]

    v0 = gathered(0) * inv_diag
    publish(1, stiffness(v0))
    publish(5, (mat_ref[0],))
    mat_ref[3] = jnp.stack([diag[i] * plane_copies * depth_copies[i] for i in range(16)])
    weighted = mat_ref[3]
    (v1,) = advance(1, (v0,))
    publish(2, stiffness(v1))
    arrive(5)
    mat_ref[4] = gathered(STARTS[5]) * mat_ref[2]
    keep(3, mat_ref[4])
    (v2,) = advance(2, (v1,))
    basis = (v0, v1, v2)
    w0 = [values * mat_ref[4] for values in basis]
    publish(3, stiffness(*w0))
    push(0, 0, moments(v0, v1, v2, stiffness(v2)[0]))
    w1 = advance(3, w0)
    publish(4, stiffness(*w1))
    push(0, 1, pull(0, 0))
    rows = source_rows([*basis, *w0, *w1])
    w2 = advance(4, w1)
    applied = stiffness(*w2)
    rows = jnp.concatenate(
        rows + source_rows(w2) + [jnp.zeros((4, 256), jnp.float32)], axis=0
    )
    sums = jnp.dot(rows, hits, precision=HIGH, preferred_element_type=jnp.float32)
    tile = pull(0, 1)
    coef = coefficients(tile)
    wide_coef = [c[None] for c in coef]
    later_sum = blend(coef, [sums[k : k + 1, 128:256] for k in range(3)])
    earlier_sums = [
        blend(coef, [sums[3 * n + k : 3 * n + k + 1, 0:128] for k in range(3)]) for n in (1, 2, 3)
    ]
    later = blend(wide_coef, basis)
    basis = [blend(wide_coef, fields) for fields in (w0, w1, w2)]
    applied = blend(wide_coef, applied)
    push(
        1, 0, jnp.concatenate([moments(*basis, applied)] + earlier_sums + [later_sum], axis=0)
    )
    keep(0, later)
    keep(1, basis[1])
    keep(2, basis[2])
    sent(4)
    sent(5)
    for stage in range(2):
        rest(0, stage).wait_send()
    push(1, 1, pull(1, 0))

    @pl.when(moves)
    def _():
        for send_back in returns:
            send_back.wait_recv()
            send_back.wait_send()

    second_ref[...] = back_ref[0]
    for stage in range(2):
        rest(1, stage).wait_send()
    tile = pull(1, 1)
    coef = coefficients(tile[0:1])
    earlier_grad = blend(coef, [tile[1 + k : 2 + k] for k in range(3)])

    first_ref[...] = blend(
        [c[None] for c in coef], (back_ref[0] * back_ref[3], back_ref[1], back_ref[2])
    )
    scale = 1.0 / (8.0 * INV_STEP)
    grad_ref[0:1, :] = earlier_grad * scale
    grad_ref[1:2, :] = tile[4:5] * scale


def write_out(*refs):
    sources, targets, sems = refs[:3], refs[3:6], refs[6]
    stores = [
        pltpu.make_async_copy(source, target, sems.at[index])
        for index, (source, target) in enumerate(zip(sources, targets))
    ]
    for store in stores:
        store.start()
    for store in stores:
        store.wait()


def solution(mesh):
    shape = (mesh.shape["height"], mesh.shape["plane"], 4)
    const, weights, slope = tables()
    weights = [float(value) for value in weights]
    slope = [float(value) for value in slope]
    run, stack = shape[1] // 2, shape[0] * 2

    def per_device(cotangent, conductivity, capacity, sources):
        block = jax.ShapeDtypeStruct(cotangent.shape, jnp.float32)
        outs = (block, block, jax.ShapeDtypeStruct(sources.shape, jnp.float32))
        results = pl.pallas_call(
            functools.partial(kernel, shape, weights, slope),
            out_shape=tuple(pltpu.VMEM(item.shape, item.dtype) for item in outs),
            in_specs=[pl.BlockSpec(memory_space=pl.ANY)] * 5,
            out_specs=(pl.BlockSpec(memory_space=pltpu.VMEM),) * 3,
            scratch_shapes=[
                pltpu.VMEM(conductivity.shape, jnp.float32),
                pltpu.VMEM(capacity.shape, jnp.float32),
                pltpu.VMEM(sources.shape, jnp.int32),
                pltpu.VMEM(const.shape, jnp.float32),
                pltpu.VMEM(cotangent.shape, jnp.float32),
                pltpu.VMEM((8, 128), jnp.float32),
                pltpu.VMEM((128, 128), jnp.float32),
                pltpu.VMEM((8, 128), jnp.float32),
                pltpu.VMEM((4, 16, 8, 128), jnp.float32),
                pltpu.VMEM((4, 16, 8, 128), jnp.float32),
                pltpu.VMEM((TOTAL, 128, 128), jnp.float32),
                pltpu.VMEM((2, TOTAL, 16, 128), jnp.float32),
                pltpu.VMEM((2, TOTAL, 16, 128), jnp.float32),
                pltpu.VMEM((2, TOTAL, 8, 128), jnp.float32),
                pltpu.VMEM((4, TOTAL, 1, 128), jnp.float32),
                pltpu.VMEM((4, TOTAL, 1, 128), jnp.float32),
                pltpu.VMEM((TOTAL, 128, 128), jnp.float32),
                pltpu.VMEM((5, 16, 8, 128), jnp.float32),
                pltpu.VMEM((run, 1, 128), jnp.float32),
                pltpu.VMEM((stack, 1, 128), jnp.float32),
                pltpu.VMEM((run, 5, 128), jnp.float32),
                pltpu.VMEM((stack, 5, 128), jnp.float32),
                pltpu.SemaphoreType.DMA((6, 8)),
                pltpu.SemaphoreType.DMA((6, 8)),
                pltpu.SemaphoreType.DMA((2, 2)),
                pltpu.SemaphoreType.DMA((2, 2)),
                pltpu.SemaphoreType.DMA((6,)),
                pltpu.SemaphoreType.DMA((6,)),
                pltpu.SemaphoreType.DMA((5,)),
            ],
            compiler_params=pltpu.CompilerParams(collective_id=0, has_side_effects=True),
        )(cotangent, conductivity, capacity, sources, jnp.asarray(const))
        return pl.pallas_call(
            write_out,
            out_shape=outs,
            in_specs=[pl.BlockSpec(memory_space=pltpu.VMEM)] * 3,
            out_specs=(pl.BlockSpec(memory_space=pl.ANY),) * 3,
            scratch_shapes=[pltpu.SemaphoreType.DMA((3,))],
        )(*[pltpu.with_memory_space_constraint(item, pltpu.VMEM) for item in results])

    split = P("height", "plane", None)
    return jax.shard_map(
        per_device,
        mesh=mesh,
        in_specs=(split, split, split, P(None, None)),
        out_specs=(split, split, P(None, None)),
        check_vma=False,
    )
```
